32 devices in a mesh: groups: 2 (over y), replica: 1, da: 4 (over x, core), db: 4 (over z).
Axes of the slice: x: 2, y: 2, z: 4, core: 2. Of those that a mesh axis runs over, the one named last changes fastest.
Arguments:
- tokens: bfloat16 [4096, 1024], P(('groups', 'replica', 'da', 'db')), parts along dimension 0, may hold values from -6 to 6
- grad_out: bfloat16 [4096, 1024], P(('groups', 'replica', 'da', 'db')), parts along dimension 0, may hold values from -3 to 3
- routes: int32 [4096, 8], P(('groups', 'replica', 'da', 'db')), parts along dimension 0, may hold values from 0 to 15, as said below
- gates: bfloat16 [4096, 8], P(('groups', 'replica', 'da', 'db')), parts along dimension 0, may hold values from 0.019897461 to 0.5
- w_gate_up: bfloat16 [16, 1024, 768], P(('da', 'db'), 'replica'), may hold values from -0.1875 to 0.1875
- w_down: bfloat16 [16, 384, 1024], P(('da', 'db'), 'replica'), may hold values from -0.3125 to 0.3125
Outputs:
- token_grads: bfloat16 [4096, 1024], P(('groups', 'replica', 'da', 'db')), parts along dimension 0
- gate_grads: bfloat16 [4096, 8], P(('groups', 'replica', 'da', 'db')), parts along dimension 0
- gate_up_grads: bfloat16 [32, 1024, 768], P(('groups', 'da', 'db'), 'replica'), parts along dimension 0
- down_grads: bfloat16 [32, 384, 1024], P(('groups', 'da', 'db'), 'replica'), parts along dimension 0
The draws below stay inside these ranges and needn't reach their ends.
There are 2 independent parts, one for each index of `groups`. The reference program is written for one: setup_inputs(seed, part) draws one part's arguments, and reference() takes and returns one part's arrays. A program takes and returns all parts, laid end to end along the dimension named above; an argument that names none is the same for every part. Nothing has to cross between parts.
Inputs may be any that keep to these rules, and one draw needn't show every extreme that they name: `routes`: each token names 8 different experts. In every aligned block of 2 consecutive tokens, each expert is named exactly once, so the tokens of one device name every expert exactly 64 times.
All inputs are finite; a program needn't handle non-finite values.
Results may differ from the reference program's by a relative error of at most 0.0085.
Values may be sent and summed in bfloat16 or wider, within the bound.
A program may use at most 64 MiB of HBM per device.

```python
import math
import jax
import jax.numpy as jnp
from jax import lax

D = 1024
FF = 384
TOP = 8
TOK_DEV = 128
EXPERTS = 16
TOKENS = 2048
N_REPLICA = 1
N_DA = 4
N_DB = 4


def draw_routes(key, part):
    per_round = EXPERTS // TOP
    round_count = TOKENS // per_round
    keys = jax.random.split(jax.random.fold_in(key, 7), round_count)
    orders = jax.vmap(lambda one: jax.random.permutation(one, EXPERTS))(keys)
    return orders.reshape(TOKENS, TOP).astype(jnp.int32)


def block_levels(stream_key, shape, shards, least, top_value):
    def one(dim, shards_of):
        heights = jax.random.uniform(jax.random.fold_in(jax.random.fold_in(stream_key, 6), dim), (shards_of,), jnp.float32, least / len(shards), top_value / len(shards))
        return jnp.repeat(jnp.exp(heights), shape[dim] // shards_of).reshape((-1,) + (1,) * (len(shape) - dim - 1))

    loudness = one(*shards[0])
    for cut in shards[1:]:
        loudness = loudness * one(*cut)
    return loudness


def centred(own_key, extent, spread, most, cuts=(), held_as=jnp.bfloat16):
    array = jax.random.normal(own_key, extent, jnp.float32) * spread
    if len(cuts) > 0:
        array = block_levels(own_key, extent, cuts, -0.22, 0.18) * array
    return jnp.clip(array, min=-most, max=most).astype(held_as)


def setup_inputs(seed: int = 0, part: int = 0) -> dict:
    splits = jax.random.split(jax.random.key(seed), 7)
    own_keys = jax.random.split(jax.random.fold_in(splits[6], part), 7)
    return {
        "tokens": centred(own_keys[0], (TOKENS, D), 1.0, 6.0, ((0, 16),)),
        "grad_out": centred(own_keys[1], (TOKENS, D), 0.5, 3.0, ((0, 16),)),
        "routes": draw_routes(jax.random.fold_in(jax.random.fold_in(splits[6], part), 71), part),
        "gates": jnp.clip(jnp.exp(math.log(0.5) - 3.224016 * jax.random.uniform(own_keys[3], (TOKENS, TOP), jnp.float32) ** block_levels(own_keys[3], (TOKENS, TOP), ((0, 16),), -0.2, 0.2)), 0.019897461, 0.5).astype(jnp.bfloat16),
        "w_gate_up": centred(splits[4], (EXPERTS, D, 2 * FF), D ** -0.5, 0.1875, ((0, 16),)),
        "w_down": centred(splits[5], (EXPERTS, FF, D), FF ** -0.5, 0.3125, ((0, 16),)),
    }


def silu_parts(projected):
    sigmoid = jax.nn.sigmoid(projected)
    return projected * sigmoid, sigmoid * (1.0 + projected * (1.0 - sigmoid))


def replica_sum(partials):
    rounded = lax.optimization_barrier(partials.astype(jnp.bfloat16))
    return jnp.sum(rounded.astype(jnp.float32), axis=0).astype(jnp.bfloat16)


def reference(tokens, grad_out, routes, gates, w_gate_up, w_down):
    per_replica = TOK_DEV * N_DA * N_DB
    flat_routes = routes.reshape(N_REPLICA, per_replica * TOP)
    ordering = jnp.argsort(flat_routes, axis=1, stable=True).astype(jnp.int32)
    rows_expert = per_replica * TOP // EXPERTS
    ordering = ordering.reshape(N_REPLICA, EXPERTS, rows_expert)
    offsets = (jnp.arange(N_REPLICA, dtype=jnp.int32) * (per_replica * TOP)).astype(jnp.int32)
    route_index = (ordering + offsets[:, None, None]).astype(jnp.int32)
    route_index = jnp.transpose(route_index, (1, 0, 2))
    flat_gates = gates.reshape(-1)

    def expert_step(carry, inputs):
        token_acc, gate_acc = carry
        index, w_in, w_out = inputs
        token_ids = (index // TOP).astype(jnp.int32)
        input_rows = tokens[token_ids].astype(jnp.float32)
        upstream = grad_out[token_ids].astype(jnp.float32)
        gate_rows = flat_gates[index].astype(jnp.float32)[..., None]
        w_in_f = w_in.astype(jnp.float32)
        w_out_f = w_out.astype(jnp.float32)
        projected = jnp.einsum("prd,df->prf", input_rows, w_in_f)
        gate_part = projected[..., :FF]
        up_part = projected[..., FF:]
        activated, derivative = silu_parts(gate_part)
        hidden = (activated * up_part).astype(jnp.bfloat16)
        back_raw = jnp.einsum("prd,fd->prf", upstream, w_out_f)
        gate_scores = jnp.sum(hidden.astype(jnp.float32) * back_raw, axis=-1).astype(jnp.bfloat16)
        back_hidden = gate_rows * back_raw
        grad_projected = jnp.concatenate([back_hidden * up_part * derivative, back_hidden * activated], axis=-1).astype(jnp.bfloat16)
        scaled_upstream = (gate_rows * upstream).astype(jnp.bfloat16)
        input_grads = jnp.einsum("prf,df->prd", grad_projected.astype(jnp.float32), w_in_f).astype(jnp.bfloat16)
        grad_in = replica_sum(jnp.einsum("prd,prf->pdf", input_rows, grad_projected.astype(jnp.float32)))
        grad_down = replica_sum(jnp.einsum("prf,prd->pfd", hidden.astype(jnp.float32), scaled_upstream.astype(jnp.float32)))
        token_acc = token_acc.at[token_ids.reshape(-1)].add(input_grads.reshape(-1, D).astype(jnp.float32))
        gate_acc = gate_acc.at[index.reshape(-1)].set(gate_scores.reshape(-1))
        return (token_acc, gate_acc), (grad_in, grad_down)

    start = (jnp.zeros((TOKENS, D), jnp.float32), jnp.zeros((TOKENS * TOP,), jnp.bfloat16))
    (token_acc, gate_acc), (gate_up_grads, down_grads) = lax.scan(expert_step, start, (route_index, w_gate_up, w_down))
    return token_acc.astype(jnp.bfloat16), gate_acc.reshape(TOKENS, TOP), gate_up_grads, down_grads
```

```python
import functools

import jax
import jax.numpy as jnp
from jax import lax
from jax.experimental import pallas as pl
from jax.experimental.pallas import tpu as pltpu
from jax.sharding import PartitionSpec as P


CORES = 2
HALVES = 2
MESH = pl.DeviceIdType.MESH


def silu_parts(projected):
    sigmoid = jax.nn.sigmoid(projected)
    return (projected * sigmoid, sigmoid * (1.0 + projected * (1.0 - sigmoid)))


def body(tokens, grad_out, routes, gates, w_gate_up, w_down):
    local_tokens, features = tokens.shape
    top_count = routes.shape[1]
    hidden_units = w_gate_up.shape[2] // 2
    first_size = lax.axis_size("da")
    second_size = lax.axis_size("db")
    experts = first_size * second_size
    per_round = experts // top_count
    rounds = local_tokens // per_round
    expert_ids = lax.broadcasted_iota(jnp.int32, (1, 1, 1, experts), 3)
    matches = routes.reshape(rounds, per_round, top_count, 1) == expert_ids
    gate_values = gates.reshape(rounds, per_round, top_count, 1).astype(jnp.float32)
    gate_table = jnp.sum(jnp.where(matches, gate_values, 0.0), axis=(1, 2)).astype(jnp.bfloat16)
    chosen = jnp.any(matches, axis=2).astype(jnp.bfloat16)
    input_send = jnp.einsum(
        "rge,rgd->red",
        chosen,
        tokens.reshape(rounds, per_round, features),
        preferred_element_type=jnp.float32,
    ).astype(jnp.bfloat16)
    upstream_send = jnp.einsum(
        "rge,rgd->red",
        chosen,
        grad_out.reshape(rounds, per_round, features),
        preferred_element_type=jnp.float32,
    ).astype(jnp.bfloat16)
    input_recv, upstream_recv, gate_recv = (
        lax.all_to_all(input_send, ("da", "db"), split_axis=1, concat_axis=1, tiled=True),
        lax.all_to_all(upstream_send, ("da", "db"), split_axis=1, concat_axis=1, tiled=True),
        lax.all_to_all(gate_table, ("da", "db"), split_axis=1, concat_axis=1, tiled=True),
    )
    input_rows = input_recv.reshape(-1, features)
    upstream_rows = upstream_recv.reshape(-1, features)
    gate_rows = gate_recv.reshape(-1, 1).astype(jnp.float32)
    w_in, w_out = (
        lax.all_gather(w_gate_up[0], "replica", axis=0, tiled=True),
        lax.all_gather(w_down[0], "replica", axis=0, tiled=True),
    )
    projected = jnp.dot(input_rows, w_in, preferred_element_type=jnp.float32)
    back_raw = jnp.einsum("rd,fd->rf", upstream_rows, w_out, preferred_element_type=jnp.float32)
    gate_part = projected[:, :hidden_units]
    up_part = projected[:, hidden_units:]
    activated, derivative = silu_parts(gate_part)
    hidden = (activated * up_part).astype(jnp.bfloat16)
    gate_scores = jnp.sum(hidden.astype(jnp.float32) * back_raw, axis=1).astype(jnp.bfloat16)
    back_hidden = gate_rows * back_raw
    grad_projected = jnp.concatenate(
        [back_hidden * up_part * derivative, back_hidden * activated], axis=1
    ).astype(jnp.bfloat16)
    scaled_upstream = (gate_rows * upstream_rows.astype(jnp.float32)).astype(jnp.bfloat16)
    input_grads = jnp.einsum("rf,df->rd", grad_projected, w_in, preferred_element_type=jnp.float32)
    input_grads = input_grads.astype(jnp.bfloat16).reshape(rounds, experts, features)
    score_back = gate_scores.reshape(rounds, experts)
    returned, score_ret = (
        lax.all_to_all(input_grads, ("da", "db"), split_axis=1, concat_axis=1, tiled=True),
        lax.all_to_all(score_back, ("da", "db"), split_axis=1, concat_axis=1, tiled=True),
    )
    score_ret = score_ret.reshape(rounds, 1, 1, experts).astype(jnp.float32)
    token_grads = (
        jnp.einsum("rge,red->rgd", chosen, returned, preferred_element_type=jnp.float32)
        .astype(jnp.bfloat16)
        .reshape(local_tokens, features)
    )
    gate_grads = (
        jnp.sum(jnp.where(matches, score_ret, 0.0), axis=3)
        .astype(jnp.bfloat16)
        .reshape(local_tokens, top_count)
    )
    columns = input_rows
    grad_in = lax.psum_scatter(
        jnp.einsum("rd,rf->df", columns, grad_projected, preferred_element_type=jnp.float32).astype(
            jnp.bfloat16
        ),
        "replica",
        scatter_dimension=0,
        tiled=True,
    )
    columns = hidden
    grad_down = lax.psum_scatter(
        jnp.einsum(
            "rf,rd->fd", columns, scaled_upstream, preferred_element_type=jnp.float32
        ).astype(jnp.bfloat16),
        "replica",
        scatter_dimension=0,
        tiled=True,
    )
    return (token_grads, gate_grads, grad_in[None], grad_down[None])


def visit(j, z, n):
    m = jnp.minimum(z, n - 1 - z)
    near = z + (1 - 2 * (j % 2)) * ((j + 1) // 2)
    far = jnp.where(z < n - 1 - z, j, n - 1 - j)
    return jnp.where(j <= 2 * m, near, far)


def dot(a, b, dims):
    return lax.dot_general(a, b, (dims, ((), ())), preferred_element_type=jnp.float32)


def position(d, z, n):
    away = abs(d - z)
    if away <= min(z, n - 1 - z):
        return 2 * away - (1 if d < z else 0)
    return d if z < n - 1 - z else n - 1 - d


def relay_slots(n):
    last = 2 * n - 1

    def ready(z, d, h):
        k = position(d, z, n)
        k = last - k if h else k
        feeds = [u for u in (z - 1, z + 1) if 0 <= u < n and abs(u - d) == abs(z - d) + 1]
        return max([k + 1] + [ready(u, d, h) + 1 for u in feeds])

    table = []
    for z in range(n):
        row = [0] * (2 * n)
        for d in range(n):
            k = position(d, z, n)
            row[k] = ready(z, d, 0)
            row[last - k] = ready(z, d, 1)
        table.append(row)
    return table


def lag_words(n):
    return [sum((at - k - 1) * 8**k for k, at in enumerate(row)) for row in relay_slots(n)]


def fused_kernel(
    cols, depth, group,
    tok_hbm, up_hbm, routes_hbm, gates_hbm, win_hbm, wout_hbm,
    tg_ref, gg_ref, gin_ref, gdown_ref,
    routes_ref, gates_ref, tok, up, table, win, wout, xs, su, hid, gp, igs, igb, acc, cs, cr, rk, rx, scs, scr,
    load_sem, recv_sem, zup_sem, zdn_sem, x_sem, p_sem, igs_sem, igr_sem, cs_sem, cr_sem, rx_sem, scs_sem, scr_sem,
):
    da = lax.axis_index("da")
    z = lax.axis_index("db")
    x, c = da // CORES, da % CORES
    half, features = tok.shape[2], tok.shape[3]
    local = HALVES * half
    experts = table.shape[1]
    top = routes_ref.shape[0]
    rows = half // group
    ff = wout.shape[0]
    steps = HALVES * depth

    def slot(xx, zz, cc):
        return (xx * CORES + cc) * depth + zz

    me = slot(x, z, c)
    loads = []
    for h in range(HALVES):
        span = pl.ds(h * half, half)
        loads.append(pltpu.make_async_copy(tok_hbm.at[span], tok.at[me, h], load_sem.at[2 * h]))
        loads.append(pltpu.make_async_copy(up_hbm.at[span], up.at[me, h], load_sem.at[2 * h + 1]))
    loads += [
        pltpu.make_async_copy(win_hbm.at[0], win, load_sem.at[4]),
        pltpu.make_async_copy(wout_hbm.at[0], wout, load_sem.at[5]),
        pltpu.make_async_copy(routes_hbm, routes_ref, load_sem.at[6]),
        pltpu.make_async_copy(gates_hbm, gates_ref, load_sem.at[7]),
    ]
    barrier = pltpu.get_barrier_semaphore()
    count = cols * CORES * depth

    def greet(xx, zz, cc):
        pl.semaphore_signal(
            barrier, inc=1, device_id={"da": xx * CORES + cc, "db": zz}, device_id_type=MESH
        )

    @pl.when(z > 0)
    def _():
        greet(x, z - 1, c)

    @pl.when(z < depth - 1)
    def _():
        greet(x, z + 1, c)

    greet(1 - x, z, c)
    greet(x, z, 1 - c)
    for k in (6, 7, 0, 1, 2, 3, 4, 5):
        loads[k].start()

    loads[6].wait()
    loads[7].wait()
    routes = routes_ref[...]
    gates = gates_ref[...].astype(jnp.float32)
    ids = lax.broadcasted_iota(jnp.int32, (experts, local), 0)
    chart = jnp.zeros((experts, local), jnp.float32)
    for k in range(top):
        chart = chart + jnp.where(routes[k : k + 1] == ids, gates[k : k + 1], 0.0)
    table[me] = chart.astype(jnp.bfloat16)

    for k in range(4):
        loads[k].wait()
    pl.semaphore_wait(barrier, 2 + jnp.where(z > 0, 1, 0) + jnp.where(z < depth - 1, 1, 0))

    held = (tok, up)

    def send(src, dst, send_sem, recv, to_x, to_z, to_c):
        return pltpu.make_async_remote_copy(
            src_ref=src,
            dst_ref=dst,
            send_sem=send_sem,
            recv_sem=recv,
            device_id={"da": to_x * CORES + to_c, "db": to_z},
            device_id_type=MESH,
        )

    def relay(s, h, a, sem, to_x, to_z, to_c):
        ref = held[a].at[s, h]
        return send(ref, ref, sem, recv_sem.at[s, h, a], to_x, to_z, to_c)

    def relay_table(s, sem, to_x, to_z, to_c):
        ref = table.at[s]
        return send(ref, ref, sem, recv_sem.at[s, 0, 2], to_x, to_z, to_c)

    def both(s, zz, h, a, sems, act, to_x, to_z, to_c):
        act(relay(s, h, a, sems.at[zz, h, a], to_x, to_z, to_c))
        if a == 0:

            @pl.when(h == 0)
            def _():
                act(relay_table(s, sems.at[zz, 0, 2], to_x, to_z, to_c))

    def start(copy):
        copy.start()

    def wait_send(copy):
        copy.wait_send()

    def wait_recv(copy):
        copy.wait_recv()

    def step_of(i):
        j = jnp.minimum(i, steps - 1 - i)
        return visit(j, z, depth), jnp.where(i >= depth, 1, 0)

    def along_z(e, a):
        def one(reach, sign, sems):
            last = 2 * reach + 1
            k = jnp.minimum(e, last - e)
            h = jnp.where(e > reach, 1, 0)
            zz = z + sign * k
            s = slot(x, zz, c)

            @pl.when((e <= last) & (k > 0))
            def _():
                both(s, zz, h, a, p_sem.at[0], wait_recv, x, z, 1 - c)

            ahead = z - sign

            @pl.when((e <= last) & (ahead >= 0) & (ahead < depth))
            def _():
                both(s, zz, h, a, sems, start, x, ahead, c)

        one(depth - 1 - z, 1, zdn_sem)
        one(z, -1, zup_sem)

    def across(i, a):
        zz, h = step_of(i)
        s = slot(x, zz, c)
        if a == 0:

            @pl.when(i < steps - 1)
            def _():
                both(s, zz, h, a, x_sem, start, 1 - x, z, c)
        else:
            both(s, zz, h, a, x_sem, start, 1 - x, z, c)
        both(s, zz, h, a, p_sem.at[0], start, x, z, 1 - c)

    def from_across(i, a):
        zz, h = step_of(i)
        s = slot(1 - x, zz, c)
        both(s, zz, h, a, p_sem.at[1], wait_recv, x, z, 1 - c)
        both(s, zz, h, a, p_sem.at[1], start, x, z, 1 - c)

    def from_partner(i):
        zz, h = step_of(i)
        for xx in (x, 1 - x):
            for a in range(2):
                both(slot(xx, zz, 1 - c), zz, h, a, p_sem.at[0], wait_recv, x, z, 1 - c)

    def pick(s, e, h):
        chart_s = table[s].astype(jnp.float32)
        which = lax.broadcasted_iota(jnp.int32, chart_s.shape, 0) == e
        row = jnp.sum(jnp.where(which, chart_s, 0.0), axis=0, keepdims=True)
        row = jnp.where(h == 0, row[:, :half], row[:, half:])
        off = lax.broadcasted_iota(jnp.int32, (rows, half), 1) - group * lax.broadcasted_iota(
            jnp.int32, (rows, half), 0
        )
        hit = (off >= 0) & (off < group) & (row > 0.0)
        return jnp.where(hit, 1.0, 0.0), row

    def send_ig(q, k):
        return send(igs.at[k, q], igb.at[k, q, c], igs_sem.at[k, q], igr_sem.at[k, q], x, z, 1 - c)

    def send_score(s):
        return pltpu.make_async_remote_copy(
            src_ref=scs.at[s],
            dst_ref=scr.at[me],
            send_sem=scs_sem.at[s],
            recv_sem=scr_sem.at[me],
            device_id={"da": s // depth, "db": s % depth},
            device_id_type=MESH,
        )

    blocks = [(q, r) for q in range(cols) for r in range(CORES)]
    batch = len(blocks) * rows

    def compute(k):
        zz, h = step_of(k)
        base = pl.multiple_of(k * batch, batch)
        picks = []
        gate_cols = []
        for n, (q, r) in enumerate(blocks):
            s = slot((x + q) % cols, zz, (c + r) % CORES)
            chosen, row = pick(s, me, h)
            picks.append((s, chosen))
            gate_cols.append(jnp.sum(chosen * row, axis=1, keepdims=True))
            hot = chosen.astype(jnp.bfloat16)
            where = pl.ds(pl.multiple_of(base + n * rows, rows), rows)
            xs[where, :] = dot(hot, tok[s, h], ((1,), (0,))).astype(jnp.bfloat16)
            su[where, :] = dot(hot, up[s, h], ((1,), (0,))).astype(jnp.bfloat16)
        here = pl.ds(base, batch)
        gate = jnp.concatenate(gate_cols, axis=0)
        upstream = su[here, :]
        projected = dot(xs[here, :], win[...], ((1,), (0,)))
        back_raw = dot(upstream, wout[...], ((1,), (1,)))
        su[here, :] = (gate * upstream.astype(jnp.float32)).astype(jnp.bfloat16)
        gate_part, up_part = projected[:, :ff], projected[:, ff:]
        activated, derivative = silu_parts(gate_part)
        hidden = (activated * up_part).astype(jnp.bfloat16)
        hid[here, :] = hidden
        scores = jnp.sum(hidden.astype(jnp.float32) * back_raw, axis=1, keepdims=True)
        scores = scores.astype(jnp.bfloat16).astype(jnp.float32)
        back_hidden = gate * back_raw
        gp[here, :ff] = (back_hidden * up_part * derivative).astype(jnp.bfloat16)
        gp[here, ff:] = (back_hidden * activated).astype(jnp.bfloat16)
        grads = dot(gp[here, :], win[...], ((1,), (1,))).astype(jnp.bfloat16)
        for n, (q, r) in enumerate(blocks):
            piece = grads[n * rows : (n + 1) * rows]
            if r == 0:
                igb[k, q, c] = piece
            else:
                igs[k, q] = piece
                send_ig(q, k).start()
        for n, (q, r) in enumerate(blocks):
            s, chosen = picks[n]
            line = jnp.sum(chosen * scores[n * rows : (n + 1) * rows], axis=0, keepdims=True)
            rest = jnp.zeros_like(line)
            first = jnp.concatenate([line, rest], axis=1)
            second = jnp.concatenate([rest, line], axis=1)

            @pl.when(h == 0)
            def _():
                scs[s] = jnp.broadcast_to(first, scs.shape[1:])

            @pl.when(h == 1)
            def _():
                scs[s] = scs[s] + jnp.broadcast_to(second, scs.shape[1:])
                if q == 0 and r == 0:

                    @pl.when(zz == z)
                    def _():
                        scr[me] = scs[me]

                    @pl.when(zz != z)
                    def _():
                        send_score(s).start()
                else:
                    send_score(s).start()

    def chip_sum(k, q):
        zz, h = step_of(k)
        s = slot((x + q) % cols, zz, c)
        hot = jnp.concatenate([pick(s, slot(x, z, m), h)[0] for m in range(CORES)], axis=0)
        pair = igb[k, q].reshape(CORES * rows, features)
        return dot(hot.astype(jnp.bfloat16), pair, ((0,), (0,)))

    def send_sum(zz, h, q, side, to_z):
        return send(
            cs.at[zz, h, q], cr.at[side, zz, h, q], cs_sem.at[zz, h, q], cr_sem.at[side, zz, h, q], x, to_z, c
        )

    def send_across(h):
        return send(cs.at[z, h, 1], rx.at[h], cs_sem.at[z, h, 1], rx_sem.at[h], 1 - x, z, c)

    def pass_on(k, q):
        zz, h = step_of(k)
        send_ig(q, k).wait_recv()
        acc[...] = chip_sum(k, q)
        for side, ok in ((0, (zz <= z) & (z < depth - 1)), (1, (zz >= z) & (z > 0))):

            @pl.when(ok)
            def _():
                send_sum(zz, h, q, side, z).wait_recv()
                acc[...] += cr[side, zz, h, q].astype(jnp.float32)

        if q == 0:

            @pl.when(zz == z)
            def _():
                rk[h] = acc[...]

        @pl.when((zz != z) if q == 0 else True)
        def _():
            cs[zz, h, q] = acc[...].astype(jnp.bfloat16)

        @pl.when(zz < z)
        def _():
            send_sum(zz, h, q, 0, z - 1).start()

        @pl.when(zz > z)
        def _():
            send_sum(zz, h, q, 1, z + 1).start()

        if q == 1:

            @pl.when(zz == z)
            def _():
                send_across(h).start()

    words = lag_words(depth)
    word = jnp.int32(words[0])
    for k in range(1, depth):
        word = jnp.where(z == k, words[k], word)

    def pass_all(i, q):
        def one(k, left):
            @pl.when(k + 1 + left % 8 == i)
            def _():
                pass_on(k, q)

            return left // 8

        lax.fori_loop(0, jnp.minimum(i, steps), one, word)

    along_z(0, 0)
    across(0, 0)

    def step(i, carry):
        @pl.when(i < steps)
        def _():
            along_z(i, 1)
            across(i, 1)

        @pl.when(i == 0)
        def _():
            relay(me, 1, 0, x_sem.at[z, 1, 0], 1 - x, z, c).start()
            loads[4].wait()
            loads[5].wait()

        @pl.when(i >= 1)
        def _():
            from_across(i - 1, 1)
            pass_all(i - 1, 0)
            from_partner(i - 1)
            compute(i - 1)

        @pl.when(i + 1 < steps)
        def _():
            along_z(i + 1, 0)
            across(i + 1, 0)

        @pl.when(i < steps)
        def _():
            from_across(i, 0)

        @pl.when(i >= 1)
        def _():
            pass_all(i, 1)

        return carry

    lax.fori_loop(0, steps + 1, step, 0)
    pass_all(steps, 0)

    wide = min(features, 256)

    @pl.loop(0, features // wide)
    def _(t):
        at = pl.ds(pl.multiple_of(t * wide, wide), wide)
        gin_ref[0, at, :] = dot(xs[:, at], gp[...], ((0,), (0,))).astype(jnp.bfloat16)

    thin = 128

    @pl.loop(0, ff // thin)
    def _(t):
        at = pl.ds(pl.multiple_of(t * thin, thin), thin)
        gdown_ref[0, at, :] = dot(hid[:, at], su[...], ((0,), (0,))).astype(jnp.bfloat16)

    @pl.loop(1, count)
    def _(k):
        s = (me + k) % count
        pltpu.make_async_remote_copy(
            src_ref=scs.at[s],
            dst_ref=scr.at[s],
            send_sem=scs_sem.at[s],
            recv_sem=scr_sem.at[s],
            device_id={"da": s // depth, "db": s % depth},
            device_id_type=MESH,
        ).wait()

    scores = scr[:, 0, :]
    place = lax.broadcasted_iota(jnp.int32, (top, local), 0)
    gate_grads = jnp.zeros((top, local), jnp.float32)
    for k in range(top):
        value = jnp.sum(jnp.where(routes[k : k + 1] == ids, scores, 0.0), axis=0, keepdims=True)
        gate_grads = jnp.where(place == k, value, gate_grads)
    gg_ref[...] = gate_grads.astype(jnp.bfloat16)

    for h in range(HALVES):
        send_across(h).wait_recv()
        tg_ref[pl.ds(h * half, half), :] = (rk[h] + rx[h].astype(jnp.float32)).astype(jnp.bfloat16)

    def drain(k, carry):
        zz, h = k // HALVES, k % HALVES
        s = slot(x, zz, c)
        for a in range(2):

            @pl.when((zz <= z) & (z < depth - 1))
            def _():
                both(s, zz, h, a, zup_sem, wait_send, x, z + 1, c)

            @pl.when((zz >= z) & (z > 0))
            def _():
                both(s, zz, h, a, zdn_sem, wait_send, x, z - 1, c)

            both(s, zz, h, a, x_sem, wait_send, 1 - x, z, c)
            for o in range(2):
                both(s, zz, h, a, p_sem.at[o], wait_send, x, z, 1 - c)
        for q in range(cols):
            send_ig(q, k).wait_send()
        send(cs.at[zz, h, 1], rx.at[h], cs_sem.at[zz, h, 1], rx_sem.at[h], 1 - x, z, c).wait_send()

        @pl.when(zz != z)
        def _():
            send(cs.at[zz, h, 0], rx.at[h], cs_sem.at[zz, h, 0], rx_sem.at[h], 1 - x, z, c).wait_send()

        return carry

    lax.fori_loop(0, steps, drain, 0)


def store_kernel(*refs):
    count = len(refs) // 2
    sems = refs[-1]
    copies = [
        pltpu.make_async_copy(refs[k], refs[count + k], sems.at[k]) for k in range(count)
    ]
    for one in copies:
        one.start()
    for one in copies:
        one.wait()


def store(*arrays):
    anywhere = pl.BlockSpec(memory_space=pl.ANY)
    return pl.pallas_call(
        store_kernel,
        out_shape=tuple(jax.ShapeDtypeStruct(a.shape, a.dtype) for a in arrays),
        in_specs=[pl.BlockSpec(memory_space=pltpu.VMEM)] * len(arrays),
        out_specs=(pl.BlockSpec(memory_space=pltpu.HBM),) * len(arrays),
        scratch_shapes=[pltpu.SemaphoreType.DMA((len(arrays),))],
        compiler_params=pltpu.CompilerParams(vmem_limit_bytes=8 * 2**20),
    )(*arrays)


def fused(tokens, grad_out, routes, gates, w_gate_up, w_down):
    first_size, depth = lax.axis_size("da"), lax.axis_size("db")
    cols = first_size // CORES
    experts = first_size * depth
    local, features = tokens.shape
    top = routes.shape[1]
    group = experts // top
    ff = w_down.shape[1]
    bf, f32 = jnp.bfloat16, jnp.float32
    half = local // HALVES
    rows = half // group
    steps = HALVES * depth
    total = rows * experts * HALVES
    dma = pltpu.SemaphoreType.DMA
    scratch = [
        pltpu.VMEM((top, local), routes.dtype),
        pltpu.VMEM((top, local), gates.dtype),
        pltpu.VMEM((experts, HALVES, half, features), bf),
        pltpu.VMEM((experts, HALVES, half, features), bf),
        pltpu.VMEM((experts, experts, local), bf),
        pltpu.VMEM((features, 2 * ff), bf),
        pltpu.VMEM((ff, features), bf),
        pltpu.VMEM((total, features), bf),
        pltpu.VMEM((total, features), bf),
        pltpu.VMEM((total, ff), bf),
        pltpu.VMEM((total, 2 * ff), bf),
        pltpu.VMEM((steps, cols, rows, features), bf),
        pltpu.VMEM((steps, cols, CORES, rows, features), bf),
        pltpu.VMEM((half, features), f32),
        pltpu.VMEM((depth, HALVES, cols, half, features), bf),
        pltpu.VMEM((2, depth, HALVES, cols, half, features), bf),
        pltpu.VMEM((HALVES, half, features), f32),
        pltpu.VMEM((HALVES, half, features), bf),
        pltpu.VMEM((experts, 8, local), f32),
        pltpu.VMEM((experts, 8, local), f32),
        dma((8,)),
        dma((experts, HALVES, 3)),
        dma((depth, HALVES, 3)),
        dma((depth, HALVES, 3)),
        dma((depth, HALVES, 3)),
        dma((cols, depth, HALVES, 3)),
        dma((steps, cols)),
        dma((steps, cols)),
        dma((depth, HALVES, cols)),
        dma((2, depth, HALVES, cols)),
        dma((HALVES,)),
        dma((experts,)),
        dma((experts,)),
    ]
    vmem = pl.BlockSpec(memory_space=pltpu.VMEM)
    hbm = pl.BlockSpec(memory_space=pltpu.HBM)
    token_grads, gate_grads, grad_in, grad_down = pl.pallas_call(
        functools.partial(fused_kernel, cols, depth, group),
        out_shape=(
            jax.ShapeDtypeStruct((local, features), bf),
            jax.ShapeDtypeStruct((top, local), bf),
            jax.ShapeDtypeStruct(w_gate_up.shape, bf),
            jax.ShapeDtypeStruct(w_down.shape, bf),
        ),
        in_specs=[hbm] * 6,
        out_specs=(vmem, vmem, vmem, vmem),
        scratch_shapes=scratch,
        compiler_params=pltpu.CompilerParams(
            collective_id=0, has_side_effects=True, vmem_limit_bytes=44 * 2**20
        ),
    )(
        *(
            pltpu.with_memory_space_constraint(a, pltpu.HBM)
            for a in (tokens, grad_out, routes.T, gates.T, w_gate_up, w_down)
        )
    )
    token_grads, gate_grads, grad_in, grad_down = store(token_grads, gate_grads, grad_in, grad_down)
    return token_grads, gate_grads.T, grad_in, grad_down


def fits(tokens, routes, w_down):
    first_size = lax.axis_size("da")
    experts = first_size * lax.axis_size("db")
    local, features = tokens.shape
    group = experts // routes.shape[1]
    held = 2 * experts * local * features * 2
    return (
        lax.axis_size("replica") == 1
        and first_size % CORES == 0
        and first_size == 2 * CORES
        and 2 * 3 * lax.axis_size("db") <= 30
        and held <= 16 * 2**20
        and local == 128
        and experts <= local
        and (local // (HALVES * group)) % 16 == 0
        and w_down.shape[1] % 128 == 0
    )


def route(*arrays):
    if fits(arrays[0], arrays[2], arrays[5]):
        return fused(*arrays)
    return body(*arrays)


def solution(mesh):
    placed = (
        P(("groups", "replica", "da", "db"), None),
        P(("groups", "replica", "da", "db"), None),
        P(("groups", "replica", "da", "db"), None),
        P(("groups", "replica", "da", "db"), None),
        P(("da", "db"), "replica", None),
        P(("da", "db"), "replica", None),
    )
    return jax.shard_map(
        route,
        mesh=mesh,
        in_specs=placed,
        out_specs=(
            P(("groups", "replica", "da", "db"), None),
            P(("groups", "replica", "da", "db"), None),
            P(("groups", "da", "db"), "replica", None),
            P(("groups", "da", "db"), "replica", None),
        ),
        check_vma=False,
    )
```

```python
import functools

import jax
import jax.numpy as jnp
from jax import lax
from jax.experimental import pallas as pl
from jax.experimental.pallas import tpu as pltpu
from jax.sharding import PartitionSpec as P


CORES = 2
HALVES = 2
MESH = pl.DeviceIdType.MESH


def silu_parts(projected):
    sigmoid = jax.nn.sigmoid(projected)
    return (projected * sigmoid, sigmoid * (1.0 + projected * (1.0 - sigmoid)))


def body(tokens, grad_out, routes, gates, w_gate_up, w_down):
    local_tokens, features = tokens.shape
    top_count = routes.shape[1]
    hidden_units = w_gate_up.shape[2] // 2
    first_size = lax.axis_size("da")
    second_size = lax.axis_size("db")
    experts = first_size * second_size
    per_round = experts // top_count
    rounds = local_tokens // per_round
    expert_ids = lax.broadcasted_iota(jnp.int32, (1, 1, 1, experts), 3)
    matches = routes.reshape(rounds, per_round, top_count, 1) == expert_ids
    gate_values = gates.reshape(rounds, per_round, top_count, 1).astype(jnp.float32)
    gate_table = jnp.sum(jnp.where(matches, gate_values, 0.0), axis=(1, 2)).astype(jnp.bfloat16)
    chosen = jnp.any(matches, axis=2).astype(jnp.bfloat16)
    input_send = jnp.einsum(
        "rge,rgd->red",
        chosen,
        tokens.reshape(rounds, per_round, features),
        preferred_element_type=jnp.float32,
    ).astype(jnp.bfloat16)
    upstream_send = jnp.einsum(
        "rge,rgd->red",
        chosen,
        grad_out.reshape(rounds, per_round, features),
        preferred_element_type=jnp.float32,
    ).astype(jnp.bfloat16)
    input_recv, upstream_recv, gate_recv = (
        lax.all_to_all(input_send, ("da", "db"), split_axis=1, concat_axis=1, tiled=True),
        lax.all_to_all(upstream_send, ("da", "db"), split_axis=1, concat_axis=1, tiled=True),
        lax.all_to_all(gate_table, ("da", "db"), split_axis=1, concat_axis=1, tiled=True),
    )
    input_rows = input_recv.reshape(-1, features)
    upstream_rows = upstream_recv.reshape(-1, features)
    gate_rows = gate_recv.reshape(-1, 1).astype(jnp.float32)
    w_in, w_out = (
        lax.all_gather(w_gate_up[0], "replica", axis=0, tiled=True),
        lax.all_gather(w_down[0], "replica", axis=0, tiled=True),
    )
    projected = jnp.dot(input_rows, w_in, preferred_element_type=jnp.float32)
    back_raw = jnp.einsum("rd,fd->rf", upstream_rows, w_out, preferred_element_type=jnp.float32)
    gate_part = projected[:, :hidden_units]
    up_part = projected[:, hidden_units:]
    activated, derivative = silu_parts(gate_part)
    hidden = (activated * up_part).astype(jnp.bfloat16)
    gate_scores = jnp.sum(hidden.astype(jnp.float32) * back_raw, axis=1).astype(jnp.bfloat16)
    back_hidden = gate_rows * back_raw
    grad_projected = jnp.concatenate(
        [back_hidden * up_part * derivative, back_hidden * activated], axis=1
    ).astype(jnp.bfloat16)
    scaled_upstream = (gate_rows * upstream_rows.astype(jnp.float32)).astype(jnp.bfloat16)
    input_grads = jnp.einsum("rf,df->rd", grad_projected, w_in, preferred_element_type=jnp.float32)
    input_grads = input_grads.astype(jnp.bfloat16).reshape(rounds, experts, features)
    score_back = gate_scores.reshape(rounds, experts)
    returned, score_ret = (
        lax.all_to_all(input_grads, ("da", "db"), split_axis=1, concat_axis=1, tiled=True),
        lax.all_to_all(score_back, ("da", "db"), split_axis=1, concat_axis=1, tiled=True),
    )
    score_ret = score_ret.reshape(rounds, 1, 1, experts).astype(jnp.float32)
    token_grads = (
        jnp.einsum("rge,red->rgd", chosen, returned, preferred_element_type=jnp.float32)
        .astype(jnp.bfloat16)
        .reshape(local_tokens, features)
    )
    gate_grads = (
        jnp.sum(jnp.where(matches, score_ret, 0.0), axis=3)
        .astype(jnp.bfloat16)
        .reshape(local_tokens, top_count)
    )
    columns = input_rows
    grad_in = lax.psum_scatter(
        jnp.einsum("rd,rf->df", columns, grad_projected, preferred_element_type=jnp.float32).astype(
            jnp.bfloat16
        ),
        "replica",
        scatter_dimension=0,
        tiled=True,
    )
    columns = hidden
    grad_down = lax.psum_scatter(
        jnp.einsum(
            "rf,rd->fd", columns, scaled_upstream, preferred_element_type=jnp.float32
        ).astype(jnp.bfloat16),
        "replica",
        scatter_dimension=0,
        tiled=True,
    )
    return (token_grads, gate_grads, grad_in[None], grad_down[None])


def visit(j, z, n):
    m = jnp.minimum(z, n - 1 - z)
    near = z + (1 - 2 * (j % 2)) * ((j + 1) // 2)
    far = jnp.where(z < n - 1 - z, j, n - 1 - j)
    return jnp.where(j <= 2 * m, near, far)


def dot(a, b, dims):
    return lax.dot_general(a, b, (dims, ((), ())), preferred_element_type=jnp.float32)


def position(d, z, n):
    away = abs(d - z)
    if away <= min(z, n - 1 - z):
        return 2 * away - (1 if d < z else 0)
    return d if z < n - 1 - z else n - 1 - d


def relay_slots(n):
    last = 2 * n - 1

    def ready(z, d, h):
        k = position(d, z, n)
        k = last - k if h else k
        feeds = [u for u in (z - 1, z + 1) if 0 <= u < n and abs(u - d) == abs(z - d) + 1]
        return max([k + 2] + [ready(u, d, h) + 1 for u in feeds])

    table = []
    for z in range(n):
        row = [0] * (2 * n)
        for d in range(n):
            k = position(d, z, n)
            row[k] = ready(z, d, 0)
            row[last - k] = ready(z, d, 1)
        table.append(row)
    return table


def lag_words(n):
    return [sum((at - k - 2) * 8**k for k, at in enumerate(row)) for row in relay_slots(n)]


def fused_kernel(
    cols, depth, group,
    tok_hbm, up_hbm, routes_hbm, gates_hbm, win_hbm, wout_hbm,
    tg_ref, gg_ref, gin_ref, gdown_ref,
    routes_ref, gates_ref, tok, up, table, win, wout, xs, su, hid, gp, igs, igb, acc, cs, cr, rk, rx, scs, scr,
    load_sem, recv_sem, chart_sem, near_sem, near_chart_sem, igr_sem, cr_sem, rx_sem, scr_sem, sent_sem,
):
    da = lax.axis_index("da")
    z = lax.axis_index("db")
    x, c = da // CORES, da % CORES
    half, features = tok.shape[2], tok.shape[3]
    local = HALVES * half
    experts = table.shape[1]
    top = routes_ref.shape[0]
    rows = half // group
    ff = wout.shape[0]
    steps = HALVES * depth

    def slot(xx, zz, cc):
        return (xx * CORES + cc) * depth + zz

    me = slot(x, z, c)
    loads = []
    for h in range(HALVES):
        span = pl.ds(h * half, half)
        loads.append(pltpu.make_async_copy(tok_hbm.at[span], tok.at[me, h], load_sem.at[0]))
        loads.append(pltpu.make_async_copy(up_hbm.at[span], up.at[me, h], load_sem.at[0]))
    loads += [
        pltpu.make_async_copy(win_hbm.at[0], win, load_sem.at[1]),
        pltpu.make_async_copy(wout_hbm.at[0], wout, load_sem.at[2]),
        pltpu.make_async_copy(routes_hbm, routes_ref, load_sem.at[3]),
        pltpu.make_async_copy(gates_hbm, gates_ref, load_sem.at[4]),
    ]
    def settle(view, sem):
        pltpu.make_async_copy(view, view, sem).wait()

    barrier = pltpu.get_barrier_semaphore()
    count = cols * CORES * depth

    def greet(xx, zz, cc):
        pl.semaphore_signal(
            barrier, inc=1, device_id={"da": xx * CORES + cc, "db": zz}, device_id_type=MESH
        )

    @pl.when(z > 0)
    def _():
        greet(x, z - 1, c)

    @pl.when(z < depth - 1)
    def _():
        greet(x, z + 1, c)

    greet(1 - x, z, c)
    greet(x, z, 1 - c)
    for k in (6, 7, 0, 1, 2, 3, 4, 5):
        loads[k].start()

    loads[6].wait()
    loads[7].wait()
    routes = routes_ref[...]
    gates = gates_ref[...].astype(jnp.float32)
    ids = lax.broadcasted_iota(jnp.int32, (experts, local), 0)
    chart = jnp.zeros((experts, local), jnp.float32)
    for k in range(top):
        chart = chart + jnp.where(routes[k : k + 1] == ids, gates[k : k + 1], 0.0)
    table[me] = chart.astype(jnp.bfloat16)

    settle(tok.at[pl.ds(0, CORES)], load_sem.at[0])
    pl.semaphore_wait(barrier, 2 + jnp.where(z > 0, 1, 0) + jnp.where(z < depth - 1, 1, 0))

    held = (tok, up)

    def send(src, dst, send_sem, recv, to_x, to_z, to_c):
        return pltpu.make_async_remote_copy(
            src_ref=src,
            dst_ref=dst,
            send_sem=send_sem,
            recv_sem=recv,
            device_id={"da": to_x * CORES + to_c, "db": to_z},
            device_id_type=MESH,
        )

    def start(copy):
        copy.start()

    def wait_recv(copy):
        copy.wait_recv()

    def both(xx, zz, h, a, way, act, to_x, to_z, to_c, near=None):
        s = slot(xx, zz, c)
        ref = held[a].at[s, h]
        landed = recv_sem.at[xx, zz, h, a] if near is None else near_sem.at[near]
        act(send(ref, ref, sent_sem.at[way], landed, to_x, to_z, to_c))
        if a == 0:

            @pl.when(h == 0)
            def _():
                ref = table.at[s]
                landed = chart_sem.at[xx, zz] if near is None else near_chart_sem.at[zz]
                act(send(ref, ref, sent_sem.at[3 + (way > 0)], landed, to_x, to_z, to_c))

    def step_of(i):
        j = jnp.minimum(i, steps - 1 - i)
        return visit(j, z, depth), jnp.where(i >= depth, 1, 0)

    def along_z(e, a):
        def one(reach, sign):
            last = 2 * reach + 1
            k = jnp.minimum(e, last - e)
            h = jnp.where(e > reach, 1, 0)
            zz = z + sign * k

            @pl.when((e <= last) & (k > 0))
            def _():
                both(x, zz, h, a, 0, wait_recv, x, z, 1 - c)

            ahead = z - sign

            @pl.when((e <= last) & (ahead >= 0) & (ahead < depth))
            def _():
                both(x, zz, h, a, 0, start, x, ahead, c)

        one(depth - 1 - z, 1)
        one(z, -1)

    def across(i, a):
        zz, h = step_of(i)
        both(x, zz, h, a, 1, start, 1 - x, z, c)
        both(x, zz, h, a, 2, start, x, z, 1 - c, near=i)

    def from_across(i, a):
        zz, h = step_of(i)
        both(1 - x, zz, h, a, 1, wait_recv, 1 - x, z, c)
        both(1 - x, zz, h, a, 2, start, x, z, 1 - c, near=i)

    def from_partner(i):
        zz, h = step_of(i)
        settle(tok.at[pl.ds(0, cols)], near_sem.at[i])

        @pl.when(h == 0)
        def _():
            settle(table.at[pl.ds(0, cols)], near_chart_sem.at[zz])

    def pick(s, e, h):
        chart_s = table[s].astype(jnp.float32)
        which = lax.broadcasted_iota(jnp.int32, chart_s.shape, 0) == e
        row = jnp.sum(jnp.where(which, chart_s, 0.0), axis=0, keepdims=True)
        row = jnp.where(h == 0, row[:, :half], row[:, half:])
        off = lax.broadcasted_iota(jnp.int32, (rows, half), 1) - group * lax.broadcasted_iota(
            jnp.int32, (rows, half), 0
        )
        hit = (off >= 0) & (off < group) & (row > 0.0)
        return jnp.where(hit, 1.0, 0.0), row

    def send_ig(q, k):
        return send(igs.at[k, q], igb.at[k, q, c], sent_sem.at[5], igr_sem.at[k, q], x, z, 1 - c)

    def send_score(s):
        return pltpu.make_async_remote_copy(
            src_ref=scs.at[s],
            dst_ref=scr.at[me],
            send_sem=sent_sem.at[7],
            recv_sem=scr_sem.at[0],
            device_id={"da": s // depth, "db": s % depth},
            device_id_type=MESH,
        )

    blocks = [(q, r) for q in range(cols) for r in range(CORES)]
    batch = len(blocks) * rows

    def compute(k):
        zz, h = step_of(k)
        base = pl.multiple_of(k * batch, batch)
        picks = []
        gate_cols = []
        for n, (q, r) in enumerate(blocks):
            s = slot((x + q) % cols, zz, (c + r) % CORES)
            chosen, row = pick(s, me, h)
            picks.append((s, chosen))
            gate_cols.append(jnp.sum(chosen * row, axis=1, keepdims=True))
            hot = chosen.astype(jnp.bfloat16)
            where = pl.ds(pl.multiple_of(base + n * rows, rows), rows)
            xs[where, :] = dot(hot, tok[s, h], ((1,), (0,))).astype(jnp.bfloat16)
            su[where, :] = dot(hot, up[s, h], ((1,), (0,))).astype(jnp.bfloat16)
        here = pl.ds(base, batch)
        gate = jnp.concatenate(gate_cols, axis=0)
        upstream = su[here, :]
        projected = dot(xs[here, :], win[...], ((1,), (0,)))
        back_raw = dot(upstream, wout[...], ((1,), (1,)))
        su[here, :] = (gate * upstream.astype(jnp.float32)).astype(jnp.bfloat16)
        gate_part, up_part = projected[:, :ff], projected[:, ff:]
        activated, derivative = silu_parts(gate_part)
        hidden = (activated * up_part).astype(jnp.bfloat16)
        hid[here, :] = hidden
        scores = jnp.sum(hidden.astype(jnp.float32) * back_raw, axis=1, keepdims=True)
        scores = scores.astype(jnp.bfloat16).astype(jnp.float32)
        back_hidden = gate * back_raw
        gp[here, :ff] = (back_hidden * up_part * derivative).astype(jnp.bfloat16)
        gp[here, ff:] = (back_hidden * activated).astype(jnp.bfloat16)
        grads = dot(gp[here, :], win[...], ((1,), (1,))).astype(jnp.bfloat16)
        for n, (q, r) in enumerate(blocks):
            piece = grads[n * rows : (n + 1) * rows]
            if r == 0:
                igb[k, q, c] = piece
            else:
                igs[k, q] = piece
                send_ig(q, k).start()
        for n, (q, r) in enumerate(blocks):
            s, chosen = picks[n]
            line = jnp.sum(chosen * scores[n * rows : (n + 1) * rows], axis=0, keepdims=True)
            rest = jnp.zeros_like(line)
            first = jnp.concatenate([line, rest], axis=1)
            second = jnp.concatenate([rest, line], axis=1)

            @pl.when(h == 0)
            def _():
                scs[s] = jnp.broadcast_to(first, scs.shape[1:])

            @pl.when(h == 1)
            def _():
                scs[s] = scs[s] + jnp.broadcast_to(second, scs.shape[1:])
                if q == 0 and r == 0:

                    @pl.when(zz == z)
                    def _():
                        scr[me] = scs[me]

                    @pl.when(zz != z)
                    def _():
                        send_score(s).start()
                else:
                    send_score(s).start()

    def chip_sum(k, q):
        zz, h = step_of(k)
        s = slot((x + q) % cols, zz, c)
        hot = jnp.concatenate([pick(s, slot(x, z, m), h)[0] for m in range(CORES)], axis=0)
        pair = igb[k, q].reshape(CORES * rows, features)
        return dot(hot.astype(jnp.bfloat16), pair, ((0,), (0,)))

    def send_sum(zz, h, q, side, to_z):
        place = jnp.where((zz == to_z) & (side == 1), depth, zz)
        landed = cr.at[place, h, q]
        return send(cs.at[zz, h, q], landed, sent_sem.at[6], cr_sem.at[place, h, q], x, to_z, c)

    def send_across(h):
        return send(cs.at[z, h, 1], rx.at[h], sent_sem.at[6], rx_sem.at[h], 1 - x, z, c)

    def pass_on(k, q):
        zz, h = step_of(k)
        send_ig(q, k).wait_recv()
        acc[...] = chip_sum(k, q)
        for side, ok in ((0, (zz <= z) & (z < depth - 1)), (1, (zz >= z) & (z > 0))):

            @pl.when(ok)
            def _():
                send_sum(zz, h, q, side, z).wait_recv()
                place = jnp.where((zz == z) & (side == 1), depth, zz)
                acc[...] += cr[place, h, q].astype(jnp.float32)

        if q == 0:

            @pl.when(zz == z)
            def _():
                rk[h] = acc[...]

        @pl.when((zz != z) if q == 0 else True)
        def _():
            cs[zz, h, q] = acc[...].astype(jnp.bfloat16)

        @pl.when(zz < z)
        def _():
            send_sum(zz, h, q, 0, z - 1).start()

        @pl.when(zz > z)
        def _():
            send_sum(zz, h, q, 1, z + 1).start()

        if q == 1:

            @pl.when(zz == z)
            def _():
                send_across(h).start()

    words = lag_words(depth)
    word = jnp.int32(words[0])
    for k in range(1, depth):
        word = jnp.where(z == k, words[k], word)

    edge = (z == 0) | (z == depth - 1)

    def pass_all(i, q, which=None):
        def one(k, left):
            due = k + 2 + left % 8 == i
            if which is not None:
                due = due & which(step_of(k)[0] == z)

            @pl.when(due)
            def _():
                pass_on(k, q)

            return left // 8

        lax.fori_loop(0, jnp.minimum(i - 1, steps), one, word)

    def head(home):
        return edge & jnp.logical_not(home)

    def inner(home):
        return jnp.logical_not(head(home))

    def away(home):
        return jnp.logical_not(home)

    along_z(0, 0)
    across(0, 0)

    def step(i, carry):
        @pl.when(i < steps)
        def _():
            along_z(i, 1)
            across(i, 1)

        @pl.when(i == 0)
        def _():
            loads[4].wait()
            loads[5].wait()

        @pl.when(i == steps)
        def _():
            pass_all(i, 1)

        @pl.when(i >= 1)
        def _():
            from_across(i - 1, 1)

        @pl.when((i >= 2) & (i < steps))
        def _():
            pass_all(i, 1)
            pass_all(i, 0, head)

        @pl.when(i == steps)
        def _():
            pass_all(i, 0, away)

        @pl.when(i >= 1)
        def _():
            from_partner(i - 1)
            compute(i - 1)

        @pl.when(i + 1 < steps)
        def _():
            along_z(i + 1, 0)
            across(i + 1, 0)

        @pl.when((i >= 2) & (i < steps))
        def _():
            pass_all(i, 0, inner)

        @pl.when(i < steps)
        def _():
            from_across(i, 0)

        return carry

    lax.fori_loop(0, steps + 1, step, 0)
    pass_all(steps + 1, 1)

    wide = min(features, 256)

    @pl.loop(0, features // wide)
    def _(t):
        at = pl.ds(pl.multiple_of(t * wide, wide), wide)
        gin_ref[0, at, :] = dot(xs[:, at], gp[...], ((0,), (0,))).astype(jnp.bfloat16)

    thin = 128

    @pl.loop(0, ff // thin)
    def _(t):
        at = pl.ds(pl.multiple_of(t * thin, thin), thin)
        gdown_ref[0, at, :] = dot(hid[:, at], su[...], ((0,), (0,))).astype(jnp.bfloat16)

    def home(is_home):
        return is_home

    pass_all(steps, 0, home)
    pass_all(steps + 1, 0)
    settle(scr.at[pl.ds(0, count - 1)], scr_sem.at[0])
    scores = scr[:, 0, :]
    place = lax.broadcasted_iota(jnp.int32, (top, local), 0)
    gate_grads = jnp.zeros((top, local), jnp.float32)
    for k in range(top):
        value = jnp.sum(jnp.where(routes[k : k + 1] == ids, scores, 0.0), axis=0, keepdims=True)
        gate_grads = jnp.where(place == k, value, gate_grads)
    gg_ref[...] = gate_grads.astype(jnp.bfloat16)

    for h in range(HALVES):
        send_across(h).wait_recv()
        tg_ref[pl.ds(h * half, half), :] = (rk[h] + rx[h].astype(jnp.float32)).astype(jnp.bfloat16)

    for at in range(depth):
        sent = (depth - at if at > 0 else 0) + (at + 1 if at < depth - 1 else 0)

        @pl.when(z == at)
        def _():
            settle(tok.at[pl.ds(0, 2 * sent)], sent_sem.at[0])
            settle(table.at[pl.ds(0, sent)], sent_sem.at[3])

    settle(tok.at[pl.ds(0, 2 * depth)], sent_sem.at[1])
    settle(tok, sent_sem.at[2])
    settle(table.at[pl.ds(0, 3 * depth)], sent_sem.at[4])
    settle(igs, sent_sem.at[5])
    settle(tok.at[pl.ds(0, depth * cols - 1)], sent_sem.at[6])
    settle(scs.at[pl.ds(0, count - 1)], sent_sem.at[7])


def store_kernel(*refs):
    count = len(refs) // 2
    sems = refs[-1]
    copies = [
        pltpu.make_async_copy(refs[k], refs[count + k], sems.at[k]) for k in range(count)
    ]
    for one in copies:
        one.start()
    for one in copies:
        one.wait()


def store(*arrays):
    anywhere = pl.BlockSpec(memory_space=pl.ANY)
    return pl.pallas_call(
        store_kernel,
        out_shape=tuple(jax.ShapeDtypeStruct(a.shape, a.dtype) for a in arrays),
        in_specs=[pl.BlockSpec(memory_space=pltpu.VMEM)] * len(arrays),
        out_specs=(pl.BlockSpec(memory_space=pltpu.HBM),) * len(arrays),
        scratch_shapes=[pltpu.SemaphoreType.DMA((len(arrays),))],
        compiler_params=pltpu.CompilerParams(vmem_limit_bytes=8 * 2**20),
    )(*arrays)


def fused(tokens, grad_out, routes, gates, w_gate_up, w_down):
    first_size, depth = lax.axis_size("da"), lax.axis_size("db")
    cols = first_size // CORES
    experts = first_size * depth
    local, features = tokens.shape
    top = routes.shape[1]
    group = experts // top
    ff = w_down.shape[1]
    bf, f32 = jnp.bfloat16, jnp.float32
    half = local // HALVES
    rows = half // group
    steps = HALVES * depth
    total = rows * experts * HALVES
    dma = pltpu.SemaphoreType.DMA
    scratch = [
        pltpu.VMEM((top, local), routes.dtype),
        pltpu.VMEM((top, local), gates.dtype),
        pltpu.VMEM((experts, HALVES, half, features), bf),
        pltpu.VMEM((experts, HALVES, half, features), bf),
        pltpu.VMEM((experts, experts, local), bf),
        pltpu.VMEM((features, 2 * ff), bf),
        pltpu.VMEM((ff, features), bf),
        pltpu.VMEM((total, features), bf),
        pltpu.VMEM((total, features), bf),
        pltpu.VMEM((total, ff), bf),
        pltpu.VMEM((total, 2 * ff), bf),
        pltpu.VMEM((steps, cols, rows, features), bf),
        pltpu.VMEM((steps, cols, CORES, rows, features), bf),
        pltpu.VMEM((half, features), f32),
        pltpu.VMEM((depth, HALVES, cols, half, features), bf),
        pltpu.VMEM((depth + 1, HALVES, cols, half, features), bf),
        pltpu.VMEM((HALVES, half, features), f32),
        pltpu.VMEM((HALVES, half, features), bf),
        pltpu.VMEM((experts, 8, local), f32),
        pltpu.VMEM((experts, 8, local), f32),
        dma((5,)),
        dma((cols, depth, HALVES, 2)),
        dma((cols, depth)),
        dma((steps,)),
        dma((depth,)),
        dma((steps, cols)),
        dma((depth + 1, HALVES, cols)),
        dma((HALVES,)),
        dma((1,)),
        dma((8,)),
    ]
    vmem = pl.BlockSpec(memory_space=pltpu.VMEM)
    hbm = pl.BlockSpec(memory_space=pltpu.HBM)
    token_grads, gate_grads, grad_in, grad_down = pl.pallas_call(
        functools.partial(fused_kernel, cols, depth, group),
        out_shape=(
            jax.ShapeDtypeStruct((local, features), bf),
            jax.ShapeDtypeStruct((top, local), bf),
            jax.ShapeDtypeStruct(w_gate_up.shape, bf),
            jax.ShapeDtypeStruct(w_down.shape, bf),
        ),
        in_specs=[hbm] * 6,
        out_specs=(vmem, vmem, vmem, vmem),
        scratch_shapes=scratch,
        compiler_params=pltpu.CompilerParams(
            collective_id=0, has_side_effects=True, vmem_limit_bytes=44 * 2**20
        ),
    )(
        *(
            pltpu.with_memory_space_constraint(a, pltpu.HBM)
            for a in (tokens, grad_out, routes.T, gates.T, w_gate_up, w_down)
        )
    )
    token_grads, gate_grads, grad_in, grad_down = store(token_grads, gate_grads, grad_in, grad_down)
    return token_grads, gate_grads.T, grad_in, grad_down


def fits(tokens, routes, w_down):
    first_size = lax.axis_size("da")
    experts = first_size * lax.axis_size("db")
    local, features = tokens.shape
    group = experts // routes.shape[1]
    held = 2 * experts * local * features * 2
    return (
        lax.axis_size("replica") == 1
        and first_size % CORES == 0
        and first_size == 2 * CORES
        and 2 * 3 * lax.axis_size("db") <= 30
        and held <= 16 * 2**20
        and local == 128
        and experts <= local
        and max(map(max, relay_slots(lax.axis_size("db")))) == HALVES * lax.axis_size("db") + 1
        and (local // (HALVES * group)) % 16 == 0
        and w_down.shape[1] % 128 == 0
    )


def route(*arrays):
    if fits(arrays[0], arrays[2], arrays[5]):
        return fused(*arrays)
    return body(*arrays)


def solution(mesh):
    placed = (
        P(("groups", "replica", "da", "db"), None),
        P(("groups", "replica", "da", "db"), None),
        P(("groups", "replica", "da", "db"), None),
        P(("groups", "replica", "da", "db"), None),
        P(("da", "db"), "replica", None),
        P(("da", "db"), "replica", None),
    )
    return jax.shard_map(
        route,
        mesh=mesh,
        in_specs=placed,
        out_specs=(
            P(("groups", "replica", "da", "db"), None),
            P(("groups", "replica", "da", "db"), None),
            P(("groups", "da", "db"), "replica", None),
            P(("groups", "da", "db"), "replica", None),
        ),
        check_vma=False,
    )
```

```python
import functools

import jax
import jax.numpy as jnp
from jax import lax
from jax.experimental import pallas as pl
from jax.experimental.pallas import tpu as pltpu
from jax.sharding import PartitionSpec as P


CORES = 2
HALVES = 2
MESH = pl.DeviceIdType.MESH


def silu_parts(projected):
    sigmoid = jax.nn.sigmoid(projected)
    return (projected * sigmoid, sigmoid * (1.0 + projected * (1.0 - sigmoid)))


def body(tokens, grad_out, routes, gates, w_gate_up, w_down):
    local_tokens, features = tokens.shape
    top_count = routes.shape[1]
    hidden_units = w_gate_up.shape[2] // 2
    first_size = lax.axis_size("da")
    second_size = lax.axis_size("db")
    experts = first_size * second_size
    per_round = experts // top_count
    rounds = local_tokens // per_round
    expert_ids = lax.broadcasted_iota(jnp.int32, (1, 1, 1, experts), 3)
    matches = routes.reshape(rounds, per_round, top_count, 1) == expert_ids
    gate_values = gates.reshape(rounds, per_round, top_count, 1).astype(jnp.float32)
    gate_table = jnp.sum(jnp.where(matches, gate_values, 0.0), axis=(1, 2)).astype(jnp.bfloat16)
    chosen = jnp.any(matches, axis=2).astype(jnp.bfloat16)
    input_send = jnp.einsum(
        "rge,rgd->red",
        chosen,
        tokens.reshape(rounds, per_round, features),
        preferred_element_type=jnp.float32,
    ).astype(jnp.bfloat16)
    upstream_send = jnp.einsum(
        "rge,rgd->red",
        chosen,
        grad_out.reshape(rounds, per_round, features),
        preferred_element_type=jnp.float32,
    ).astype(jnp.bfloat16)
    input_recv, upstream_recv, gate_recv = (
        lax.all_to_all(input_send, ("da", "db"), split_axis=1, concat_axis=1, tiled=True),
        lax.all_to_all(upstream_send, ("da", "db"), split_axis=1, concat_axis=1, tiled=True),
        lax.all_to_all(gate_table, ("da", "db"), split_axis=1, concat_axis=1, tiled=True),
    )
    input_rows = input_recv.reshape(-1, features)
    upstream_rows = upstream_recv.reshape(-1, features)
    gate_rows = gate_recv.reshape(-1, 1).astype(jnp.float32)
    w_in, w_out = (
        lax.all_gather(w_gate_up[0], "replica", axis=0, tiled=True),
        lax.all_gather(w_down[0], "replica", axis=0, tiled=True),
    )
    projected = jnp.dot(input_rows, w_in, preferred_element_type=jnp.float32)
    back_raw = jnp.einsum("rd,fd->rf", upstream_rows, w_out, preferred_element_type=jnp.float32)
    gate_part = projected[:, :hidden_units]
    up_part = projected[:, hidden_units:]
    activated, derivative = silu_parts(gate_part)
    hidden = (activated * up_part).astype(jnp.bfloat16)
    gate_scores = jnp.sum(hidden.astype(jnp.float32) * back_raw, axis=1).astype(jnp.bfloat16)
    back_hidden = gate_rows * back_raw
    grad_projected = jnp.concatenate(
        [back_hidden * up_part * derivative, back_hidden * activated], axis=1
    ).astype(jnp.bfloat16)
    scaled_upstream = (gate_rows * upstream_rows.astype(jnp.float32)).astype(jnp.bfloat16)
    input_grads = jnp.einsum("rf,df->rd", grad_projected, w_in, preferred_element_type=jnp.float32)
    input_grads = input_grads.astype(jnp.bfloat16).reshape(rounds, experts, features)
    score_back = gate_scores.reshape(rounds, experts)
    returned, score_ret = (
        lax.all_to_all(input_grads, ("da", "db"), split_axis=1, concat_axis=1, tiled=True),
        lax.all_to_all(score_back, ("da", "db"), split_axis=1, concat_axis=1, tiled=True),
    )
    score_ret = score_ret.reshape(rounds, 1, 1, experts).astype(jnp.float32)
    token_grads = (
        jnp.einsum("rge,red->rgd", chosen, returned, preferred_element_type=jnp.float32)
        .astype(jnp.bfloat16)
        .reshape(local_tokens, features)
    )
    gate_grads = (
        jnp.sum(jnp.where(matches, score_ret, 0.0), axis=3)
        .astype(jnp.bfloat16)
        .reshape(local_tokens, top_count)
    )
    columns = input_rows
    grad_in = lax.psum_scatter(
        jnp.einsum("rd,rf->df", columns, grad_projected, preferred_element_type=jnp.float32).astype(
            jnp.bfloat16
        ),
        "replica",
        scatter_dimension=0,
        tiled=True,
    )
    columns = hidden
    grad_down = lax.psum_scatter(
        jnp.einsum(
            "rf,rd->fd", columns, scaled_upstream, preferred_element_type=jnp.float32
        ).astype(jnp.bfloat16),
        "replica",
        scatter_dimension=0,
        tiled=True,
    )
    return (token_grads, gate_grads, grad_in[None], grad_down[None])


def visit(j, z, n):
    m = jnp.minimum(z, n - 1 - z)
    near = z + (1 - 2 * (j % 2)) * ((j + 1) // 2)
    far = jnp.where(z < n - 1 - z, j, n - 1 - j)
    return jnp.where(j <= 2 * m, near, far)


def dot(a, b, dims):
    return lax.dot_general(a, b, (dims, ((), ())), preferred_element_type=jnp.float32)


def position(d, z, n):
    away = abs(d - z)
    if away <= min(z, n - 1 - z):
        return 2 * away - (1 if d < z else 0)
    return d if z < n - 1 - z else n - 1 - d


def relay_slots(n):
    last = 2 * n - 1

    def ready(z, d, h):
        k = position(d, z, n)
        k = last - k if h else k
        feeds = [u for u in (z - 1, z + 1) if 0 <= u < n and abs(u - d) == abs(z - d) + 1]
        return max([k + 2] + [ready(u, d, h) + 1 for u in feeds])

    table = []
    for z in range(n):
        row = [0] * (2 * n)
        for d in range(n):
            k = position(d, z, n)
            row[k] = ready(z, d, 0)
            row[last - k] = ready(z, d, 1)
        table.append(row)
    return table


def lag_words(n):
    return [sum((at - k - 2) * 8 ** (2 * n - 1 - k) for k, at in enumerate(row)) for row in relay_slots(n)]


def fused_kernel(
    cols, depth, group,
    tok_hbm, up_hbm, routes_hbm, gates_hbm, win_hbm, wout_hbm,
    tg_ref, gg_ref, gin_ref, gdown_ref,
    routes_ref, gates_ref, tok, up, table, win, wout, xs, su, hid, gp, igs, igb, acc, cs, cr, rk, rx, scs, scr,
    load_sem, recv_sem, chart_sem, near_sem, near_chart_sem, igr_sem, cr_sem, rx_sem, scr_sem, sent_sem,
):
    da = lax.axis_index("da")
    z = lax.axis_index("db")
    x, c = da // CORES, da % CORES
    half, features = tok.shape[2], tok.shape[3]
    local = HALVES * half
    experts = table.shape[1]
    top = routes_ref.shape[0]
    rows = half // group
    ff = wout.shape[0]
    steps = HALVES * depth

    def slot(xx, zz, cc):
        return (xx * CORES + cc) * depth + zz

    me = slot(x, z, c)
    loads = []
    for h in range(HALVES):
        span = pl.ds(h * half, half)
        loads.append(pltpu.make_async_copy(tok_hbm.at[span], tok.at[me, h], load_sem.at[0]))
        loads.append(pltpu.make_async_copy(up_hbm.at[span], up.at[me, h], load_sem.at[0]))
    loads += [
        pltpu.make_async_copy(win_hbm.at[0], win, load_sem.at[1]),
        pltpu.make_async_copy(wout_hbm.at[0], wout, load_sem.at[2]),
        pltpu.make_async_copy(routes_hbm, routes_ref, load_sem.at[3]),
        pltpu.make_async_copy(gates_hbm, gates_ref, load_sem.at[4]),
    ]
    def settle(view, sem):
        pltpu.make_async_copy(view, view, sem).wait()

    barrier = pltpu.get_barrier_semaphore()
    count = cols * CORES * depth

    def greet(xx, zz, cc):
        pl.semaphore_signal(
            barrier, inc=1, device_id={"da": xx * CORES + cc, "db": zz}, device_id_type=MESH
        )

    @pl.when(z > 0)
    def _():
        greet(x, z - 1, c)

    @pl.when(z < depth - 1)
    def _():
        greet(x, z + 1, c)

    greet(1 - x, z, c)
    greet(x, z, 1 - c)
    for k in (6, 7, 0, 1, 2, 3, 4, 5):
        loads[k].start()

    loads[6].wait()
    loads[7].wait()
    routes = routes_ref[...]
    gates = gates_ref[...].astype(jnp.float32)
    ids = lax.broadcasted_iota(jnp.int32, (experts, local), 0)
    chart = jnp.zeros((experts, local), jnp.float32)
    for k in range(top):
        chart = chart + jnp.where(routes[k : k + 1] == ids, gates[k : k + 1], 0.0)
    table[me] = chart.astype(jnp.bfloat16)

    settle(tok.at[pl.ds(0, CORES)], load_sem.at[0])
    pl.semaphore_wait(barrier, 2 + jnp.where(z > 0, 1, 0) + jnp.where(z < depth - 1, 1, 0))

    held = (tok, up)

    def send(src, dst, send_sem, recv, to_x, to_z, to_c):
        return pltpu.make_async_remote_copy(
            src_ref=src,
            dst_ref=dst,
            send_sem=send_sem,
            recv_sem=recv,
            device_id={"da": to_x * CORES + to_c, "db": to_z},
            device_id_type=MESH,
        )

    def start(copy):
        copy.start()

    def wait_recv(copy):
        copy.wait_recv()

    def both(xx, zz, h, a, way, act, to_x, to_z, to_c, near=None):
        s = slot(xx, zz, c)
        ref = held[a].at[s, h]
        landed = recv_sem.at[xx, zz, h, a] if near is None else near_sem.at[near]
        act(send(ref, ref, sent_sem.at[way], landed, to_x, to_z, to_c))
        if a == 0:

            @pl.when(h == 0)
            def _():
                ref = table.at[s]
                landed = chart_sem.at[xx, zz] if near is None else near_chart_sem.at[zz]
                act(send(ref, ref, sent_sem.at[3 + (way > 0)], landed, to_x, to_z, to_c))

    def step_of(i):
        j = jnp.minimum(i, steps - 1 - i)
        return visit(j, z, depth), jnp.where(i >= depth, 1, 0)

    def along_z(e, a):
        def one(reach, sign):
            last = 2 * reach + 1
            k = jnp.minimum(e, last - e)
            h = jnp.where(e > reach, 1, 0)
            zz = z + sign * k

            @pl.when((e <= last) & (k > 0))
            def _():
                both(x, zz, h, a, 0, wait_recv, x, z, 1 - c)

            ahead = z - sign

            @pl.when((e <= last) & (ahead >= 0) & (ahead < depth))
            def _():
                both(x, zz, h, a, 0, start, x, ahead, c)

        one(depth - 1 - z, 1)
        one(z, -1)

    def across(i, a):
        zz, h = step_of(i)
        both(x, zz, h, a, 1, start, 1 - x, z, c)
        both(x, zz, h, a, 2, start, x, z, 1 - c, near=i)

    def from_across(i, a):
        zz, h = step_of(i)
        both(1 - x, zz, h, a, 1, wait_recv, 1 - x, z, c)
        both(1 - x, zz, h, a, 2, start, x, z, 1 - c, near=i)

    def from_partner(i):
        zz, h = step_of(i)
        settle(tok.at[pl.ds(0, cols)], near_sem.at[i])

        @pl.when(h == 0)
        def _():
            settle(table.at[pl.ds(0, cols)], near_chart_sem.at[zz])

    def pick(s, e, h):
        chart_s = table[s].astype(jnp.float32)
        which = lax.broadcasted_iota(jnp.int32, chart_s.shape, 0) == e
        row = jnp.sum(jnp.where(which, chart_s, 0.0), axis=0, keepdims=True)
        row = jnp.where(h == 0, row[:, :half], row[:, half:])
        off = lax.broadcasted_iota(jnp.int32, (rows, half), 1) - group * lax.broadcasted_iota(
            jnp.int32, (rows, half), 0
        )
        hit = (off >= 0) & (off < group) & (row > 0.0)
        return jnp.where(hit, 1.0, 0.0), row

    def send_ig(q, k):
        return send(igs.at[k, q], igb.at[k, q, c], sent_sem.at[5], igr_sem.at[k, q], x, z, 1 - c)

    def send_score(s):
        return pltpu.make_async_remote_copy(
            src_ref=scs.at[s],
            dst_ref=scr.at[me],
            send_sem=sent_sem.at[7],
            recv_sem=scr_sem.at[0],
            device_id={"da": s // depth, "db": s % depth},
            device_id_type=MESH,
        )

    blocks = [(q, r) for q in range(cols) for r in range(CORES)]
    batch = len(blocks) * rows

    def compute(k):
        zz, h = step_of(k)
        base = pl.multiple_of(k * batch, batch)
        picks = []
        gate_cols = []
        for n, (q, r) in enumerate(blocks):
            s = slot((x + q) % cols, zz, (c + r) % CORES)
            chosen, row = pick(s, me, h)
            picks.append((s, chosen))
            gate_cols.append(jnp.sum(chosen * row, axis=1, keepdims=True))
            hot = chosen.astype(jnp.bfloat16)
            where = pl.ds(pl.multiple_of(base + n * rows, rows), rows)
            xs[where, :] = dot(hot, tok[s, h], ((1,), (0,))).astype(jnp.bfloat16)
            su[where, :] = dot(hot, up[s, h], ((1,), (0,))).astype(jnp.bfloat16)
        here = pl.ds(base, batch)
        gate = jnp.concatenate(gate_cols, axis=0)
        upstream = su[here, :]
        projected = dot(xs[here, :], win[...], ((1,), (0,)))
        back_raw = dot(upstream, wout[...], ((1,), (1,)))
        su[here, :] = (gate * upstream.astype(jnp.float32)).astype(jnp.bfloat16)
        gate_part, up_part = projected[:, :ff], projected[:, ff:]
        activated, derivative = silu_parts(gate_part)
        hidden = (activated * up_part).astype(jnp.bfloat16)
        hid[here, :] = hidden
        scores = jnp.sum(hidden.astype(jnp.float32) * back_raw, axis=1, keepdims=True)
        scores = scores.astype(jnp.bfloat16).astype(jnp.float32)
        back_hidden = gate * back_raw
        gp[here, :ff] = (back_hidden * up_part * derivative).astype(jnp.bfloat16)
        gp[here, ff:] = (back_hidden * activated).astype(jnp.bfloat16)
        grads = dot(gp[here, :], win[...], ((1,), (1,))).astype(jnp.bfloat16)
        for n, (q, r) in enumerate(blocks):
            piece = grads[n * rows : (n + 1) * rows]
            if r == 0:
                igb[k, q, c] = piece
            else:
                igs[k, q] = piece
                send_ig(q, k).start()
        for n, (q, r) in enumerate(blocks):
            s, chosen = picks[n]
            line = jnp.sum(chosen * scores[n * rows : (n + 1) * rows], axis=0, keepdims=True)
            rest = jnp.zeros_like(line)
            first = jnp.concatenate([line, rest], axis=1)
            second = jnp.concatenate([rest, line], axis=1)

            @pl.when(h == 0)
            def _():
                scs[s] = jnp.broadcast_to(first, scs.shape[1:])

            @pl.when(h == 1)
            def _():
                scs[s] = scs[s] + jnp.broadcast_to(second, scs.shape[1:])
                if q == 0 and r == 0:

                    @pl.when(zz == z)
                    def _():
                        scr[me] = scs[me]

                    @pl.when(zz != z)
                    def _():
                        send_score(s).start()
                else:
                    send_score(s).start()

    def chip_sum(k, q):
        zz, h = step_of(k)
        s = slot((x + q) % cols, zz, c)
        hot = jnp.concatenate([pick(s, slot(x, z, m), h)[0] for m in range(CORES)], axis=0)
        pair = igb[k, q].reshape(CORES * rows, features)
        return dot(hot.astype(jnp.bfloat16), pair, ((0,), (0,)))

    def send_sum(zz, h, q, side, to_z):
        place = jnp.where((zz == to_z) & (side == 1), depth, zz)
        landed = cr.at[place, h, q]
        return send(cs.at[zz, h, q], landed, sent_sem.at[6], cr_sem.at[place, h, q], x, to_z, c)

    def send_across(h):
        return send(cs.at[z, h, 1], rx.at[h], sent_sem.at[6], rx_sem.at[h], 1 - x, z, c)

    def pass_on(k, q):
        zz, h = step_of(k)
        send_ig(q, k).wait_recv()
        acc[...] = chip_sum(k, q)
        for side, ok in ((0, (zz <= z) & (z < depth - 1)), (1, (zz >= z) & (z > 0))):

            @pl.when(ok)
            def _():
                send_sum(zz, h, q, side, z).wait_recv()
                place = jnp.where((zz == z) & (side == 1), depth, zz)
                acc[...] += cr[place, h, q].astype(jnp.float32)

        if q == 0:

            @pl.when(zz == z)
            def _():
                rk[h] = acc[...]

        @pl.when((zz != z) if q == 0 else True)
        def _():
            cs[zz, h, q] = acc[...].astype(jnp.bfloat16)

        @pl.when(zz < z)
        def _():
            send_sum(zz, h, q, 0, z - 1).start()

        @pl.when(zz > z)
        def _():
            send_sum(zz, h, q, 1, z + 1).start()

        if q == 1:

            @pl.when(zz == z)
            def _():
                send_across(h).start()

    words = lag_words(depth)
    word = jnp.int32(words[0])
    for k in range(1, depth):
        word = jnp.where(z == k, words[k], word)

    edge = (z == 0) | (z == depth - 1)
    inner = jnp.logical_not(edge)

    def pass_all(i, q):
        def one(j, left):
            k = steps - 1 - j
            due = (k + 2 + left % 8 == i) & (j > 0)

            @pl.when(due)
            def _():
                pass_on(k, q)

            return left // 8

        lax.fori_loop(0, steps - 1, one, word)

    along_z(0, 0)
    across(0, 0)

    def step(i, carry):
        @pl.when(i < steps)
        def _():
            along_z(i, 1)
            across(i, 1)

        @pl.when(i == 0)
        def _():
            loads[4].wait()
            loads[5].wait()

        @pl.when(inner & (i >= 2))
        def _():
            pass_all(i, 1)

        @pl.when(i >= 1)
        def _():
            from_across(i - 1, 1)

        @pl.when(inner & (i >= 2) & (i < steps))
        def _():
            pass_all(i, 0)

        @pl.when(i == steps)
        def _():
            pass_on(0, 1)

        @pl.when(i >= 1)
        def _():
            from_partner(i - 1)
            compute(i - 1)

        @pl.when(i + 1 < steps)
        def _():
            along_z(i + 1, 0)
            across(i + 1, 0)

        @pl.when(i < steps)
        def _():
            from_across(i, 0)

        @pl.when(edge & (i >= 1) & (i < steps))
        def _():
            pass_all(i + 1, 1)
            pass_all(i + 1, 0)

        return carry

    lax.fori_loop(0, steps + 1, step, 0)
    @pl.when(inner)
    def _():
        pass_all(steps, 0)

    pass_on(steps - 1, 1)

    wide = min(features, 256)

    @pl.loop(0, features // wide)
    def _(t):
        at = pl.ds(pl.multiple_of(t * wide, wide), wide)
        gin_ref[0, at, :] = dot(xs[:, at], gp[...], ((0,), (0,))).astype(jnp.bfloat16)

    thin = 128

    @pl.loop(0, ff // thin)
    def _(t):
        at = pl.ds(pl.multiple_of(t * thin, thin), thin)
        gdown_ref[0, at, :] = dot(hid[:, at], su[...], ((0,), (0,))).astype(jnp.bfloat16)

    pass_on(0, 0)
    pass_on(steps - 1, 0)
    settle(scr.at[pl.ds(0, count - 1)], scr_sem.at[0])
    scores = scr[:, 0, :]
    place = lax.broadcasted_iota(jnp.int32, (top, local), 0)
    gate_grads = jnp.zeros((top, local), jnp.float32)
    for k in range(top):
        value = jnp.sum(jnp.where(routes[k : k + 1] == ids, scores, 0.0), axis=0, keepdims=True)
        gate_grads = jnp.where(place == k, value, gate_grads)
    gg_ref[...] = gate_grads.astype(jnp.bfloat16)

    for h in range(HALVES):
        send_across(h).wait_recv()
        tg_ref[pl.ds(h * half, half), :] = (rk[h] + rx[h].astype(jnp.float32)).astype(jnp.bfloat16)

    for at in range(depth):
        sent = (depth - at if at > 0 else 0) + (at + 1 if at < depth - 1 else 0)

        @pl.when(z == at)
        def _():
            settle(tok.at[pl.ds(0, 2 * sent)], sent_sem.at[0])
            settle(table.at[pl.ds(0, sent)], sent_sem.at[3])

    settle(tok.at[pl.ds(0, 2 * depth)], sent_sem.at[1])
    settle(tok, sent_sem.at[2])
    settle(table.at[pl.ds(0, 3 * depth)], sent_sem.at[4])
    settle(igs, sent_sem.at[5])
    settle(tok.at[pl.ds(0, depth * cols - 1)], sent_sem.at[6])
    settle(scs.at[pl.ds(0, count - 1)], sent_sem.at[7])


def store_kernel(*refs):
    count = len(refs) // 2
    sems = refs[-1]
    copies = [
        pltpu.make_async_copy(refs[k], refs[count + k], sems.at[k]) for k in range(count)
    ]
    for one in copies:
        one.start()
    for one in copies:
        one.wait()


def store(*arrays):
    anywhere = pl.BlockSpec(memory_space=pl.ANY)
    return pl.pallas_call(
        store_kernel,
        out_shape=tuple(jax.ShapeDtypeStruct(a.shape, a.dtype) for a in arrays),
        in_specs=[pl.BlockSpec(memory_space=pltpu.VMEM)] * len(arrays),
        out_specs=(pl.BlockSpec(memory_space=pltpu.HBM),) * len(arrays),
        scratch_shapes=[pltpu.SemaphoreType.DMA((len(arrays),))],
        compiler_params=pltpu.CompilerParams(vmem_limit_bytes=8 * 2**20),
    )(*arrays)


def fused(tokens, grad_out, routes, gates, w_gate_up, w_down):
    first_size, depth = lax.axis_size("da"), lax.axis_size("db")
    cols = first_size // CORES
    experts = first_size * depth
    local, features = tokens.shape
    top = routes.shape[1]
    group = experts // top
    ff = w_down.shape[1]
    bf, f32 = jnp.bfloat16, jnp.float32
    half = local // HALVES
    rows = half // group
    steps = HALVES * depth
    total = rows * experts * HALVES
    dma = pltpu.SemaphoreType.DMA
    scratch = [
        pltpu.VMEM((top, local), routes.dtype),
        pltpu.VMEM((top, local), gates.dtype),
        pltpu.VMEM((experts, HALVES, half, features), bf),
        pltpu.VMEM((experts, HALVES, half, features), bf),
        pltpu.VMEM((experts, experts, local), bf),
        pltpu.VMEM((features, 2 * ff), bf),
        pltpu.VMEM((ff, features), bf),
        pltpu.VMEM((total, features), bf),
        pltpu.VMEM((total, features), bf),
        pltpu.VMEM((total, ff), bf),
        pltpu.VMEM((total, 2 * ff), bf),
        pltpu.VMEM((steps, cols, rows, features), bf),
        pltpu.VMEM((steps, cols, CORES, rows, features), bf),
        pltpu.VMEM((half, features), f32),
        pltpu.VMEM((depth, HALVES, cols, half, features), bf),
        pltpu.VMEM((depth + 1, HALVES, cols, half, features), bf),
        pltpu.VMEM((HALVES, half, features), f32),
        pltpu.VMEM((HALVES, half, features), bf),
        pltpu.VMEM((experts, 8, local), f32),
        pltpu.VMEM((experts, 8, local), f32),
        dma((5,)),
        dma((cols, depth, HALVES, 2)),
        dma((cols, depth)),
        dma((steps,)),
        dma((depth,)),
        dma((steps, cols)),
        dma((depth + 1, HALVES, cols)),
        dma((HALVES,)),
        dma((1,)),
        dma((8,)),
    ]
    vmem = pl.BlockSpec(memory_space=pltpu.VMEM)
    hbm = pl.BlockSpec(memory_space=pltpu.HBM)
    token_grads, gate_grads, grad_in, grad_down = pl.pallas_call(
        functools.partial(fused_kernel, cols, depth, group),
        out_shape=(
            jax.ShapeDtypeStruct((local, features), bf),
            jax.ShapeDtypeStruct((top, local), bf),
            jax.ShapeDtypeStruct(w_gate_up.shape, bf),
            jax.ShapeDtypeStruct(w_down.shape, bf),
        ),
        in_specs=[hbm] * 6,
        out_specs=(vmem, vmem, vmem, vmem),
        scratch_shapes=scratch,
        compiler_params=pltpu.CompilerParams(
            collective_id=0, has_side_effects=True, vmem_limit_bytes=44 * 2**20
        ),
    )(
        *(
            pltpu.with_memory_space_constraint(a, pltpu.HBM)
            for a in (tokens, grad_out, routes.T, gates.T, w_gate_up, w_down)
        )
    )
    token_grads, gate_grads, grad_in, grad_down = store(token_grads, gate_grads, grad_in, grad_down)
    return token_grads, gate_grads.T, grad_in, grad_down


def fits(tokens, routes, w_down):
    first_size = lax.axis_size("da")
    experts = first_size * lax.axis_size("db")
    local, features = tokens.shape
    group = experts // routes.shape[1]
    held = 2 * experts * local * features * 2
    return (
        lax.axis_size("replica") == 1
        and first_size % CORES == 0
        and first_size == 2 * CORES
        and 2 * 3 * lax.axis_size("db") <= 30
        and held <= 16 * 2**20
        and local == 128
        and experts <= local
        and max(map(max, relay_slots(lax.axis_size("db")))) == HALVES * lax.axis_size("db") + 1
        and (local // (HALVES * group)) % 16 == 0
        and w_down.shape[1] % 128 == 0
    )


def route(*arrays):
    if fits(arrays[0], arrays[2], arrays[5]):
        return fused(*arrays)
    return body(*arrays)


def solution(mesh):
    placed = (
        P(("groups", "replica", "da", "db"), None),
        P(("groups", "replica", "da", "db"), None),
        P(("groups", "replica", "da", "db"), None),
        P(("groups", "replica", "da", "db"), None),
        P(("da", "db"), "replica", None),
        P(("da", "db"), "replica", None),
    )
    return jax.shard_map(
        route,
        mesh=mesh,
        in_specs=placed,
        out_specs=(
            P(("groups", "replica", "da", "db"), None),
            P(("groups", "replica", "da", "db"), None),
            P(("groups", "da", "db"), "replica", None),
            P(("groups", "da", "db"), "replica", None),
        ),
        check_vma=False,
    )
```

```python
import functools

import jax
import jax.numpy as jnp
from jax import lax
from jax.experimental import pallas as pl
from jax.experimental.pallas import tpu as pltpu
from jax.sharding import PartitionSpec as P


CORES = 2
HALVES = 2
SPLIT = 2
MESH = pl.DeviceIdType.MESH


def silu_parts(projected):
    sigmoid = jax.nn.sigmoid(projected)
    return (projected * sigmoid, sigmoid * (1.0 + projected * (1.0 - sigmoid)))


def body(tokens, grad_out, routes, gates, w_gate_up, w_down):
    local_tokens, features = tokens.shape
    top_count = routes.shape[1]
    hidden_units = w_gate_up.shape[2] // 2
    first_size = lax.axis_size("da")
    second_size = lax.axis_size("db")
    experts = first_size * second_size
    per_round = experts // top_count
    rounds = local_tokens // per_round
    expert_ids = lax.broadcasted_iota(jnp.int32, (1, 1, 1, experts), 3)
    matches = routes.reshape(rounds, per_round, top_count, 1) == expert_ids
    gate_values = gates.reshape(rounds, per_round, top_count, 1).astype(jnp.float32)
    gate_table = jnp.sum(jnp.where(matches, gate_values, 0.0), axis=(1, 2)).astype(jnp.bfloat16)
    chosen = jnp.any(matches, axis=2).astype(jnp.bfloat16)
    input_send = jnp.einsum(
        "rge,rgd->red",
        chosen,
        tokens.reshape(rounds, per_round, features),
        preferred_element_type=jnp.float32,
    ).astype(jnp.bfloat16)
    upstream_send = jnp.einsum(
        "rge,rgd->red",
        chosen,
        grad_out.reshape(rounds, per_round, features),
        preferred_element_type=jnp.float32,
    ).astype(jnp.bfloat16)
    input_recv, upstream_recv, gate_recv = (
        lax.all_to_all(input_send, ("da", "db"), split_axis=1, concat_axis=1, tiled=True),
        lax.all_to_all(upstream_send, ("da", "db"), split_axis=1, concat_axis=1, tiled=True),
        lax.all_to_all(gate_table, ("da", "db"), split_axis=1, concat_axis=1, tiled=True),
    )
    input_rows = input_recv.reshape(-1, features)
    upstream_rows = upstream_recv.reshape(-1, features)
    gate_rows = gate_recv.reshape(-1, 1).astype(jnp.float32)
    w_in, w_out = (
        lax.all_gather(w_gate_up[0], "replica", axis=0, tiled=True),
        lax.all_gather(w_down[0], "replica", axis=0, tiled=True),
    )
    projected = jnp.dot(input_rows, w_in, preferred_element_type=jnp.float32)
    back_raw = jnp.einsum("rd,fd->rf", upstream_rows, w_out, preferred_element_type=jnp.float32)
    gate_part = projected[:, :hidden_units]
    up_part = projected[:, hidden_units:]
    activated, derivative = silu_parts(gate_part)
    hidden = (activated * up_part).astype(jnp.bfloat16)
    gate_scores = jnp.sum(hidden.astype(jnp.float32) * back_raw, axis=1).astype(jnp.bfloat16)
    back_hidden = gate_rows * back_raw
    grad_projected = jnp.concatenate(
        [back_hidden * up_part * derivative, back_hidden * activated], axis=1
    ).astype(jnp.bfloat16)
    scaled_upstream = (gate_rows * upstream_rows.astype(jnp.float32)).astype(jnp.bfloat16)
    input_grads = jnp.einsum("rf,df->rd", grad_projected, w_in, preferred_element_type=jnp.float32)
    input_grads = input_grads.astype(jnp.bfloat16).reshape(rounds, experts, features)
    score_back = gate_scores.reshape(rounds, experts)
    returned, score_ret = (
        lax.all_to_all(input_grads, ("da", "db"), split_axis=1, concat_axis=1, tiled=True),
        lax.all_to_all(score_back, ("da", "db"), split_axis=1, concat_axis=1, tiled=True),
    )
    score_ret = score_ret.reshape(rounds, 1, 1, experts).astype(jnp.float32)
    token_grads = (
        jnp.einsum("rge,red->rgd", chosen, returned, preferred_element_type=jnp.float32)
        .astype(jnp.bfloat16)
        .reshape(local_tokens, features)
    )
    gate_grads = (
        jnp.sum(jnp.where(matches, score_ret, 0.0), axis=3)
        .astype(jnp.bfloat16)
        .reshape(local_tokens, top_count)
    )
    columns = input_rows
    grad_in = lax.psum_scatter(
        jnp.einsum("rd,rf->df", columns, grad_projected, preferred_element_type=jnp.float32).astype(
            jnp.bfloat16
        ),
        "replica",
        scatter_dimension=0,
        tiled=True,
    )
    columns = hidden
    grad_down = lax.psum_scatter(
        jnp.einsum(
            "rf,rd->fd", columns, scaled_upstream, preferred_element_type=jnp.float32
        ).astype(jnp.bfloat16),
        "replica",
        scatter_dimension=0,
        tiled=True,
    )
    return (token_grads, gate_grads, grad_in[None], grad_down[None])


def visit(j, z, n):
    m = jnp.minimum(z, n - 1 - z)
    near = z + (1 - 2 * (j % 2)) * ((j + 1) // 2)
    far = jnp.where(z < n - 1 - z, j, n - 1 - j)
    return jnp.where(j <= 2 * m, near, far)


def dot(a, b, dims):
    return lax.dot_general(a, b, (dims, ((), ())), preferred_element_type=jnp.float32)


def position(d, z, n):
    away = abs(d - z)
    if away <= min(z, n - 1 - z):
        return 2 * away - (1 if d < z else 0)
    return d if z < n - 1 - z else n - 1 - d


def relay_slots(n):
    last = 2 * n - 1

    def ready(z, d, h):
        k = position(d, z, n)
        k = last - k if h else k
        feeds = [u for u in (z - 1, z + 1) if 0 <= u < n and abs(u - d) == abs(z - d) + 1]
        return max([k + 2] + [ready(u, d, h) + 1 for u in feeds])

    table = []
    for z in range(n):
        row = [0] * (2 * n)
        for d in range(n):
            k = position(d, z, n)
            row[k] = ready(z, d, 0)
            row[last - k] = ready(z, d, 1)
        table.append(row)
    return table


def lag_words(n):
    return [sum((at - k - 2) * 8 ** (2 * n - 1 - k) for k, at in enumerate(row)) for row in relay_slots(n)]


def fused_kernel(
    cols, depth, group,
    tok_hbm, up_hbm, routes_hbm, gates_hbm, win_hbm, wout_hbm,
    tg_ref, gg_ref, gin_ref, gdown_ref,
    routes_ref, gates_ref, tok, up, table, win, wout, win_t, wout_t, xs, su, hid, gp, igs, igb, acc, cs, cr, rk, rx, scs, scr,
    load_sem, recv_sem, chart_sem, near_sem, near_chart_sem, igr_sem, cr_sem, rx_sem, scr_sem, sent_sem,
    tail_sem, near_tail_sem, igr_tail_sem,
):
    da = lax.axis_index("da")
    z = lax.axis_index("db")
    x, c = da // CORES, da % CORES
    half, features = tok.shape[2], tok.shape[3]
    local = HALVES * half
    experts = table.shape[1]
    top = routes_ref.shape[0]
    rows = half // group
    ff = wout.shape[0]
    steps = HALVES * depth
    part = half // SPLIT
    few = rows // SPLIT

    def slot(xx, zz, cc):
        return (xx * CORES + cc) * depth + zz

    me = slot(x, z, c)
    loads = []
    for h in range(HALVES):
        span = pl.ds(h * half, half)
        loads.append(pltpu.make_async_copy(tok_hbm.at[span], tok.at[me, h], load_sem.at[0]))
        loads.append(pltpu.make_async_copy(up_hbm.at[span], up.at[me, h], load_sem.at[0]))
    loads += [
        pltpu.make_async_copy(win_hbm.at[0], win, load_sem.at[1]),
        pltpu.make_async_copy(wout_hbm.at[0], wout, load_sem.at[2]),
        pltpu.make_async_copy(routes_hbm, routes_ref, load_sem.at[3]),
        pltpu.make_async_copy(gates_hbm, gates_ref, load_sem.at[4]),
    ]
    def settle(view, sem):
        pltpu.make_async_copy(view, view, sem).wait()

    barrier = pltpu.get_barrier_semaphore()
    count = cols * CORES * depth

    def greet(xx, zz, cc):
        pl.semaphore_signal(
            barrier, inc=1, device_id={"da": xx * CORES + cc, "db": zz}, device_id_type=MESH
        )

    @pl.when(z > 0)
    def _():
        greet(x, z - 1, c)

    @pl.when(z < depth - 1)
    def _():
        greet(x, z + 1, c)

    greet(1 - x, z, c)
    greet(x, z, 1 - c)
    for k in (6, 7, 0, 1, 2, 3, 4, 5):
        loads[k].start()

    loads[6].wait()
    loads[7].wait()
    routes = routes_ref[...]
    gates = gates_ref[...].astype(jnp.float32)
    ids = lax.broadcasted_iota(jnp.int32, (experts, local), 0)
    chart = jnp.zeros((experts, local), jnp.float32)
    for k in range(top):
        chart = chart + jnp.where(routes[k : k + 1] == ids, gates[k : k + 1], 0.0)
    table[me] = chart.astype(jnp.bfloat16)

    settle(tok.at[pl.ds(0, CORES)], load_sem.at[0])
    pl.semaphore_wait(barrier, 2 + jnp.where(z > 0, 1, 0) + jnp.where(z < depth - 1, 1, 0))

    held = (tok, up)

    def send(src, dst, send_sem, recv, to_x, to_z, to_c):
        return pltpu.make_async_remote_copy(
            src_ref=src,
            dst_ref=dst,
            send_sem=send_sem,
            recv_sem=recv,
            device_id={"da": to_x * CORES + to_c, "db": to_z},
            device_id_type=MESH,
        )

    def start(copy):
        copy.start()

    def wait_recv(copy):
        copy.wait_recv()

    def both(xx, zz, h, a, way, act, to_x, to_z, to_c, near=None):
        s = slot(xx, zz, c)
        ref = held[a].at[s, h]
        landed = recv_sem.at[xx, zz, h, a] if near is None else near_sem.at[near]
        act(send(ref, ref, sent_sem.at[way], landed, to_x, to_z, to_c))
        if a == 0:

            @pl.when(h == 0)
            def _():
                ref = table.at[s]
                landed = chart_sem.at[xx, zz] if near is None else near_chart_sem.at[zz]
                act(send(ref, ref, sent_sem.at[3 + (way > 0)], landed, to_x, to_z, to_c))

    def step_of(i):
        j = jnp.minimum(i, steps - 1 - i)
        return visit(j, z, depth), jnp.where(i >= depth, 1, 0)

    def along_z(e, a):
        def one(reach, sign):
            last = 2 * reach + 1
            k = jnp.minimum(e, last - e)
            h = jnp.where(e > reach, 1, 0)
            zz = z + sign * k

            @pl.when((e <= last) & (k > 0))
            def _():
                both(x, zz, h, a, 0, wait_recv, x, z, 1 - c)

            ahead = z - sign

            @pl.when((e <= last) & (ahead >= 0) & (ahead < depth))
            def _():
                both(x, zz, h, a, 0, start, x, ahead, c)

        one(depth - 1 - z, 1)
        one(z, -1)

    def last_part(xx, u, a, way, to_x, to_c, near=None):
        ref = held[a].at[slot(xx, z, c), HALVES - 1, pl.ds(u * part, part)]
        landed = near
        if near is None:
            landed = recv_sem.at[xx, z, HALVES - 1, a] if u == 0 else tail_sem.at[a]
        return send(ref, ref, sent_sem.at[way], landed, to_x, z, to_c)

    def last_from_across(u):
        near = near_sem.at[steps - 1] if u == 0 else near_tail_sem.at[0]
        for a in range(2):
            last_part(1 - x, u, a, 1, 1 - x, c).wait_recv()
            last_part(1 - x, u, a, 2, x, 1 - c, near).start()

    def last_from_partner(u):
        if u == 0:
            settle(xs.at[pl.ds(0, (cols + 1) * half)], near_sem.at[steps - 1])
        else:
            settle(tok.at[0, 0], near_tail_sem.at[0])

    def across(i, a):
        zz, h = step_of(i)

        @pl.when(i < steps - 1)
        def _():
            both(x, zz, h, a, 1, start, 1 - x, z, c)

        @pl.when(i == steps - 1)
        def _():
            for b in range(2):
                last_part(x, a, b, 1, 1 - x, c).start()

        both(x, zz, h, a, 2, start, x, z, 1 - c, near=i)

    def from_across(i, a):
        zz, h = step_of(i)
        both(1 - x, zz, h, a, 1, wait_recv, 1 - x, z, c)
        both(1 - x, zz, h, a, 2, start, x, z, 1 - c, near=i)

    def from_partner(i):
        zz, h = step_of(i)
        settle(tok.at[pl.ds(0, cols)], near_sem.at[i])

        @pl.when(h == 0)
        def _():
            settle(table.at[pl.ds(0, cols)], near_chart_sem.at[zz])

    def pick(s, e, h):
        chart_s = table[s].astype(jnp.float32)
        which = lax.broadcasted_iota(jnp.int32, chart_s.shape, 0) == e
        row = jnp.sum(jnp.where(which, chart_s, 0.0), axis=0, keepdims=True)
        row = jnp.where(h == 0, row[:, :half], row[:, half:])
        off = lax.broadcasted_iota(jnp.int32, (rows, half), 1) - group * lax.broadcasted_iota(
            jnp.int32, (rows, half), 0
        )
        hit = (off >= 0) & (off < group) & (row > 0.0)
        return jnp.where(hit, 1.0, 0.0), row

    def send_ig(q, k):
        return send(igs.at[k, q], igb.at[k, q, c], sent_sem.at[5], igr_sem.at[k, q], x, z, 1 - c)

    def send_last_ig(q, u):
        at = pl.ds(u * few, few)
        landed = igr_sem.at[steps - 1, q] if u == 0 else igr_tail_sem.at[q]
        src, dst = igs.at[steps - 1, q, at], igb.at[steps - 1, q, c, at]
        return send(src, dst, sent_sem.at[5], landed, x, z, 1 - c)

    def send_score(s):
        return pltpu.make_async_remote_copy(
            src_ref=scs.at[s],
            dst_ref=scr.at[me],
            send_sem=sent_sem.at[7],
            recv_sem=scr_sem.at[0],
            device_id={"da": s // depth, "db": s % depth},
            device_id_type=MESH,
        )

    blocks = [(q, r) for q in range(cols) for r in range(CORES)]
    batch = len(blocks) * rows

    def compute(k, u=None):
        zz, h = step_of(k) if u is None else (z, HALVES - 1)
        count_rows = rows if u is None else few
        size = len(blocks) * count_rows
        base = pl.multiple_of(k * batch, batch) if u is None else k * batch + u * size
        picks = []
        gate_cols = []
        for n, (q, r) in enumerate(blocks):
            s = slot((x + q) % cols, zz, (c + r) % CORES)
            chosen, row = pick(s, me, h)
            tokens, upstreams = tok.at[s, h], up.at[s, h]
            if u is not None:
                span = slice(u * part, (u + 1) * part)
                chosen, row = chosen[u * few : (u + 1) * few, span], row[:, span]
                tokens = tokens.at[pl.ds(u * part, part)]
                upstreams = upstreams.at[pl.ds(u * part, part)]
            picks.append((s, chosen))
            gate_cols.append(jnp.sum(chosen * row, axis=1, keepdims=True))
            hot = chosen.astype(jnp.bfloat16)
            where = base + n * count_rows
            where = pl.ds(pl.multiple_of(where, count_rows) if u is None else where, count_rows)
            xs[where, :] = dot(hot, tokens[...], ((1,), (0,))).astype(jnp.bfloat16)
            su[where, :] = dot(hot, upstreams[...], ((1,), (0,))).astype(jnp.bfloat16)
        here = pl.ds(base, size)
        gate = jnp.concatenate(gate_cols, axis=0)
        upstream = su[here, :]
        projected = dot(xs[here, :], win[...], ((1,), (0,)))
        back_raw = dot(upstream, wout_t[...], ((1,), (0,)))
        su[here, :] = (gate * upstream.astype(jnp.float32)).astype(jnp.bfloat16)
        gate_part, up_part = projected[:, :ff], projected[:, ff:]
        activated, derivative = silu_parts(gate_part)
        hidden = (activated * up_part).astype(jnp.bfloat16)
        hid[here, :] = hidden
        scores = jnp.sum(hidden.astype(jnp.float32) * back_raw, axis=1, keepdims=True)
        scores = scores.astype(jnp.bfloat16).astype(jnp.float32)
        back_hidden = gate * back_raw
        gp[here, :ff] = (back_hidden * up_part * derivative).astype(jnp.bfloat16)
        gp[here, ff:] = (back_hidden * activated).astype(jnp.bfloat16)
        grads = dot(gp[here, :], win_t[...], ((1,), (0,))).astype(jnp.bfloat16)
        for n, (q, r) in enumerate(blocks):
            piece = grads[n * count_rows : (n + 1) * count_rows]
            if u is None:
                if r == 0:
                    igb[k, q, c] = piece
                else:
                    igs[k, q] = piece
                    send_ig(q, k).start()
            else:
                at = pl.ds(u * few, few)
                if r == 0:
                    igb[k, q, c, at] = piece
                else:
                    igs[k, q, at] = piece
                    send_last_ig(q, u).start()
        for n, (q, r) in enumerate(blocks):
            s, chosen = picks[n]
            line = jnp.sum(chosen * scores[n * count_rows : (n + 1) * count_rows], axis=0, keepdims=True)
            if u is not None:
                ahead = (HALVES - 1) * half + u * part
                parts = [jnp.zeros((1, ahead), jnp.float32), line]
                if u < SPLIT - 1:
                    parts.append(jnp.zeros((1, local - ahead - part), jnp.float32))
                scs[s] = scs[s] + jnp.broadcast_to(jnp.concatenate(parts, axis=1), scs.shape[1:])
                if u == SPLIT - 1:
                    if q == 0 and r == 0:
                        scr[me] = scs[me]
                    else:
                        send_score(s).start()
                continue
            rest = jnp.zeros_like(line)
            first = jnp.concatenate([line, rest], axis=1)
            second = jnp.concatenate([rest, line], axis=1)

            @pl.when(h == 0)
            def _():
                scs[s] = jnp.broadcast_to(first, scs.shape[1:])

            @pl.when(h == 1)
            def _():
                scs[s] = scs[s] + jnp.broadcast_to(second, scs.shape[1:])
                send_score(s).start()

    def send_sum(zz, h, q, u, side, to_z):
        place = jnp.where((zz == to_z) & (side == 1), depth, zz)
        at = pl.ds(u * part, part) if q else pl.ds(0, half)
        landed = cr_sem.at[place, h, q + u]
        return send(cs.at[zz, h, q, at], cr.at[place, h, q, at], sent_sem.at[6], landed, x, to_z, c)

    def send_across(h, u=None):
        at = pl.ds(0, half) if u is None else pl.ds(u * part, part)
        landed = rx_sem.at[0 if u is None else 1 + u]
        return send(cs.at[z, h, 1, at], rx.at[h, at], sent_sem.at[6], landed, 1 - x, z, c)

    def gather(zz, h, q, u, total):
        at = pl.ds(u * part, part) if q else pl.ds(0, half)
        to = pl.ds(0, part if q else half)
        acc[to, :] = total
        for side, ok in ((0, (zz <= z) & (z < depth - 1)), (1, (zz >= z) & (z > 0))):

            @pl.when(ok)
            def _():
                send_sum(zz, h, q, u, side, z).wait_recv()
                place = jnp.where((zz == z) & (side == 1), depth, zz)
                acc[to, :] += cr[place, h, q, at].astype(jnp.float32)

        return at, to

    def hot_of(s, h):
        return [pick(s, slot(x, z, m), h)[0] for m in range(CORES)]

    def pass_on(k, q):
        zz, h = step_of(k)
        hot = jnp.concatenate(hot_of(slot((x + q) % cols, zz, c), h), axis=0).astype(jnp.bfloat16)
        send_ig(q, k).wait_recv()
        pair = igb[k, q].reshape(CORES * rows, features)
        for u in range(SPLIT if q else 1):
            mine = hot[:, u * part : (u + 1) * part] if q else hot
            at, to = gather(zz, h, q, u, dot(mine, pair, ((0,), (0,))))
            cs[zz, h, q, at] = acc[to, :].astype(jnp.bfloat16)

            @pl.when(zz < z)
            def _():
                send_sum(zz, h, q, u, 0, z - 1).start()

            @pl.when(zz > z)
            def _():
                send_sum(zz, h, q, u, 1, z + 1).start()

    def home_sum(k, h, q):
        hot = jnp.concatenate(hot_of(slot((x + q) % cols, z, c), h), axis=0).astype(jnp.bfloat16)
        pair = igb[k, q].reshape(CORES * rows, features)
        return hot, pair

    def home_first():
        send_ig(1, 0).wait_recv()
        hot, pair = home_sum(0, 0, 1)
        for u in range(SPLIT):
            span = slice(u * part, (u + 1) * part)
            at, to = gather(z, 0, 1, u, dot(hot[:, span], pair, ((0,), (0,))))
            cs[z, 0, 1, at] = acc[to, :].astype(jnp.bfloat16)
        send_across(0).start()

    def home_last(u):
        k = steps - 1
        s = slot(1 - x, z, c)
        here, span = slice(u * few, (u + 1) * few), slice(u * part, (u + 1) * part)
        hot = jnp.concatenate([one[here, span] for one in hot_of(s, HALVES - 1)], axis=0)
        send_last_ig(1, u).wait_recv()
        pair = igb[k, 1, :, pl.ds(u * few, few)].reshape(CORES * few, features)
        at, to = gather(z, HALVES - 1, 1, u, dot(hot.astype(jnp.bfloat16), pair, ((0,), (0,))))
        cs[z, HALVES - 1, 1, at] = acc[to, :].astype(jnp.bfloat16)
        send_across(HALVES - 1, u).start()

    def home_own():
        for k, h in ((0, 0), (steps - 1, HALVES - 1)):
            if h == 0:
                send_ig(0, 0).wait_recv()
            else:
                for u in range(SPLIT):
                    send_last_ig(0, u).wait_recv()
            hot, pair = home_sum(k, h, 0)
            gather(z, h, 0, 0, dot(hot, pair, ((0,), (0,))))
            rk[h] = acc[...]

    words = lag_words(depth)
    word = jnp.int32(words[0])
    for k in range(1, depth):
        word = jnp.where(z == k, words[k], word)

    edge = (z == 0) | (z == depth - 1)
    inner = jnp.logical_not(edge)

    def pass_all(i, q):
        def one(j, left):
            k = steps - 1 - j
            due = (k + 2 + left % 8 == i) & (j > 0)

            @pl.when(due)
            def _():
                pass_on(k, q)

            return left // 8

        lax.fori_loop(0, steps - 1, one, word)

    along_z(0, 0)
    across(0, 0)

    def step(i, carry):
        @pl.when(i < steps)
        def _():
            along_z(i, 1)
            across(i, 1)

        @pl.when(i == 0)
        def _():
            loads[4].wait()
            loads[5].wait()
            win_t[...] = win[...].T
            wout_t[...] = wout[...].T

        @pl.when(inner & (i >= 2))
        def _():
            pass_all(i, 1)

        @pl.when(i >= 1)
        def _():
            from_across(i - 1, 1)

        @pl.when(inner & (i >= 2))
        def _():
            pass_all(i, 0)

        @pl.when(i >= 1)
        def _():
            from_partner(i - 1)
            compute(i - 1)

        @pl.when(i + 1 < steps)
        def _():
            along_z(i + 1, 0)
            across(i + 1, 0)

        @pl.when(i < steps - 1)
        def _():
            from_across(i, 0)

        @pl.when(i == steps - 1)
        def _():
            last_from_across(0)

        @pl.when(edge & (i >= 1))
        def _():
            pass_all(i + 1, 1)
            pass_all(i + 1, 0)

        return carry

    lax.fori_loop(0, steps, step, 0)

    @pl.when(inner)
    def _():
        pass_all(steps, 1)

    last_from_partner(0)
    compute(steps - 1, 0)
    last_from_across(1)
    home_first()

    @pl.when(inner)
    def _():
        pass_all(steps, 0)

    last_from_partner(1)
    compute(steps - 1, 1)
    home_last(0)

    wide = min(features, 256)

    def gin(t, carry):
        at = pl.ds(pl.multiple_of(t * wide, wide), wide)
        gin_ref[0, at, :] = dot(xs[:, at], gp[...], ((0,), (0,))).astype(jnp.bfloat16)
        return carry

    early = jnp.where(edge, 1, 1)
    lax.fori_loop(0, early, gin, 0)
    home_last(1)
    lax.fori_loop(early, features // wide, gin, 0)

    thin = 128

    @pl.loop(0, ff // thin)
    def _(t):
        at = pl.ds(pl.multiple_of(t * thin, thin), thin)
        gdown_ref[0, at, :] = dot(hid[:, at], su[...], ((0,), (0,))).astype(jnp.bfloat16)

    home_own()
    settle(scr.at[pl.ds(0, count - 1)], scr_sem.at[0])
    scores = scr[:, 0, :]
    place = lax.broadcasted_iota(jnp.int32, (top, local), 0)
    gate_grads = jnp.zeros((top, local), jnp.float32)
    for k in range(top):
        value = jnp.sum(jnp.where(routes[k : k + 1] == ids, scores, 0.0), axis=0, keepdims=True)
        gate_grads = jnp.where(place == k, value, gate_grads)
    gg_ref[...] = gate_grads.astype(jnp.bfloat16)

    for h in range(HALVES):
        for u in (None,) if h == 0 else range(SPLIT):
            send_across(h, u).wait_recv()
        tg_ref[pl.ds(h * half, half), :] = (rk[h] + rx[h].astype(jnp.float32)).astype(jnp.bfloat16)

    for at in range(depth):
        sent = (depth - at if at > 0 else 0) + (at + 1 if at < depth - 1 else 0)

        @pl.when(z == at)
        def _():
            settle(tok.at[pl.ds(0, 2 * sent)], sent_sem.at[0])
            settle(table.at[pl.ds(0, sent)], sent_sem.at[3])

    settle(tok.at[pl.ds(0, 2 * depth)], sent_sem.at[1])
    settle(tok, sent_sem.at[2])
    settle(table.at[pl.ds(0, 3 * depth)], sent_sem.at[4])
    settle(igs, sent_sem.at[5])
    settle(tok.at[pl.ds(0, depth * cols - 1)], sent_sem.at[6])
    settle(scs.at[pl.ds(0, count - 1)], sent_sem.at[7])


def store_kernel(*refs):
    count = len(refs) // 2
    sems = refs[-1]
    copies = [
        pltpu.make_async_copy(refs[k], refs[count + k], sems.at[k]) for k in range(count)
    ]
    for one in copies:
        one.start()
    for one in copies:
        one.wait()


def store(*arrays):
    anywhere = pl.BlockSpec(memory_space=pl.ANY)
    return pl.pallas_call(
        store_kernel,
        out_shape=tuple(jax.ShapeDtypeStruct(a.shape, a.dtype) for a in arrays),
        in_specs=[pl.BlockSpec(memory_space=pltpu.VMEM)] * len(arrays),
        out_specs=(pl.BlockSpec(memory_space=pltpu.HBM),) * len(arrays),
        scratch_shapes=[pltpu.SemaphoreType.DMA((len(arrays),))],
        compiler_params=pltpu.CompilerParams(vmem_limit_bytes=8 * 2**20),
    )(*arrays)


def fused(tokens, grad_out, routes, gates, w_gate_up, w_down):
    first_size, depth = lax.axis_size("da"), lax.axis_size("db")
    cols = first_size // CORES
    experts = first_size * depth
    local, features = tokens.shape
    top = routes.shape[1]
    group = experts // top
    ff = w_down.shape[1]
    bf, f32 = jnp.bfloat16, jnp.float32
    half = local // HALVES
    rows = half // group
    steps = HALVES * depth
    total = rows * experts * HALVES
    dma = pltpu.SemaphoreType.DMA
    scratch = [
        pltpu.VMEM((top, local), routes.dtype),
        pltpu.VMEM((top, local), gates.dtype),
        pltpu.VMEM((experts, HALVES, half, features), bf),
        pltpu.VMEM((experts, HALVES, half, features), bf),
        pltpu.VMEM((experts, experts, local), bf),
        pltpu.VMEM((features, 2 * ff), bf),
        pltpu.VMEM((ff, features), bf),
        pltpu.VMEM((2 * ff, features), bf),
        pltpu.VMEM((features, ff), bf),
        pltpu.VMEM((total, features), bf),
        pltpu.VMEM((total, features), bf),
        pltpu.VMEM((total, ff), bf),
        pltpu.VMEM((total, 2 * ff), bf),
        pltpu.VMEM((steps, cols, rows, features), bf),
        pltpu.VMEM((steps, cols, CORES, rows, features), bf),
        pltpu.VMEM((half, features), f32),
        pltpu.VMEM((depth, HALVES, cols, half, features), bf),
        pltpu.VMEM((depth + 1, HALVES, cols, half, features), bf),
        pltpu.VMEM((HALVES, half, features), f32),
        pltpu.VMEM((HALVES, half, features), bf),
        pltpu.VMEM((experts, 8, local), f32),
        pltpu.VMEM((experts, 8, local), f32),
        dma((5,)),
        dma((cols, depth, HALVES, 2)),
        dma((cols, depth)),
        dma((steps,)),
        dma((depth,)),
        dma((steps, cols)),
        dma((depth + 1, HALVES, 1 + SPLIT)),
        dma((1 + SPLIT,)),
        dma((1,)),
        dma((8,)),
        dma((2,)),
        dma((1,)),
        dma((cols,)),
    ]
    vmem = pl.BlockSpec(memory_space=pltpu.VMEM)
    hbm = pl.BlockSpec(memory_space=pltpu.HBM)
    token_grads, gate_grads, grad_in, grad_down = pl.pallas_call(
        functools.partial(fused_kernel, cols, depth, group),
        out_shape=(
            jax.ShapeDtypeStruct((local, features), bf),
            jax.ShapeDtypeStruct((top, local), bf),
            jax.ShapeDtypeStruct(w_gate_up.shape, bf),
            jax.ShapeDtypeStruct(w_down.shape, bf),
        ),
        in_specs=[hbm] * 6,
        out_specs=(vmem, vmem, vmem, vmem),
        scratch_shapes=scratch,
        compiler_params=pltpu.CompilerParams(
            collective_id=0, has_side_effects=True, vmem_limit_bytes=44 * 2**20
        ),
    )(
        *(
            pltpu.with_memory_space_constraint(a, pltpu.HBM)
            for a in (tokens, grad_out, routes.T, gates.T, w_gate_up, w_down)
        )
    )
    token_grads, gate_grads, grad_in, grad_down = store(token_grads, gate_grads, grad_in, grad_down)
    return token_grads, gate_grads.T, grad_in, grad_down


def fits(tokens, routes, w_down):
    first_size = lax.axis_size("da")
    experts = first_size * lax.axis_size("db")
    local, features = tokens.shape
    group = experts // routes.shape[1]
    held = 2 * experts * local * features * 2
    return (
        lax.axis_size("replica") == 1
        and first_size % CORES == 0
        and first_size == 2 * CORES
        and 2 * 3 * lax.axis_size("db") <= 30
        and held <= 16 * 2**20
        and local == 128
        and experts <= local
        and max(map(max, relay_slots(lax.axis_size("db")))) == HALVES * lax.axis_size("db") + 1
        and (local // (HALVES * SPLIT * group)) % 16 == 0
        and w_down.shape[1] % 128 == 0
    )


def route(*arrays):
    if fits(arrays[0], arrays[2], arrays[5]):
        return fused(*arrays)
    return body(*arrays)


def solution(mesh):
    placed = (
        P(("groups", "replica", "da", "db"), None),
        P(("groups", "replica", "da", "db"), None),
        P(("groups", "replica", "da", "db"), None),
        P(("groups", "replica", "da", "db"), None),
        P(("da", "db"), "replica", None),
        P(("da", "db"), "replica", None),
    )
    return jax.shard_map(
        route,
        mesh=mesh,
        in_specs=placed,
        out_specs=(
            P(("groups", "replica", "da", "db"), None),
            P(("groups", "replica", "da", "db"), None),
            P(("groups", "da", "db"), "replica", None),
            P(("groups", "da", "db"), "replica", None),
        ),
        check_vma=False,
    )
```

```python
import functools

import jax
import jax.numpy as jnp
from jax import lax
from jax.experimental import pallas as pl
from jax.experimental.pallas import tpu as pltpu
from jax.sharding import PartitionSpec as P


CORES = 2
HALVES = 2
SPLIT = 2
MESH = pl.DeviceIdType.MESH


def silu_parts(projected):
    sigmoid = jax.nn.sigmoid(projected)
    return (projected * sigmoid, sigmoid * (1.0 + projected * (1.0 - sigmoid)))


def body(tokens, grad_out, routes, gates, w_gate_up, w_down):
    local_tokens, features = tokens.shape
    top_count = routes.shape[1]
    hidden_units = w_gate_up.shape[2] // 2
    first_size = lax.axis_size("da")
    second_size = lax.axis_size("db")
    experts = first_size * second_size
    per_round = experts // top_count
    rounds = local_tokens // per_round
    expert_ids = lax.broadcasted_iota(jnp.int32, (1, 1, 1, experts), 3)
    matches = routes.reshape(rounds, per_round, top_count, 1) == expert_ids
    gate_values = gates.reshape(rounds, per_round, top_count, 1).astype(jnp.float32)
    gate_table = jnp.sum(jnp.where(matches, gate_values, 0.0), axis=(1, 2)).astype(jnp.bfloat16)
    chosen = jnp.any(matches, axis=2).astype(jnp.bfloat16)
    input_send = jnp.einsum(
        "rge,rgd->red",
        chosen,
        tokens.reshape(rounds, per_round, features),
        preferred_element_type=jnp.float32,
    ).astype(jnp.bfloat16)
    upstream_send = jnp.einsum(
        "rge,rgd->red",
        chosen,
        grad_out.reshape(rounds, per_round, features),
        preferred_element_type=jnp.float32,
    ).astype(jnp.bfloat16)
    input_recv, upstream_recv, gate_recv = (
        lax.all_to_all(input_send, ("da", "db"), split_axis=1, concat_axis=1, tiled=True),
        lax.all_to_all(upstream_send, ("da", "db"), split_axis=1, concat_axis=1, tiled=True),
        lax.all_to_all(gate_table, ("da", "db"), split_axis=1, concat_axis=1, tiled=True),
    )
    input_rows = input_recv.reshape(-1, features)
    upstream_rows = upstream_recv.reshape(-1, features)
    gate_rows = gate_recv.reshape(-1, 1).astype(jnp.float32)
    w_in, w_out = (
        lax.all_gather(w_gate_up[0], "replica", axis=0, tiled=True),
        lax.all_gather(w_down[0], "replica", axis=0, tiled=True),
    )
    projected = jnp.dot(input_rows, w_in, preferred_element_type=jnp.float32)
    back_raw = jnp.einsum("rd,fd->rf", upstream_rows, w_out, preferred_element_type=jnp.float32)
    gate_part = projected[:, :hidden_units]
    up_part = projected[:, hidden_units:]
    activated, derivative = silu_parts(gate_part)
    hidden = (activated * up_part).astype(jnp.bfloat16)
    gate_scores = jnp.sum(hidden.astype(jnp.float32) * back_raw, axis=1).astype(jnp.bfloat16)
    back_hidden = gate_rows * back_raw
    grad_projected = jnp.concatenate(
        [back_hidden * up_part * derivative, back_hidden * activated], axis=1
    ).astype(jnp.bfloat16)
    scaled_upstream = (gate_rows * upstream_rows.astype(jnp.float32)).astype(jnp.bfloat16)
    input_grads = jnp.einsum("rf,df->rd", grad_projected, w_in, preferred_element_type=jnp.float32)
    input_grads = input_grads.astype(jnp.bfloat16).reshape(rounds, experts, features)
    score_back = gate_scores.reshape(rounds, experts)
    returned, score_ret = (
        lax.all_to_all(input_grads, ("da", "db"), split_axis=1, concat_axis=1, tiled=True),
        lax.all_to_all(score_back, ("da", "db"), split_axis=1, concat_axis=1, tiled=True),
    )
    score_ret = score_ret.reshape(rounds, 1, 1, experts).astype(jnp.float32)
    token_grads = (
        jnp.einsum("rge,red->rgd", chosen, returned, preferred_element_type=jnp.float32)
        .astype(jnp.bfloat16)
        .reshape(local_tokens, features)
    )
    gate_grads = (
        jnp.sum(jnp.where(matches, score_ret, 0.0), axis=3)
        .astype(jnp.bfloat16)
        .reshape(local_tokens, top_count)
    )
    columns = input_rows
    grad_in = lax.psum_scatter(
        jnp.einsum("rd,rf->df", columns, grad_projected, preferred_element_type=jnp.float32).astype(
            jnp.bfloat16
        ),
        "replica",
        scatter_dimension=0,
        tiled=True,
    )
    columns = hidden
    grad_down = lax.psum_scatter(
        jnp.einsum(
            "rf,rd->fd", columns, scaled_upstream, preferred_element_type=jnp.float32
        ).astype(jnp.bfloat16),
        "replica",
        scatter_dimension=0,
        tiled=True,
    )
    return (token_grads, gate_grads, grad_in[None], grad_down[None])


def visit(j, z, n):
    m = jnp.minimum(z, n - 1 - z)
    near = z + (1 - 2 * (j % 2)) * ((j + 1) // 2)
    far = jnp.where(z < n - 1 - z, j, n - 1 - j)
    return jnp.where(j <= 2 * m, near, far)


def dot(a, b, dims):
    return lax.dot_general(a, b, (dims, ((), ())), preferred_element_type=jnp.float32)


def position(d, z, n):
    away = abs(d - z)
    if away <= min(z, n - 1 - z):
        return 2 * away - (1 if d < z else 0)
    return d if z < n - 1 - z else n - 1 - d


def relay_slots(n):
    last = 2 * n - 1

    def ready(z, d, h):
        k = position(d, z, n)
        k = last - k if h else k
        feeds = [u for u in (z - 1, z + 1) if 0 <= u < n and abs(u - d) == abs(z - d) + 1]
        return max([k + 2] + [ready(u, d, h) + 1 for u in feeds])

    table = []
    for z in range(n):
        row = [0] * (2 * n)
        for d in range(n):
            k = position(d, z, n)
            row[k] = ready(z, d, 0)
            row[last - k] = ready(z, d, 1)
        table.append(row)
    return table


def lag_words(n):
    return [sum((at - k - 2) * 8 ** (2 * n - 1 - k) for k, at in enumerate(row)) for row in relay_slots(n)]


def fused_kernel(
    cols, depth, group,
    tok_hbm, up_hbm, routes_hbm, gates_hbm, win_hbm, wout_hbm,
    tg_ref, gg_ref, gin_ref, gdown_ref,
    routes_ref, gates_ref, tok, up, table, win, wout, win_t, wout_t, xs, su, hid, gp, igs, igb, acc, cs, cr, rk, rx, scs, scr, bulk,
    load_sem, recv_sem, near_sem, igr_sem, cr_sem, rx_sem, scr_sem, sent_sem,
    tail_sem, near_tail_sem, igr_tail_sem,
):
    da = lax.axis_index("da")
    z = lax.axis_index("db")
    x, c = da // CORES, da % CORES
    half, features = tok.shape[2], tok.shape[3]
    local = HALVES * half
    experts = table.shape[1]
    top = routes_ref.shape[0]
    rows = half // group
    ff = wout.shape[0]
    steps = HALVES * depth
    part = half // SPLIT
    few = rows // SPLIT

    def slot(xx, zz, cc):
        return (xx * CORES + cc) * depth + zz

    me = slot(x, z, c)
    loads = []
    for h in range(HALVES):
        span = pl.ds(h * half, half)
        loads.append(pltpu.make_async_copy(tok_hbm.at[span], tok.at[me, h], load_sem.at[0]))
        loads.append(pltpu.make_async_copy(up_hbm.at[span], up.at[me, h], load_sem.at[0]))
    loads += [
        pltpu.make_async_copy(win_hbm.at[0], win, load_sem.at[1]),
        pltpu.make_async_copy(wout_hbm.at[0], wout, load_sem.at[2]),
        pltpu.make_async_copy(routes_hbm, routes_ref, load_sem.at[3]),
        pltpu.make_async_copy(gates_hbm, gates_ref, load_sem.at[4]),
    ]
    def settle(view, sem):
        pltpu.make_async_copy(view, view, sem).wait()

    barrier = pltpu.get_barrier_semaphore()
    count = cols * CORES * depth

    def greet(xx, zz, cc):
        pl.semaphore_signal(
            barrier, inc=1, device_id={"da": xx * CORES + cc, "db": zz}, device_id_type=MESH
        )

    @pl.when(z > 0)
    def _():
        greet(x, z - 1, c)

    @pl.when(z < depth - 1)
    def _():
        greet(x, z + 1, c)

    greet(1 - x, z, c)
    greet(x, z, 1 - c)
    for k in (6, 7, 0, 1, 2, 3, 4, 5):
        loads[k].start()

    loads[6].wait()
    loads[7].wait()
    routes = routes_ref[...]
    gates = gates_ref[...].astype(jnp.float32)
    ids = lax.broadcasted_iota(jnp.int32, (experts, local), 0)
    chart = jnp.zeros((experts, local), jnp.float32)
    for k in range(top):
        chart = chart + jnp.where(routes[k : k + 1] == ids, gates[k : k + 1], 0.0)
    table[me] = chart.astype(jnp.bfloat16)

    settle(tok.at[pl.ds(0, CORES)], load_sem.at[0])
    pl.semaphore_wait(barrier, 2 + jnp.where(z > 0, 1, 0) + jnp.where(z < depth - 1, 1, 0))

    held = (tok, up)

    def send(src, dst, send_sem, recv, to_x, to_z, to_c):
        return pltpu.make_async_remote_copy(
            src_ref=src,
            dst_ref=dst,
            send_sem=send_sem,
            recv_sem=recv,
            device_id={"da": to_x * CORES + to_c, "db": to_z},
            device_id_type=MESH,
        )

    def start(copy):
        copy.start()

    def wait_recv(copy):
        copy.wait_recv()

    def both(xx, zz, h, a, way, act, to_x, to_z, to_c, near=None):
        s = slot(xx, zz, c)
        ref = held[a].at[s, h]
        landed = recv_sem.at[xx, zz, h, a] if near is None else near_sem.at[near]
        copy = send(ref, ref, sent_sem.at[way], landed, to_x, to_z, to_c)
        if a != 0:
            act(copy)
            return

        @pl.when(h != 0)
        def _():
            act(copy)

        @pl.when(h == 0)
        def _():
            if act is start:
                copy.start()
                page = table.at[s]
                send(page, page, sent_sem.at[3 + (way > 0)], landed, to_x, to_z, to_c).start()
            else:
                settle(bulk.at[pl.ds(0, half * features // 128 + experts)], landed)

    def step_of(i):
        j = jnp.minimum(i, steps - 1 - i)
        return visit(j, z, depth), jnp.where(i >= depth, 1, 0)

    def along_z(e, a):
        def one(reach, sign):
            last = 2 * reach + 1
            k = jnp.minimum(e, last - e)
            h = jnp.where(e > reach, 1, 0)
            zz = z + sign * k

            @pl.when((e <= last) & (k > 0))
            def _():
                both(x, zz, h, a, 0, wait_recv, x, z, 1 - c)

            ahead = z - sign

            @pl.when((e <= last) & (ahead >= 0) & (ahead < depth))
            def _():
                both(x, zz, h, a, 0, start, x, ahead, c)

        one(depth - 1 - z, 1)
        one(z, -1)

    def last_part(xx, u, a, way, to_x, to_c, near=None):
        ref = held[a].at[slot(xx, z, c), HALVES - 1, pl.ds(u * part, part)]
        landed = near
        if near is None:
            landed = recv_sem.at[xx, z, HALVES - 1, a] if u == 0 else tail_sem.at[a]
        return send(ref, ref, sent_sem.at[way], landed, to_x, z, to_c)

    def last_from_across(u):
        near = near_sem.at[steps - 1] if u == 0 else near_tail_sem.at[0]
        for a in range(2):
            last_part(1 - x, u, a, 1, 1 - x, c).wait_recv()
            last_part(1 - x, u, a, 2, x, 1 - c, near).start()

    def last_from_partner(u):
        if u == 0:
            settle(xs.at[pl.ds(0, (cols + 1) * half)], near_sem.at[steps - 1])
        else:
            settle(tok.at[0, 0], near_tail_sem.at[0])

    def across(i, a):
        zz, h = step_of(i)

        @pl.when(i < steps - 1)
        def _():
            both(x, zz, h, a, 1, start, 1 - x, z, c)

        @pl.when(i == steps - 1)
        def _():
            for b in range(2):
                last_part(x, a, b, 1, 1 - x, c).start()

        both(x, zz, h, a, 2, start, x, z, 1 - c, near=i)

    def from_across(i, a):
        zz, h = step_of(i)
        both(1 - x, zz, h, a, 1, wait_recv, 1 - x, z, c)
        both(1 - x, zz, h, a, 2, start, x, z, 1 - c, near=i)

    def from_partner(i):
        zz, h = step_of(i)

        @pl.when(h == 0)
        def _():
            settle(bulk, near_sem.at[i])

        @pl.when(h != 0)
        def _():
            settle(tok.at[pl.ds(0, cols)], near_sem.at[i])

    def pick(s, e, h):
        chart_s = table[s].astype(jnp.float32)
        which = lax.broadcasted_iota(jnp.int32, chart_s.shape, 0) == e
        row = jnp.sum(jnp.where(which, chart_s, 0.0), axis=0, keepdims=True)
        row = jnp.where(h == 0, row[:, :half], row[:, half:])
        off = lax.broadcasted_iota(jnp.int32, (rows, half), 1) - group * lax.broadcasted_iota(
            jnp.int32, (rows, half), 0
        )
        hit = (off >= 0) & (off < group) & (row > 0.0)
        return jnp.where(hit, 1.0, 0.0), row

    def send_ig(q, k):
        return send(igs.at[k, q], igb.at[k, q, c], sent_sem.at[5], igr_sem.at[k], x, z, 1 - c)

    def send_last_ig(q, u):
        at = pl.ds(u * few, few)
        landed = igr_sem.at[steps - 1] if u == 0 else igr_tail_sem.at[0]
        src, dst = igs.at[steps - 1, q, at], igb.at[steps - 1, q, c, at]
        return send(src, dst, sent_sem.at[5], landed, x, z, 1 - c)

    def send_score(s):
        return pltpu.make_async_remote_copy(
            src_ref=scs.at[s],
            dst_ref=scr.at[me],
            send_sem=sent_sem.at[7],
            recv_sem=scr_sem.at[0],
            device_id={"da": s // depth, "db": s % depth},
            device_id_type=MESH,
        )

    blocks = [(q, r) for q in range(cols) for r in range(CORES)]
    batch = len(blocks) * rows

    def compute(k, u=None):
        zz, h = step_of(k) if u is None else (z, HALVES - 1)
        count_rows = rows if u is None else few
        size = len(blocks) * count_rows
        base = pl.multiple_of(k * batch, batch) if u is None else k * batch + u * size
        picks = []
        gate_cols = []
        for n, (q, r) in enumerate(blocks):
            s = slot((x + q) % cols, zz, (c + r) % CORES)
            chosen, row = pick(s, me, h)
            tokens, upstreams = tok.at[s, h], up.at[s, h]
            if u is not None:
                span = slice(u * part, (u + 1) * part)
                chosen, row = chosen[u * few : (u + 1) * few, span], row[:, span]
                tokens = tokens.at[pl.ds(u * part, part)]
                upstreams = upstreams.at[pl.ds(u * part, part)]
            picks.append((s, chosen))
            gate_cols.append(jnp.sum(chosen * row, axis=1, keepdims=True))
            hot = chosen.astype(jnp.bfloat16)
            where = base + n * count_rows
            where = pl.ds(pl.multiple_of(where, count_rows) if u is None else where, count_rows)
            xs[where, :] = dot(hot, tokens[...], ((1,), (0,))).astype(jnp.bfloat16)
            su[where, :] = dot(hot, upstreams[...], ((1,), (0,))).astype(jnp.bfloat16)
        here = pl.ds(base, size)
        gate = jnp.concatenate(gate_cols, axis=0)
        upstream = su[here, :]
        projected = dot(xs[here, :], win[...], ((1,), (0,)))
        back_raw = dot(upstream, wout_t[...], ((1,), (0,)))
        su[here, :] = (gate * upstream.astype(jnp.float32)).astype(jnp.bfloat16)
        gate_part, up_part = projected[:, :ff], projected[:, ff:]
        activated, derivative = silu_parts(gate_part)
        hidden = (activated * up_part).astype(jnp.bfloat16)
        hid[here, :] = hidden
        scores = jnp.sum(hidden.astype(jnp.float32) * back_raw, axis=1, keepdims=True)
        scores = scores.astype(jnp.bfloat16).astype(jnp.float32)
        back_hidden = gate * back_raw
        gp[here, :ff] = (back_hidden * up_part * derivative).astype(jnp.bfloat16)
        gp[here, ff:] = (back_hidden * activated).astype(jnp.bfloat16)
        grads = dot(gp[here, :], win_t[...], ((1,), (0,))).astype(jnp.bfloat16)
        for n, (q, r) in enumerate(blocks):
            piece = grads[n * count_rows : (n + 1) * count_rows]
            if u is None:
                if r == 0:
                    igb[k, q, c] = piece
                else:
                    igs[k, q] = piece
                    send_ig(q, k).start()
            else:
                at = pl.ds(u * few, few)
                if r == 0:
                    igb[k, q, c, at] = piece
                else:
                    igs[k, q, at] = piece
                    send_last_ig(q, u).start()
        for n, (q, r) in enumerate(blocks):
            s, chosen = picks[n]
            line = jnp.sum(chosen * scores[n * count_rows : (n + 1) * count_rows], axis=0, keepdims=True)
            if u is not None:
                ahead = (HALVES - 1) * half + u * part
                parts = [jnp.zeros((1, ahead), jnp.float32), line]
                if u < SPLIT - 1:
                    parts.append(jnp.zeros((1, local - ahead - part), jnp.float32))
                scs[s] = scs[s] + jnp.broadcast_to(jnp.concatenate(parts, axis=1), scs.shape[1:])
                if u == SPLIT - 1:
                    if q == 0 and r == 0:
                        scr[me] = scs[me]
                    else:
                        send_score(s).start()
                continue
            rest = jnp.zeros_like(line)
            first = jnp.concatenate([line, rest], axis=1)
            second = jnp.concatenate([rest, line], axis=1)

            @pl.when(h == 0)
            def _():
                scs[s] = jnp.broadcast_to(first, scs.shape[1:])

            @pl.when(h == 1)
            def _():
                scs[s] = scs[s] + jnp.broadcast_to(second, scs.shape[1:])
                send_score(s).start()

    def send_sum(zz, h, q, u, side, to_z):
        place = jnp.where((zz == to_z) & (side == 1), depth, zz)
        at = pl.ds(u * part, part) if q else pl.ds(0, half)
        landed = cr_sem.at[place, h, q + u]
        return send(cs.at[zz, h, q, at], cr.at[place, h, q, at], sent_sem.at[6], landed, x, to_z, c)

    def send_across(h, u=None):
        at = pl.ds(0, half) if u is None else pl.ds(u * part, part)
        landed = rx_sem.at[0 if u is None else 1 + u]
        return send(cs.at[z, h, 1, at], rx.at[h, at], sent_sem.at[6], landed, 1 - x, z, c)

    def gather(zz, h, q, u, total):
        at = pl.ds(u * part, part) if q else pl.ds(0, half)
        to = pl.ds(0, part if q else half)
        acc[to, :] = total
        for side, ok in ((0, (zz <= z) & (z < depth - 1)), (1, (zz >= z) & (z > 0))):

            @pl.when(ok)
            def _():
                send_sum(zz, h, q, u, side, z).wait_recv()
                place = jnp.where((zz == z) & (side == 1), depth, zz)
                acc[to, :] += cr[place, h, q, at].astype(jnp.float32)

        return at, to

    def hot_of(s, h):
        return [pick(s, slot(x, z, m), h)[0] for m in range(CORES)]

    def pass_on(k, q):
        zz, h = step_of(k)
        hot = jnp.concatenate(hot_of(slot((x + q) % cols, zz, c), h), axis=0).astype(jnp.bfloat16)
        if q == 1:
            settle(igs.at[0], igr_sem.at[k])
        pair = igb[k, q].reshape(CORES * rows, features)
        for u in range(SPLIT if q else 1):
            mine = hot[:, u * part : (u + 1) * part] if q else hot
            at, to = gather(zz, h, q, u, dot(mine, pair, ((0,), (0,))))
            cs[zz, h, q, at] = acc[to, :].astype(jnp.bfloat16)

            @pl.when(zz < z)
            def _():
                send_sum(zz, h, q, u, 0, z - 1).start()

            @pl.when(zz > z)
            def _():
                send_sum(zz, h, q, u, 1, z + 1).start()

    def home_sum(k, h, q):
        hot = jnp.concatenate(hot_of(slot((x + q) % cols, z, c), h), axis=0).astype(jnp.bfloat16)
        pair = igb[k, q].reshape(CORES * rows, features)
        return hot, pair

    def home_first():
        settle(igs.at[0], igr_sem.at[0])
        hot, pair = home_sum(0, 0, 1)
        for u in range(SPLIT):
            span = slice(u * part, (u + 1) * part)
            at, to = gather(z, 0, 1, u, dot(hot[:, span], pair, ((0,), (0,))))
            cs[z, 0, 1, at] = acc[to, :].astype(jnp.bfloat16)
        send_across(0).start()

    def home_last(u):
        k = steps - 1
        s = slot(1 - x, z, c)
        here, span = slice(u * few, (u + 1) * few), slice(u * part, (u + 1) * part)
        hot = jnp.concatenate([one[here, span] for one in hot_of(s, HALVES - 1)], axis=0)
        settle(igs.at[0, 0], igr_sem.at[k] if u == 0 else igr_tail_sem.at[0])
        pair = igb[k, 1, :, pl.ds(u * few, few)].reshape(CORES * few, features)
        at, to = gather(z, HALVES - 1, 1, u, dot(hot.astype(jnp.bfloat16), pair, ((0,), (0,))))
        cs[z, HALVES - 1, 1, at] = acc[to, :].astype(jnp.bfloat16)
        send_across(HALVES - 1, u).start()

    def home_own():
        for k, h in ((0, 0), (steps - 1, HALVES - 1)):
            hot, pair = home_sum(k, h, 0)
            gather(z, h, 0, 0, dot(hot, pair, ((0,), (0,))))
            rk[h] = acc[...]

    words = lag_words(depth)
    word = jnp.int32(words[0])
    for k in range(1, depth):
        word = jnp.where(z == k, words[k], word)

    edge = (z == 0) | (z == depth - 1)
    inner = jnp.logical_not(edge)

    def pass_all(i, q):
        def one(j, left):
            k = steps - 1 - j
            due = (k + 2 + left % 8 == i) & (j > 0)

            @pl.when(due)
            def _():
                pass_on(k, q)

            return left // 8

        lax.fori_loop(0, steps - 1, one, word)

    along_z(0, 0)
    across(0, 0)

    def step(i, carry):
        @pl.when(i < steps)
        def _():
            along_z(i, 1)
            across(i, 1)

        @pl.when(i == 0)
        def _():
            loads[4].wait()
            loads[5].wait()
            win_t[...] = win[...].T
            wout_t[...] = wout[...].T

        @pl.when(inner & (i >= 2))
        def _():
            pass_all(i, 1)

        @pl.when(i >= 1)
        def _():
            from_across(i - 1, 1)

        @pl.when(inner & (i >= 2))
        def _():
            pass_all(i, 0)

        @pl.when(i >= 1)
        def _():
            from_partner(i - 1)
            compute(i - 1)

        @pl.when(i + 1 < steps)
        def _():
            along_z(i + 1, 0)
            across(i + 1, 0)

        @pl.when(i < steps - 1)
        def _():
            from_across(i, 0)

        @pl.when(i == steps - 1)
        def _():
            last_from_across(0)

        @pl.when(edge & (i >= 1))
        def _():
            pass_all(i + 1, 1)
            pass_all(i + 1, 0)

        return carry

    lax.fori_loop(0, steps, step, 0)

    @pl.when(inner)
    def _():
        pass_all(steps, 1)

    last_from_partner(0)
    compute(steps - 1, 0)
    last_from_across(1)
    home_first()

    @pl.when(inner)
    def _():
        pass_all(steps, 0)

    last_from_partner(1)
    compute(steps - 1, 1)
    home_last(0)

    wide = min(features, 256)

    def gin(t, carry):
        at = pl.ds(pl.multiple_of(t * wide, wide), wide)
        gin_ref[0, at, :] = dot(xs[:, at], gp[...], ((0,), (0,))).astype(jnp.bfloat16)
        return carry

    early = jnp.where(edge, 2, 1)
    lax.fori_loop(0, early, gin, 0)
    home_last(1)
    lax.fori_loop(early, features // wide, gin, 0)

    thin = 128

    @pl.loop(0, ff // thin)
    def _(t):
        at = pl.ds(pl.multiple_of(t * thin, thin), thin)
        gdown_ref[0, at, :] = dot(hid[:, at], su[...], ((0,), (0,))).astype(jnp.bfloat16)

    home_own()
    settle(scr.at[pl.ds(0, count - 1)], scr_sem.at[0])
    scores = scr[:, 0, :]
    place = lax.broadcasted_iota(jnp.int32, (top, local), 0)
    gate_grads = jnp.zeros((top, local), jnp.float32)
    for k in range(top):
        value = jnp.sum(jnp.where(routes[k : k + 1] == ids, scores, 0.0), axis=0, keepdims=True)
        gate_grads = jnp.where(place == k, value, gate_grads)
    gg_ref[...] = gate_grads.astype(jnp.bfloat16)

    for h in range(HALVES):
        for u in (None,) if h == 0 else range(SPLIT):
            send_across(h, u).wait_recv()
        tg_ref[pl.ds(h * half, half), :] = (rk[h] + rx[h].astype(jnp.float32)).astype(jnp.bfloat16)

    for at in range(depth):
        sent = (depth - at if at > 0 else 0) + (at + 1 if at < depth - 1 else 0)

        @pl.when(z == at)
        def _():
            settle(tok.at[pl.ds(0, 2 * sent)], sent_sem.at[0])
            settle(table.at[pl.ds(0, sent)], sent_sem.at[3])

    settle(tok.at[pl.ds(0, 2 * depth)], sent_sem.at[1])
    settle(tok, sent_sem.at[2])
    settle(table.at[pl.ds(0, 3 * depth)], sent_sem.at[4])
    settle(igs, sent_sem.at[5])
    settle(tok.at[pl.ds(0, depth * cols - 1)], sent_sem.at[6])
    settle(scs.at[pl.ds(0, count - 1)], sent_sem.at[7])


def store_kernel(*refs):
    count = len(refs) // 2
    sems = refs[-1]
    copies = [
        pltpu.make_async_copy(refs[k], refs[count + k], sems.at[k]) for k in range(count)
    ]
    for one in copies:
        one.start()
    for one in copies:
        one.wait()


def store(*arrays):
    anywhere = pl.BlockSpec(memory_space=pl.ANY)
    return pl.pallas_call(
        store_kernel,
        out_shape=tuple(jax.ShapeDtypeStruct(a.shape, a.dtype) for a in arrays),
        in_specs=[pl.BlockSpec(memory_space=pltpu.VMEM)] * len(arrays),
        out_specs=(pl.BlockSpec(memory_space=pltpu.HBM),) * len(arrays),
        scratch_shapes=[pltpu.SemaphoreType.DMA((len(arrays),))],
        compiler_params=pltpu.CompilerParams(vmem_limit_bytes=8 * 2**20),
    )(*arrays)


def fused(tokens, grad_out, routes, gates, w_gate_up, w_down):
    first_size, depth = lax.axis_size("da"), lax.axis_size("db")
    cols = first_size // CORES
    experts = first_size * depth
    local, features = tokens.shape
    top = routes.shape[1]
    group = experts // top
    ff = w_down.shape[1]
    bf, f32 = jnp.bfloat16, jnp.float32
    half = local // HALVES
    rows = half // group
    steps = HALVES * depth
    total = rows * experts * HALVES
    dma = pltpu.SemaphoreType.DMA
    scratch = [
        pltpu.VMEM((top, local), routes.dtype),
        pltpu.VMEM((top, local), gates.dtype),
        pltpu.VMEM((experts, HALVES, half, features), bf),
        pltpu.VMEM((experts, HALVES, half, features), bf),
        pltpu.VMEM((experts, experts, local), bf),
        pltpu.VMEM((features, 2 * ff), bf),
        pltpu.VMEM((ff, features), bf),
        pltpu.VMEM((2 * ff, features), bf),
        pltpu.VMEM((features, ff), bf),
        pltpu.VMEM((total, features), bf),
        pltpu.VMEM((total, features), bf),
        pltpu.VMEM((total, ff), bf),
        pltpu.VMEM((total, 2 * ff), bf),
        pltpu.VMEM((steps, cols, rows, features), bf),
        pltpu.VMEM((steps, cols, CORES, rows, features), bf),
        pltpu.VMEM((half, features), f32),
        pltpu.VMEM((depth, HALVES, cols, half, features), bf),
        pltpu.VMEM((depth + 1, HALVES, cols, half, features), bf),
        pltpu.VMEM((HALVES, half, features), f32),
        pltpu.VMEM((HALVES, half, features), bf),
        pltpu.VMEM((experts, 8, local), f32),
        pltpu.VMEM((experts, 8, local), f32),
        pltpu.VMEM((2 * cols * half * features // 128 + cols * experts, 128), bf),
        dma((5,)),
        dma((cols, depth, HALVES, 2)),
        dma((steps,)),
        dma((steps,)),
        dma((depth + 1, HALVES, 1 + SPLIT)),
        dma((1 + SPLIT,)),
        dma((1,)),
        dma((8,)),
        dma((2,)),
        dma((1,)),
        dma((1,)),
    ]
    vmem = pl.BlockSpec(memory_space=pltpu.VMEM)
    hbm = pl.BlockSpec(memory_space=pltpu.HBM)
    token_grads, gate_grads, grad_in, grad_down = pl.pallas_call(
        functools.partial(fused_kernel, cols, depth, group),
        out_shape=(
            jax.ShapeDtypeStruct((local, features), bf),
            jax.ShapeDtypeStruct((top, local), bf),
            jax.ShapeDtypeStruct(w_gate_up.shape, bf),
            jax.ShapeDtypeStruct(w_down.shape, bf),
        ),
        in_specs=[hbm] * 6,
        out_specs=(vmem, vmem, vmem, vmem),
        scratch_shapes=scratch,
        compiler_params=pltpu.CompilerParams(
            collective_id=0, has_side_effects=True, vmem_limit_bytes=44 * 2**20
        ),
    )(
        *(
            pltpu.with_memory_space_constraint(a, pltpu.HBM)
            for a in (tokens, grad_out, routes.T, gates.T, w_gate_up, w_down)
        )
    )
    token_grads, gate_grads, grad_in, grad_down = store(token_grads, gate_grads, grad_in, grad_down)
    return token_grads, gate_grads.T, grad_in, grad_down


def fits(tokens, routes, w_down):
    first_size = lax.axis_size("da")
    experts = first_size * lax.axis_size("db")
    local, features = tokens.shape
    group = experts // routes.shape[1]
    held = 2 * experts * local * features * 2
    return (
        lax.axis_size("replica") == 1
        and first_size % CORES == 0
        and first_size == 2 * CORES
        and 2 * 3 * lax.axis_size("db") <= 30
        and held <= 16 * 2**20
        and local == 128
        and experts <= local
        and max(map(max, relay_slots(lax.axis_size("db")))) == HALVES * lax.axis_size("db") + 1
        and (local // (HALVES * SPLIT * group)) % 16 == 0
        and w_down.shape[1] % 128 == 0
    )


def route(*arrays):
    if fits(arrays[0], arrays[2], arrays[5]):
        return fused(*arrays)
    return body(*arrays)


def solution(mesh):
    placed = (
        P(("groups", "replica", "da", "db"), None),
        P(("groups", "replica", "da", "db"), None),
        P(("groups", "replica", "da", "db"), None),
        P(("groups", "replica", "da", "db"), None),
        P(("da", "db"), "replica", None),
        P(("da", "db"), "replica", None),
    )
    return jax.shard_map(
        route,
        mesh=mesh,
        in_specs=placed,
        out_specs=(
            P(("groups", "replica", "da", "db"), None),
            P(("groups", "replica", "da", "db"), None),
            P(("groups", "da", "db"), "replica", None),
            P(("groups", "da", "db"), "replica", None),
        ),
        check_vma=False,
    )
```

```python
import functools

import jax
import jax.numpy as jnp
from jax import lax
from jax.experimental import pallas as pl
from jax.experimental.pallas import tpu as pltpu
from jax.sharding import PartitionSpec as P


CORES = 2
HALVES = 2
SPLIT = 2
MESH = pl.DeviceIdType.MESH


def silu_parts(projected):
    sigmoid = jax.nn.sigmoid(projected)
    return (projected * sigmoid, sigmoid * (1.0 + projected * (1.0 - sigmoid)))


def body(tokens, grad_out, routes, gates, w_gate_up, w_down):
    local_tokens, features = tokens.shape
    top_count = routes.shape[1]
    hidden_units = w_gate_up.shape[2] // 2
    first_size = lax.axis_size("da")
    second_size = lax.axis_size("db")
    experts = first_size * second_size
    per_round = experts // top_count
    rounds = local_tokens // per_round
    expert_ids = lax.broadcasted_iota(jnp.int32, (1, 1, 1, experts), 3)
    matches = routes.reshape(rounds, per_round, top_count, 1) == expert_ids
    gate_values = gates.reshape(rounds, per_round, top_count, 1).astype(jnp.float32)
    gate_table = jnp.sum(jnp.where(matches, gate_values, 0.0), axis=(1, 2)).astype(jnp.bfloat16)
    chosen = jnp.any(matches, axis=2).astype(jnp.bfloat16)
    input_send = jnp.einsum(
        "rge,rgd->red",
        chosen,
        tokens.reshape(rounds, per_round, features),
        preferred_element_type=jnp.float32,
    ).astype(jnp.bfloat16)
    upstream_send = jnp.einsum(
        "rge,rgd->red",
        chosen,
        grad_out.reshape(rounds, per_round, features),
        preferred_element_type=jnp.float32,
    ).astype(jnp.bfloat16)
    input_recv, upstream_recv, gate_recv = (
        lax.all_to_all(input_send, ("da", "db"), split_axis=1, concat_axis=1, tiled=True),
        lax.all_to_all(upstream_send, ("da", "db"), split_axis=1, concat_axis=1, tiled=True),
        lax.all_to_all(gate_table, ("da", "db"), split_axis=1, concat_axis=1, tiled=True),
    )
    input_rows = input_recv.reshape(-1, features)
    upstream_rows = upstream_recv.reshape(-1, features)
    gate_rows = gate_recv.reshape(-1, 1).astype(jnp.float32)
    w_in, w_out = (
        lax.all_gather(w_gate_up[0], "replica", axis=0, tiled=True),
        lax.all_gather(w_down[0], "replica", axis=0, tiled=True),
    )
    projected = jnp.dot(input_rows, w_in, preferred_element_type=jnp.float32)
    back_raw = jnp.einsum("rd,fd->rf", upstream_rows, w_out, preferred_element_type=jnp.float32)
    gate_part = projected[:, :hidden_units]
    up_part = projected[:, hidden_units:]
    activated, derivative = silu_parts(gate_part)
    hidden = (activated * up_part).astype(jnp.bfloat16)
    gate_scores = jnp.sum(hidden.astype(jnp.float32) * back_raw, axis=1).astype(jnp.bfloat16)
    back_hidden = gate_rows * back_raw
    grad_projected = jnp.concatenate(
        [back_hidden * up_part * derivative, back_hidden * activated], axis=1
    ).astype(jnp.bfloat16)
    scaled_upstream = (gate_rows * upstream_rows.astype(jnp.float32)).astype(jnp.bfloat16)
    input_grads = jnp.einsum("rf,df->rd", grad_projected, w_in, preferred_element_type=jnp.float32)
    input_grads = input_grads.astype(jnp.bfloat16).reshape(rounds, experts, features)
    score_back = gate_scores.reshape(rounds, experts)
    returned, score_ret = (
        lax.all_to_all(input_grads, ("da", "db"), split_axis=1, concat_axis=1, tiled=True),
        lax.all_to_all(score_back, ("da", "db"), split_axis=1, concat_axis=1, tiled=True),
    )
    score_ret = score_ret.reshape(rounds, 1, 1, experts).astype(jnp.float32)
    token_grads = (
        jnp.einsum("rge,red->rgd", chosen, returned, preferred_element_type=jnp.float32)
        .astype(jnp.bfloat16)
        .reshape(local_tokens, features)
    )
    gate_grads = (
        jnp.sum(jnp.where(matches, score_ret, 0.0), axis=3)
        .astype(jnp.bfloat16)
        .reshape(local_tokens, top_count)
    )
    columns = input_rows
    grad_in = lax.psum_scatter(
        jnp.einsum("rd,rf->df", columns, grad_projected, preferred_element_type=jnp.float32).astype(
            jnp.bfloat16
        ),
        "replica",
        scatter_dimension=0,
        tiled=True,
    )
    columns = hidden
    grad_down = lax.psum_scatter(
        jnp.einsum(
            "rf,rd->fd", columns, scaled_upstream, preferred_element_type=jnp.float32
        ).astype(jnp.bfloat16),
        "replica",
        scatter_dimension=0,
        tiled=True,
    )
    return (token_grads, gate_grads, grad_in[None], grad_down[None])


def visit(j, z, n):
    m = jnp.minimum(z, n - 1 - z)
    near = z + (1 - 2 * (j % 2)) * ((j + 1) // 2)
    far = jnp.where(z < n - 1 - z, j, n - 1 - j)
    return jnp.where(j <= 2 * m, near, far)


def dot(a, b, dims):
    return lax.dot_general(a, b, (dims, ((), ())), preferred_element_type=jnp.float32)


def position(d, z, n):
    away = abs(d - z)
    if away <= min(z, n - 1 - z):
        return 2 * away - (1 if d < z else 0)
    return d if z < n - 1 - z else n - 1 - d


def relay_slots(n):
    last = 2 * n - 1

    def ready(z, d, h):
        k = position(d, z, n)
        k = last - k if h else k
        feeds = [u for u in (z - 1, z + 1) if 0 <= u < n and abs(u - d) == abs(z - d) + 1]
        return max([k + 2] + [ready(u, d, h) + 1 for u in feeds])

    table = []
    for z in range(n):
        row = [0] * (2 * n)
        for d in range(n):
            k = position(d, z, n)
            row[k] = ready(z, d, 0)
            row[last - k] = ready(z, d, 1)
        table.append(row)
    return table


def lag_words(n):
    return [sum((at - k - 2) * 8 ** (2 * n - 1 - k) for k, at in enumerate(row)) for row in relay_slots(n)]


def fused_kernel(
    cols, depth, group,
    tok_hbm, up_hbm, routes_hbm, gates_hbm, win_hbm, wout_hbm,
    tg_ref, gg_ref, gin_ref, gdown_ref,
    routes_ref, gates_ref, tok, up, table, win, wout, win_t, wout_t, xs, su, hid, gp, igs, igb, acc, cs, cr, rk, rx, scs, scr, bulk,
    load_sem, recv_sem, near_sem, igr_sem, cr_sem, rx_sem, scr_sem, sent_sem,
    tail_sem, near_tail_sem, igr_tail_sem,
):
    da = lax.axis_index("da")
    z = lax.axis_index("db")
    x, c = da // CORES, da % CORES
    half, features = tok.shape[2], tok.shape[3]
    local = HALVES * half
    experts = table.shape[1]
    top = routes_ref.shape[0]
    rows = half // group
    ff = wout.shape[0]
    steps = HALVES * depth
    part = half // SPLIT
    few = rows // SPLIT

    def slot(xx, zz, cc):
        return (xx * CORES + cc) * depth + zz

    me = slot(x, z, c)
    loads = []
    for h in range(HALVES):
        span = pl.ds(h * half, half)
        loads.append(pltpu.make_async_copy(tok_hbm.at[span], tok.at[me, h], load_sem.at[0]))
        loads.append(pltpu.make_async_copy(up_hbm.at[span], up.at[me, h], load_sem.at[0]))
    loads += [
        pltpu.make_async_copy(win_hbm.at[0], win, load_sem.at[1]),
        pltpu.make_async_copy(wout_hbm.at[0], wout, load_sem.at[2]),
        pltpu.make_async_copy(routes_hbm, routes_ref, load_sem.at[3]),
        pltpu.make_async_copy(gates_hbm, gates_ref, load_sem.at[4]),
    ]
    def settle(view, sem):
        pltpu.make_async_copy(view, view, sem).wait()

    barrier = pltpu.get_barrier_semaphore()
    count = cols * CORES * depth

    def greet(xx, zz, cc):
        pl.semaphore_signal(
            barrier, inc=1, device_id={"da": xx * CORES + cc, "db": zz}, device_id_type=MESH
        )

    @pl.when(z > 0)
    def _():
        greet(x, z - 1, c)

    @pl.when(z < depth - 1)
    def _():
        greet(x, z + 1, c)

    greet(1 - x, z, c)
    greet(x, z, 1 - c)
    for k in (6, 7, 0, 1, 2, 3, 4, 5):
        loads[k].start()

    loads[6].wait()
    loads[7].wait()
    routes = routes_ref[...]
    gates = gates_ref[...].astype(jnp.float32)
    ids = lax.broadcasted_iota(jnp.int32, (experts, local), 0)
    chart = jnp.zeros((experts, local), jnp.float32)
    for k in range(top):
        chart = chart + jnp.where(routes[k : k + 1] == ids, gates[k : k + 1], 0.0)
    table[me] = chart.astype(jnp.bfloat16)

    settle(tok.at[pl.ds(0, CORES)], load_sem.at[0])
    pl.semaphore_wait(barrier, 2 + jnp.where(z > 0, 1, 0) + jnp.where(z < depth - 1, 1, 0))

    held = (tok, up)

    def send(src, dst, send_sem, recv, to_x, to_z, to_c):
        return pltpu.make_async_remote_copy(
            src_ref=src,
            dst_ref=dst,
            send_sem=send_sem,
            recv_sem=recv,
            device_id={"da": to_x * CORES + to_c, "db": to_z},
            device_id_type=MESH,
        )

    def start(copy):
        copy.start()

    def wait_recv(copy):
        copy.wait_recv()

    def both(xx, zz, h, a, way, act, to_x, to_z, to_c, near=None):
        s = slot(xx, zz, c)
        ref = held[a].at[s, h]
        landed = recv_sem.at[xx, zz, h, a] if near is None else near_sem.at[near]
        copy = send(ref, ref, sent_sem.at[way], landed, to_x, to_z, to_c)
        if a != 0:
            act(copy)
            return

        @pl.when(h != 0)
        def _():
            act(copy)

        @pl.when(h == 0)
        def _():
            if act is start:
                copy.start()
                page = table.at[s]
                send(page, page, sent_sem.at[3 + (way > 0)], landed, to_x, to_z, to_c).start()
            else:
                settle(bulk.at[pl.ds(0, half * features // 128 + experts)], landed)

    def step_of(i):
        j = jnp.minimum(i, steps - 1 - i)
        return visit(j, z, depth), jnp.where(i >= depth, 1, 0)

    def along_z(e, a):
        def one(reach, sign):
            last = 2 * reach + 1
            k = jnp.minimum(e, last - e)
            h = jnp.where(e > reach, 1, 0)
            zz = z + sign * k

            @pl.when((e <= last) & (k > 0))
            def _():
                both(x, zz, h, a, 0, wait_recv, x, z, 1 - c)

            ahead = z - sign

            @pl.when((e <= last) & (ahead >= 0) & (ahead < depth))
            def _():
                both(x, zz, h, a, 0, start, x, ahead, c)

        one(depth - 1 - z, 1)
        one(z, -1)

    def last_part(xx, u, a, way, to_x, to_c, near=None):
        ref = held[a].at[slot(xx, z, c), HALVES - 1, pl.ds(u * part, part)]
        landed = near
        if near is None:
            landed = recv_sem.at[xx, z, HALVES - 1, a] if u == 0 else tail_sem.at[a]
        return send(ref, ref, sent_sem.at[way], landed, to_x, z, to_c)

    def last_from_across(u):
        near = near_sem.at[steps - 1] if u == 0 else near_tail_sem.at[0]
        for a in range(2):
            last_part(1 - x, u, a, 1, 1 - x, c).wait_recv()
            last_part(1 - x, u, a, 2, x, 1 - c, near).start()

    def last_from_partner(u):
        if u == 0:
            settle(xs.at[pl.ds(0, (cols + 1) * half)], near_sem.at[steps - 1])
        else:
            settle(tok.at[0, 0], near_tail_sem.at[0])

    def across(i, a):
        zz, h = step_of(i)

        @pl.when(i < steps - 1)
        def _():
            both(x, zz, h, a, 1, start, 1 - x, z, c)

        @pl.when(i == steps - 1)
        def _():
            for b in range(2):
                last_part(x, a, b, 1, 1 - x, c).start()

        both(x, zz, h, a, 2, start, x, z, 1 - c, near=i)

    def from_across(i, a):
        zz, h = step_of(i)
        both(1 - x, zz, h, a, 1, wait_recv, 1 - x, z, c)
        both(1 - x, zz, h, a, 2, start, x, z, 1 - c, near=i)

    def from_partner(i):
        zz, h = step_of(i)

        @pl.when(h == 0)
        def _():
            settle(bulk, near_sem.at[i])

        @pl.when(h != 0)
        def _():
            settle(tok.at[pl.ds(0, cols)], near_sem.at[i])

    def pick(s, e, h):
        chart_s = table[s].astype(jnp.float32)
        which = lax.broadcasted_iota(jnp.int32, chart_s.shape, 0) == e
        row = jnp.sum(jnp.where(which, chart_s, 0.0), axis=0, keepdims=True)
        row = jnp.where(h == 0, row[:, :half], row[:, half:])
        off = lax.broadcasted_iota(jnp.int32, (rows, half), 1) - group * lax.broadcasted_iota(
            jnp.int32, (rows, half), 0
        )
        hit = (off >= 0) & (off < group) & (row > 0.0)
        return jnp.where(hit, 1.0, 0.0), row

    def send_ig(q, k):
        return send(igs.at[k, q], igb.at[k, q, c], sent_sem.at[5], igr_sem.at[k], x, z, 1 - c)

    def send_last_ig(q, u):
        at = pl.ds(u * few, few)
        landed = igr_sem.at[steps - 1] if u == 0 else igr_tail_sem.at[0]
        src, dst = igs.at[steps - 1, q, at], igb.at[steps - 1, q, c, at]
        return send(src, dst, sent_sem.at[5], landed, x, z, 1 - c)

    def send_score(s):
        return pltpu.make_async_remote_copy(
            src_ref=scs.at[s],
            dst_ref=scr.at[me],
            send_sem=sent_sem.at[7],
            recv_sem=scr_sem.at[0],
            device_id={"da": s // depth, "db": s % depth},
            device_id_type=MESH,
        )

    blocks = [(q, r) for q in range(cols) for r in range(CORES)]
    batch = len(blocks) * rows

    def compute(k, u=None):
        zz, h = step_of(k) if u is None else (z, HALVES - 1)
        count_rows = rows if u is None else few
        size = len(blocks) * count_rows
        base = pl.multiple_of(k * batch, batch) if u is None else k * batch + u * size
        picks = []
        gate_cols = []
        for n, (q, r) in enumerate(blocks):
            s = slot((x + q) % cols, zz, (c + r) % CORES)
            chosen, row = pick(s, me, h)
            tokens, upstreams = tok.at[s, h], up.at[s, h]
            if u is not None:
                span = slice(u * part, (u + 1) * part)
                chosen, row = chosen[u * few : (u + 1) * few, span], row[:, span]
                tokens = tokens.at[pl.ds(u * part, part)]
                upstreams = upstreams.at[pl.ds(u * part, part)]
            picks.append((s, chosen))
            gate_cols.append(jnp.sum(chosen * row, axis=1, keepdims=True))
            hot = chosen.astype(jnp.bfloat16)
            where = base + n * count_rows
            where = pl.ds(pl.multiple_of(where, count_rows) if u is None else where, count_rows)
            xs[where, :] = dot(hot, tokens[...], ((1,), (0,))).astype(jnp.bfloat16)
            su[where, :] = dot(hot, upstreams[...], ((1,), (0,))).astype(jnp.bfloat16)
        here = pl.ds(base, size)
        gate = jnp.concatenate(gate_cols, axis=0)
        upstream = su[here, :]
        projected = dot(xs[here, :], win[...], ((1,), (0,)))
        back_raw = dot(upstream, wout_t[...], ((1,), (0,)))
        su[here, :] = (gate * upstream.astype(jnp.float32)).astype(jnp.bfloat16)
        gate_part, up_part = projected[:, :ff], projected[:, ff:]
        activated, derivative = silu_parts(gate_part)
        hidden = (activated * up_part).astype(jnp.bfloat16)
        hid[here, :] = hidden
        scores = jnp.sum(hidden.astype(jnp.float32) * back_raw, axis=1, keepdims=True)
        scores = scores.astype(jnp.bfloat16).astype(jnp.float32)
        back_hidden = gate * back_raw
        gp[here, :ff] = (back_hidden * up_part * derivative).astype(jnp.bfloat16)
        gp[here, ff:] = (back_hidden * activated).astype(jnp.bfloat16)
        grads = dot(gp[here, :], win_t[...], ((1,), (0,))).astype(jnp.bfloat16)
        for n, (q, r) in enumerate(blocks):
            piece = grads[n * count_rows : (n + 1) * count_rows]
            if u is None:
                if r == 0:
                    igb[k, q, c] = piece
                else:
                    igs[k, q] = piece
                    send_ig(q, k).start()
            else:
                at = pl.ds(u * few, few)
                if r == 0:
                    igb[k, q, c, at] = piece
                else:
                    igs[k, q, at] = piece
                    send_last_ig(q, u).start()
        for n, (q, r) in enumerate(blocks):
            s, chosen = picks[n]
            line = jnp.sum(chosen * scores[n * count_rows : (n + 1) * count_rows], axis=0, keepdims=True)
            if u is not None:
                ahead = (HALVES - 1) * half + u * part
                parts = [jnp.zeros((1, ahead), jnp.float32), line]
                if u < SPLIT - 1:
                    parts.append(jnp.zeros((1, local - ahead - part), jnp.float32))
                scs[s] = scs[s] + jnp.broadcast_to(jnp.concatenate(parts, axis=1), scs.shape[1:])
                if u == SPLIT - 1:
                    if q == 0 and r == 0:
                        scr[me] = scs[me]
                    else:
                        send_score(s).start()
                continue
            rest = jnp.zeros_like(line)
            first = jnp.concatenate([line, rest], axis=1)
            second = jnp.concatenate([rest, line], axis=1)

            @pl.when(h == 0)
            def _():
                scs[s] = jnp.broadcast_to(first, scs.shape[1:])

            @pl.when(h == 1)
            def _():
                scs[s] = scs[s] + jnp.broadcast_to(second, scs.shape[1:])
                send_score(s).start()

    def send_sum(zz, h, q, u, side, to_z):
        place = jnp.where((zz == to_z) & (side == 1), depth, zz)
        at = pl.ds(u * part, part) if q else pl.ds(0, half)
        landed = cr_sem.at[place, h, q + u]
        return send(cs.at[zz, h, q, at], cr.at[place, h, q, at], sent_sem.at[6], landed, x, to_z, c)

    def send_across(h, u=None):
        at = pl.ds(0, half) if u is None else pl.ds(u * part, part)
        landed = rx_sem.at[0 if u is None else 1 + u]
        return send(cs.at[z, h, 1, at], rx.at[h, at], sent_sem.at[6], landed, 1 - x, z, c)

    def gather(zz, h, q, u, total):
        at = pl.ds(u * part, part) if q else pl.ds(0, half)
        to = pl.ds(0, part if q else half)
        acc[to, :] = total
        for side, ok in ((0, (zz <= z) & (z < depth - 1)), (1, (zz >= z) & (z > 0))):

            @pl.when(ok)
            def _():
                send_sum(zz, h, q, u, side, z).wait_recv()
                place = jnp.where((zz == z) & (side == 1), depth, zz)
                acc[to, :] += cr[place, h, q, at].astype(jnp.float32)

        return at, to

    def hot_of(s, h):
        return [pick(s, slot(x, z, m), h)[0] for m in range(CORES)]

    def pass_on(k, q):
        zz, h = step_of(k)
        hot = jnp.concatenate(hot_of(slot((x + q) % cols, zz, c), h), axis=0).astype(jnp.bfloat16)
        if q == 1:
            settle(igs.at[0], igr_sem.at[k])
        pair = igb[k, q].reshape(CORES * rows, features)
        for u in range(SPLIT if q else 1):
            mine = hot[:, u * part : (u + 1) * part] if q else hot
            at, to = gather(zz, h, q, u, dot(mine, pair, ((0,), (0,))))
            cs[zz, h, q, at] = acc[to, :].astype(jnp.bfloat16)

            @pl.when(zz < z)
            def _():
                send_sum(zz, h, q, u, 0, z - 1).start()

            @pl.when(zz > z)
            def _():
                send_sum(zz, h, q, u, 1, z + 1).start()

    def home_sum(k, h, q):
        hot = jnp.concatenate(hot_of(slot((x + q) % cols, z, c), h), axis=0).astype(jnp.bfloat16)
        pair = igb[k, q].reshape(CORES * rows, features)
        return hot, pair

    def home_first():
        settle(igs.at[0], igr_sem.at[0])
        hot, pair = home_sum(0, 0, 1)
        for u in range(SPLIT):
            span = slice(u * part, (u + 1) * part)
            at, to = gather(z, 0, 1, u, dot(hot[:, span], pair, ((0,), (0,))))
            cs[z, 0, 1, at] = acc[to, :].astype(jnp.bfloat16)
        send_across(0).start()

    def home_last(u):
        k = steps - 1
        s = slot(1 - x, z, c)
        here, span = slice(u * few, (u + 1) * few), slice(u * part, (u + 1) * part)
        hot = jnp.concatenate([one[here, span] for one in hot_of(s, HALVES - 1)], axis=0)
        settle(igs.at[0, 0], igr_sem.at[k] if u == 0 else igr_tail_sem.at[0])
        pair = igb[k, 1, :, pl.ds(u * few, few)].reshape(CORES * few, features)
        at, to = gather(z, HALVES - 1, 1, u, dot(hot.astype(jnp.bfloat16), pair, ((0,), (0,))))
        cs[z, HALVES - 1, 1, at] = acc[to, :].astype(jnp.bfloat16)
        send_across(HALVES - 1, u).start()

    def home_own():
        for k, h in ((0, 0), (steps - 1, HALVES - 1)):
            hot, pair = home_sum(k, h, 0)
            gather(z, h, 0, 0, dot(hot, pair, ((0,), (0,))))
            rk[h] = acc[...]

    words = lag_words(depth)
    word = jnp.int32(words[0])
    for k in range(1, depth):
        word = jnp.where(z == k, words[k], word)

    edge = (z == 0) | (z == depth - 1)
    inner = jnp.logical_not(edge)

    def pass_all(i, q):
        def one(j, left):
            k = steps - 1 - j
            due = (k + 2 + left % 8 == i) & (j > 0)

            @pl.when(due)
            def _():
                pass_on(k, q)

            return left // 8

        lax.fori_loop(0, steps - 1, one, word)

    along_z(0, 0)
    across(0, 0)

    def step(i, carry):
        @pl.when(i < steps)
        def _():
            along_z(i, 1)
            across(i, 1)

        @pl.when(i == 0)
        def _():
            loads[4].wait()
            loads[5].wait()
            win_t[...] = win[...].T
            wout_t[...] = wout[...].T

        @pl.when(inner & (i >= 2))
        def _():
            pass_all(i, 1)

        @pl.when(i >= 1)
        def _():
            from_across(i - 1, 1)

        @pl.when(inner & (i >= 2))
        def _():
            pass_all(i, 0)

        @pl.when(i >= 1)
        def _():
            from_partner(i - 1)
            compute(i - 1)

        @pl.when(i + 1 < steps)
        def _():
            along_z(i + 1, 0)
            across(i + 1, 0)

        @pl.when(i < steps - 1)
        def _():
            from_across(i, 0)

        @pl.when(i == steps - 1)
        def _():
            last_from_across(0)

        @pl.when(edge & (i >= 1))
        def _():
            pass_all(i + 1, 1)
            pass_all(i + 1, 0)

        return carry

    lax.fori_loop(0, steps, step, 0)

    @pl.when(inner)
    def _():
        pass_all(steps, 1)

    last_from_partner(0)
    compute(steps - 1, 0)
    last_from_across(1)
    home_first()

    @pl.when(inner)
    def _():
        pass_all(steps, 0)

    last_from_partner(1)
    compute(steps - 1, 1)
    home_last(0)

    wide = min(features, 256)

    def gin(t, carry):
        at = pl.ds(pl.multiple_of(t * wide, wide), wide)
        gin_ref[0, at, :] = dot(xs[:, at], gp[...], ((0,), (0,))).astype(jnp.bfloat16)
        return carry

    early = jnp.where(edge, 2, 1)
    lax.fori_loop(0, early, gin, 0)
    home_last(1)
    lax.fori_loop(early, features // wide, gin, 0)

    thin = 128

    @pl.loop(0, ff // thin)
    def _(t):
        at = pl.ds(pl.multiple_of(t * thin, thin), thin)
        gdown_ref[0, at, :] = dot(hid[:, at], su[...], ((0,), (0,))).astype(jnp.bfloat16)

    home_own()
    settle(scr.at[pl.ds(0, count - 1)], scr_sem.at[0])
    scores = scr[:, 0, :]
    place = lax.broadcasted_iota(jnp.int32, (top, local), 0)
    gate_grads = jnp.zeros((top, local), jnp.float32)
    for k in range(top):
        value = jnp.sum(jnp.where(routes[k : k + 1] == ids, scores, 0.0), axis=0, keepdims=True)
        gate_grads = jnp.where(place == k, value, gate_grads)
    gg_ref[...] = gate_grads.astype(jnp.bfloat16)

    for at in range(depth):
        sent = (depth - at if at > 0 else 0) + (at + 1 if at < depth - 1 else 0)

        @pl.when(z == at)
        def _():
            settle(tok.at[pl.ds(0, 2 * sent)], sent_sem.at[0])
            settle(table.at[pl.ds(0, sent)], sent_sem.at[3])

    settle(tok.at[pl.ds(0, 2 * depth)], sent_sem.at[1])
    settle(tok, sent_sem.at[2])
    settle(table.at[pl.ds(0, 3 * depth)], sent_sem.at[4])
    settle(igs, sent_sem.at[5])
    settle(scs.at[pl.ds(0, count - 1)], sent_sem.at[7])

    for h in range(HALVES):
        for u in (None,) if h == 0 else range(SPLIT):
            send_across(h, u).wait_recv()
        tg_ref[pl.ds(h * half, half), :] = (rk[h] + rx[h].astype(jnp.float32)).astype(jnp.bfloat16)
    settle(tok.at[pl.ds(0, depth * cols - 1)], sent_sem.at[6])


def store_kernel(*refs):
    count = len(refs) // 2
    sems = refs[-1]
    copies = [
        pltpu.make_async_copy(refs[k], refs[count + k], sems.at[k]) for k in range(count)
    ]
    for one in copies:
        one.start()
    for one in copies:
        one.wait()


def store(*arrays):
    anywhere = pl.BlockSpec(memory_space=pl.ANY)
    return pl.pallas_call(
        store_kernel,
        out_shape=tuple(jax.ShapeDtypeStruct(a.shape, a.dtype) for a in arrays),
        in_specs=[pl.BlockSpec(memory_space=pltpu.VMEM)] * len(arrays),
        out_specs=(pl.BlockSpec(memory_space=pltpu.HBM),) * len(arrays),
        scratch_shapes=[pltpu.SemaphoreType.DMA((len(arrays),))],
        compiler_params=pltpu.CompilerParams(vmem_limit_bytes=8 * 2**20),
    )(*arrays)


def fused(tokens, grad_out, routes, gates, w_gate_up, w_down):
    first_size, depth = lax.axis_size("da"), lax.axis_size("db")
    cols = first_size // CORES
    experts = first_size * depth
    local, features = tokens.shape
    top = routes.shape[1]
    group = experts // top
    ff = w_down.shape[1]
    bf, f32 = jnp.bfloat16, jnp.float32
    half = local // HALVES
    rows = half // group
    steps = HALVES * depth
    total = rows * experts * HALVES
    dma = pltpu.SemaphoreType.DMA
    scratch = [
        pltpu.VMEM((top, local), routes.dtype),
        pltpu.VMEM((top, local), gates.dtype),
        pltpu.VMEM((experts, HALVES, half, features), bf),
        pltpu.VMEM((experts, HALVES, half, features), bf),
        pltpu.VMEM((experts, experts, local), bf),
        pltpu.VMEM((features, 2 * ff), bf),
        pltpu.VMEM((ff, features), bf),
        pltpu.VMEM((2 * ff, features), bf),
        pltpu.VMEM((features, ff), bf),
        pltpu.VMEM((total, features), bf),
        pltpu.VMEM((total, features), bf),
        pltpu.VMEM((total, ff), bf),
        pltpu.VMEM((total, 2 * ff), bf),
        pltpu.VMEM((steps, cols, rows, features), bf),
        pltpu.VMEM((steps, cols, CORES, rows, features), bf),
        pltpu.VMEM((half, features), f32),
        pltpu.VMEM((depth, HALVES, cols, half, features), bf),
        pltpu.VMEM((depth + 1, HALVES, cols, half, features), bf),
        pltpu.VMEM((HALVES, half, features), f32),
        pltpu.VMEM((HALVES, half, features), bf),
        pltpu.VMEM((experts, 8, local), f32),
        pltpu.VMEM((experts, 8, local), f32),
        pltpu.VMEM((2 * cols * half * features // 128 + cols * experts, 128), bf),
        dma((5,)),
        dma((cols, depth, HALVES, 2)),
        dma((steps,)),
        dma((steps,)),
        dma((depth + 1, HALVES, 1 + SPLIT)),
        dma((1 + SPLIT,)),
        dma((1,)),
        dma((8,)),
        dma((2,)),
        dma((1,)),
        dma((1,)),
    ]
    vmem = pl.BlockSpec(memory_space=pltpu.VMEM)
    hbm = pl.BlockSpec(memory_space=pltpu.HBM)
    token_grads, gate_grads, grad_in, grad_down = pl.pallas_call(
        functools.partial(fused_kernel, cols, depth, group),
        out_shape=(
            jax.ShapeDtypeStruct((local, features), bf),
            jax.ShapeDtypeStruct((top, local), bf),
            jax.ShapeDtypeStruct(w_gate_up.shape, bf),
            jax.ShapeDtypeStruct(w_down.shape, bf),
        ),
        in_specs=[hbm] * 6,
        out_specs=(vmem, vmem, vmem, vmem),
        scratch_shapes=scratch,
        compiler_params=pltpu.CompilerParams(
            collective_id=0, has_side_effects=True, vmem_limit_bytes=44 * 2**20
        ),
    )(
        *(
            pltpu.with_memory_space_constraint(a, pltpu.HBM)
            for a in (tokens, grad_out, routes.T, gates.T, w_gate_up, w_down)
        )
    )
    token_grads, gate_grads, grad_in, grad_down = store(token_grads, gate_grads, grad_in, grad_down)
    return token_grads, gate_grads.T, grad_in, grad_down


def fits(tokens, routes, w_down):
    first_size = lax.axis_size("da")
    experts = first_size * lax.axis_size("db")
    local, features = tokens.shape
    group = experts // routes.shape[1]
    held = 2 * experts * local * features * 2
    return (
        lax.axis_size("replica") == 1
        and first_size % CORES == 0
        and first_size == 2 * CORES
        and 2 * 3 * lax.axis_size("db") <= 30
        and held <= 16 * 2**20
        and local == 128
        and experts <= local
        and max(map(max, relay_slots(lax.axis_size("db")))) == HALVES * lax.axis_size("db") + 1
        and (local // (HALVES * SPLIT * group)) % 16 == 0
        and w_down.shape[1] % 128 == 0
    )


def route(*arrays):
    if fits(arrays[0], arrays[2], arrays[5]):
        return fused(*arrays)
    return body(*arrays)


def solution(mesh):
    placed = (
        P(("groups", "replica", "da", "db"), None),
        P(("groups", "replica", "da", "db"), None),
        P(("groups", "replica", "da", "db"), None),
        P(("groups", "replica", "da", "db"), None),
        P(("da", "db"), "replica", None),
        P(("da", "db"), "replica", None),
    )
    return jax.shard_map(
        route,
        mesh=mesh,
        in_specs=placed,
        out_specs=(
            P(("groups", "replica", "da", "db"), None),
            P(("groups", "replica", "da", "db"), None),
            P(("groups", "da", "db"), "replica", None),
            P(("groups", "da", "db"), "replica", None),
        ),
        check_vma=False,
    )
```

```python
import functools

import jax
import jax.numpy as jnp
from jax import lax
from jax.experimental import pallas as pl
from jax.experimental.pallas import tpu as pltpu
from jax.sharding import PartitionSpec as P


CORES = 2
HALVES = 2
SPLIT = 2
MESH = pl.DeviceIdType.MESH


def silu_parts(projected):
    sigmoid = jax.nn.sigmoid(projected)
    return (projected * sigmoid, sigmoid * (1.0 + projected * (1.0 - sigmoid)))


def body(tokens, grad_out, routes, gates, w_gate_up, w_down):
    local_tokens, features = tokens.shape
    top_count = routes.shape[1]
    hidden_units = w_gate_up.shape[2] // 2
    first_size = lax.axis_size("da")
    second_size = lax.axis_size("db")
    experts = first_size * second_size
    per_round = experts // top_count
    rounds = local_tokens // per_round
    expert_ids = lax.broadcasted_iota(jnp.int32, (1, 1, 1, experts), 3)
    matches = routes.reshape(rounds, per_round, top_count, 1) == expert_ids
    gate_values = gates.reshape(rounds, per_round, top_count, 1).astype(jnp.float32)
    gate_table = jnp.sum(jnp.where(matches, gate_values, 0.0), axis=(1, 2)).astype(jnp.bfloat16)
    chosen = jnp.any(matches, axis=2).astype(jnp.bfloat16)
    input_send = jnp.einsum(
        "rge,rgd->red",
        chosen,
        tokens.reshape(rounds, per_round, features),
        preferred_element_type=jnp.float32,
    ).astype(jnp.bfloat16)
    upstream_send = jnp.einsum(
        "rge,rgd->red",
        chosen,
        grad_out.reshape(rounds, per_round, features),
        preferred_element_type=jnp.float32,
    ).astype(jnp.bfloat16)
    input_recv, upstream_recv, gate_recv = (
        lax.all_to_all(input_send, ("da", "db"), split_axis=1, concat_axis=1, tiled=True),
        lax.all_to_all(upstream_send, ("da", "db"), split_axis=1, concat_axis=1, tiled=True),
        lax.all_to_all(gate_table, ("da", "db"), split_axis=1, concat_axis=1, tiled=True),
    )
    input_rows = input_recv.reshape(-1, features)
    upstream_rows = upstream_recv.reshape(-1, features)
    gate_rows = gate_recv.reshape(-1, 1).astype(jnp.float32)
    w_in, w_out = (
        lax.all_gather(w_gate_up[0], "replica", axis=0, tiled=True),
        lax.all_gather(w_down[0], "replica", axis=0, tiled=True),
    )
    projected = jnp.dot(input_rows, w_in, preferred_element_type=jnp.float32)
    back_raw = jnp.einsum("rd,fd->rf", upstream_rows, w_out, preferred_element_type=jnp.float32)
    gate_part = projected[:, :hidden_units]
    up_part = projected[:, hidden_units:]
    activated, derivative = silu_parts(gate_part)
    hidden = (activated * up_part).astype(jnp.bfloat16)
    gate_scores = jnp.sum(hidden.astype(jnp.float32) * back_raw, axis=1).astype(jnp.bfloat16)
    back_hidden = gate_rows * back_raw
    grad_projected = jnp.concatenate(
        [back_hidden * up_part * derivative, back_hidden * activated], axis=1
    ).astype(jnp.bfloat16)
    scaled_upstream = (gate_rows * upstream_rows.astype(jnp.float32)).astype(jnp.bfloat16)
    input_grads = jnp.einsum("rf,df->rd", grad_projected, w_in, preferred_element_type=jnp.float32)
    input_grads = input_grads.astype(jnp.bfloat16).reshape(rounds, experts, features)
    score_back = gate_scores.reshape(rounds, experts)
    returned, score_ret = (
        lax.all_to_all(input_grads, ("da", "db"), split_axis=1, concat_axis=1, tiled=True),
        lax.all_to_all(score_back, ("da", "db"), split_axis=1, concat_axis=1, tiled=True),
    )
    score_ret = score_ret.reshape(rounds, 1, 1, experts).astype(jnp.float32)
    token_grads = (
        jnp.einsum("rge,red->rgd", chosen, returned, preferred_element_type=jnp.float32)
        .astype(jnp.bfloat16)
        .reshape(local_tokens, features)
    )
    gate_grads = (
        jnp.sum(jnp.where(matches, score_ret, 0.0), axis=3)
        .astype(jnp.bfloat16)
        .reshape(local_tokens, top_count)
    )
    columns = input_rows
    grad_in = lax.psum_scatter(
        jnp.einsum("rd,rf->df", columns, grad_projected, preferred_element_type=jnp.float32).astype(
            jnp.bfloat16
        ),
        "replica",
        scatter_dimension=0,
        tiled=True,
    )
    columns = hidden
    grad_down = lax.psum_scatter(
        jnp.einsum(
            "rf,rd->fd", columns, scaled_upstream, preferred_element_type=jnp.float32
        ).astype(jnp.bfloat16),
        "replica",
        scatter_dimension=0,
        tiled=True,
    )
    return (token_grads, gate_grads, grad_in[None], grad_down[None])


def visit(j, z, n):
    m = jnp.minimum(z, n - 1 - z)
    near = z + (1 - 2 * (j % 2)) * ((j + 1) // 2)
    far = jnp.where(z < n - 1 - z, j, n - 1 - j)
    return jnp.where(j <= 2 * m, near, far)


def dot(a, b, dims):
    return lax.dot_general(a, b, (dims, ((), ())), preferred_element_type=jnp.float32)


def position(d, z, n):
    away = abs(d - z)
    if away <= min(z, n - 1 - z):
        return 2 * away - (1 if d < z else 0)
    return d if z < n - 1 - z else n - 1 - d


def relay_slots(n):
    last = 2 * n - 1

    def ready(z, d, h):
        k = position(d, z, n)
        k = last - k if h else k
        feeds = [u for u in (z - 1, z + 1) if 0 <= u < n and abs(u - d) == abs(z - d) + 1]
        return max([k + 2] + [ready(u, d, h) + 1 for u in feeds])

    table = []
    for z in range(n):
        row = [0] * (2 * n)
        for d in range(n):
            k = position(d, z, n)
            row[k] = ready(z, d, 0)
            row[last - k] = ready(z, d, 1)
        table.append(row)
    return table


def lag_words(n):
    return [sum((at - k - 2) * 8 ** (2 * n - 1 - k) for k, at in enumerate(row)) for row in relay_slots(n)]


def fused_kernel(
    cols, depth, group,
    tok_hbm, up_hbm, routes_hbm, gates_hbm, win_hbm, wout_hbm,
    tg_ref, gg_ref, gin_ref, gdown_ref,
    routes_ref, gates_ref, tok, up, table, win, wout, win_t, wout_t, xs, su, hid, gp, igs, igb, acc, cs, cr, rk, rx, scs, scr, bulk,
    load_sem, recv_sem, near_sem, igr_sem, cr_sem, rx_sem, scr_sem, sent_sem,
    tail_sem, near_tail_sem, igr_tail_sem,
):
    da = lax.axis_index("da")
    z = lax.axis_index("db")
    x, c = da // CORES, da % CORES
    half, features = tok.shape[2], tok.shape[3]
    local = HALVES * half
    experts = table.shape[1]
    top = routes_ref.shape[0]
    rows = half // group
    ff = wout.shape[0]
    steps = HALVES * depth
    part = half // SPLIT
    few = rows // SPLIT

    def slot(xx, zz, cc):
        return (xx * CORES + cc) * depth + zz

    me = slot(x, z, c)
    loads = []
    for h in range(HALVES):
        span = pl.ds(h * half, half)
        loads.append(pltpu.make_async_copy(tok_hbm.at[span], tok.at[me, h], load_sem.at[0]))
        loads.append(pltpu.make_async_copy(up_hbm.at[span], up.at[me, h], load_sem.at[0]))
    loads += [
        pltpu.make_async_copy(win_hbm.at[0], win, load_sem.at[1]),
        pltpu.make_async_copy(wout_hbm.at[0], wout, load_sem.at[2]),
        pltpu.make_async_copy(routes_hbm, routes_ref, load_sem.at[3]),
        pltpu.make_async_copy(gates_hbm, gates_ref, load_sem.at[4]),
    ]
    def settle(view, sem):
        pltpu.make_async_copy(view, view, sem).wait()

    barrier = pltpu.get_barrier_semaphore()
    count = cols * CORES * depth

    def greet(xx, zz, cc):
        pl.semaphore_signal(
            barrier, inc=1, device_id={"da": xx * CORES + cc, "db": zz}, device_id_type=MESH
        )

    @pl.when(z > 0)
    def _():
        greet(x, z - 1, c)

    @pl.when(z < depth - 1)
    def _():
        greet(x, z + 1, c)

    greet(1 - x, z, c)
    greet(x, z, 1 - c)
    for k in (6, 7, 0, 1, 2, 3, 4, 5):
        loads[k].start()

    loads[6].wait()
    loads[7].wait()
    routes = routes_ref[...]
    gates = gates_ref[...].astype(jnp.float32)
    ids = lax.broadcasted_iota(jnp.int32, (experts, local), 0)
    chart = jnp.zeros((experts, local), jnp.float32)
    for k in range(top):
        chart = chart + jnp.where(routes[k : k + 1] == ids, gates[k : k + 1], 0.0)
    table[me] = chart.astype(jnp.bfloat16)

    settle(tok.at[pl.ds(0, CORES)], load_sem.at[0])
    pl.semaphore_wait(barrier, 2 + jnp.where(z > 0, 1, 0) + jnp.where(z < depth - 1, 1, 0))

    held = (tok, up)

    def send(src, dst, send_sem, recv, to_x, to_z, to_c):
        return pltpu.make_async_remote_copy(
            src_ref=src,
            dst_ref=dst,
            send_sem=send_sem,
            recv_sem=recv,
            device_id={"da": to_x * CORES + to_c, "db": to_z},
            device_id_type=MESH,
        )

    def start(copy):
        copy.start()

    def wait_recv(copy):
        copy.wait_recv()

    def both(xx, zz, h, a, way, act, to_x, to_z, to_c, near=None):
        s = slot(xx, zz, c)
        ref = held[a].at[s, h]
        landed = recv_sem.at[xx, zz, h, a] if near is None else near_sem.at[near]
        copy = send(ref, ref, sent_sem.at[way], landed, to_x, to_z, to_c)
        if a != 0:
            act(copy)
            return

        @pl.when(h != 0)
        def _():
            act(copy)

        @pl.when(h == 0)
        def _():
            if act is start:
                copy.start()
                page = table.at[s]
                send(page, page, sent_sem.at[3 + (way > 0)], landed, to_x, to_z, to_c).start()
            else:
                settle(bulk.at[pl.ds(0, half * features // 128 + experts)], landed)

    def step_of(i):
        j = jnp.minimum(i, steps - 1 - i)
        return visit(j, z, depth), jnp.where(i >= depth, 1, 0)

    def along_z(e, a):
        def one(reach, sign):
            last = 2 * reach + 1
            k = jnp.minimum(e, last - e)
            h = jnp.where(e > reach, 1, 0)
            zz = z + sign * k

            @pl.when((e <= last) & (k > 0))
            def _():
                both(x, zz, h, a, 0, wait_recv, x, z, 1 - c)

            ahead = z - sign

            @pl.when((e <= last) & (ahead >= 0) & (ahead < depth))
            def _():
                both(x, zz, h, a, 0, start, x, ahead, c)

        one(depth - 1 - z, 1)
        one(z, -1)

    def last_part(xx, u, a, way, to_x, to_c, near=None):
        ref = held[a].at[slot(xx, z, c), HALVES - 1, pl.ds(u * part, part)]
        landed = near
        if near is None:
            landed = recv_sem.at[xx, z, HALVES - 1, a] if u == 0 else tail_sem.at[a]
        return send(ref, ref, sent_sem.at[way], landed, to_x, z, to_c)

    def last_from_across(u):
        near = near_sem.at[steps - 1] if u == 0 else near_tail_sem.at[0]
        for a in range(2):
            last_part(1 - x, u, a, 1, 1 - x, c).wait_recv()
            last_part(1 - x, u, a, 2, x, 1 - c, near).start()

    def last_from_partner(u):
        if u == 0:
            settle(xs.at[pl.ds(0, (cols + 1) * half)], near_sem.at[steps - 1])
        else:
            settle(tok.at[0, 0], near_tail_sem.at[0])

    def across(i, a):
        zz, h = step_of(i)

        @pl.when(i < steps - 1)
        def _():
            both(x, zz, h, a, 1, start, 1 - x, z, c)

        @pl.when(i == steps - 1)
        def _():
            for b in range(2):
                last_part(x, a, b, 1, 1 - x, c).start()

        both(x, zz, h, a, 2, start, x, z, 1 - c, near=i)

    def from_across(i, a):
        zz, h = step_of(i)
        both(1 - x, zz, h, a, 1, wait_recv, 1 - x, z, c)
        both(1 - x, zz, h, a, 2, start, x, z, 1 - c, near=i)

    def from_partner(i):
        zz, h = step_of(i)

        @pl.when(h == 0)
        def _():
            settle(bulk, near_sem.at[i])

        @pl.when(h != 0)
        def _():
            settle(tok.at[pl.ds(0, cols)], near_sem.at[i])

    def pick(s, e, h):
        chart_s = table[s].astype(jnp.float32)
        which = lax.broadcasted_iota(jnp.int32, chart_s.shape, 0) == e
        row = jnp.sum(jnp.where(which, chart_s, 0.0), axis=0, keepdims=True)
        row = jnp.where(h == 0, row[:, :half], row[:, half:])
        off = lax.broadcasted_iota(jnp.int32, (rows, half), 1) - group * lax.broadcasted_iota(
            jnp.int32, (rows, half), 0
        )
        hit = (off >= 0) & (off < group) & (row > 0.0)
        return jnp.where(hit, 1.0, 0.0), row

    def send_ig(q, k):
        return send(igs.at[k, q], igb.at[k, q, c], sent_sem.at[5], igr_sem.at[k], x, z, 1 - c)

    def send_last_ig(q, u):
        at = pl.ds(u * few, few)
        landed = igr_sem.at[steps - 1] if u == 0 else igr_tail_sem.at[0]
        src, dst = igs.at[steps - 1, q, at], igb.at[steps - 1, q, c, at]
        return send(src, dst, sent_sem.at[5], landed, x, z, 1 - c)

    def send_score(s):
        return pltpu.make_async_remote_copy(
            src_ref=scs.at[s],
            dst_ref=scr.at[me],
            send_sem=sent_sem.at[7],
            recv_sem=scr_sem.at[0],
            device_id={"da": s // depth, "db": s % depth},
            device_id_type=MESH,
        )

    blocks = [(q, r) for q in range(cols) for r in range(CORES)]
    batch = len(blocks) * rows

    def compute(k, u=None):
        zz, h = step_of(k) if u is None else (z, HALVES - 1)
        count_rows = rows if u is None else few
        size = len(blocks) * count_rows
        base = pl.multiple_of(k * batch, batch) if u is None else k * batch + u * size
        picks = []
        gate_cols = []
        for n, (q, r) in enumerate(blocks):
            s = slot((x + q) % cols, zz, (c + r) % CORES)
            chosen, row = pick(s, me, h)
            tokens, upstreams = tok.at[s, h], up.at[s, h]
            if u is not None:
                span = slice(u * part, (u + 1) * part)
                chosen, row = chosen[u * few : (u + 1) * few, span], row[:, span]
                tokens = tokens.at[pl.ds(u * part, part)]
                upstreams = upstreams.at[pl.ds(u * part, part)]
            picks.append((s, chosen))
            gate_cols.append(jnp.sum(chosen * row, axis=1, keepdims=True))
            hot = chosen.astype(jnp.bfloat16)
            where = base + n * count_rows
            where = pl.ds(pl.multiple_of(where, count_rows) if u is None else where, count_rows)
            xs[where, :] = dot(hot, tokens[...], ((1,), (0,))).astype(jnp.bfloat16)
            su[where, :] = dot(hot, upstreams[...], ((1,), (0,))).astype(jnp.bfloat16)
        here = pl.ds(base, size)
        gate = jnp.concatenate(gate_cols, axis=0)
        upstream = su[here, :]
        projected = dot(xs[here, :], win[...], ((1,), (0,)))
        back_raw = dot(upstream, wout_t[...], ((1,), (0,)))
        su[here, :] = (gate * upstream.astype(jnp.float32)).astype(jnp.bfloat16)
        gate_part, up_part = projected[:, :ff], projected[:, ff:]
        activated, derivative = silu_parts(gate_part)
        hidden = (activated * up_part).astype(jnp.bfloat16)
        hid[here, :] = hidden
        scores = jnp.sum(hidden.astype(jnp.float32) * back_raw, axis=1, keepdims=True)
        scores = scores.astype(jnp.bfloat16).astype(jnp.float32)
        back_hidden = gate * back_raw
        gp[here, :ff] = (back_hidden * up_part * derivative).astype(jnp.bfloat16)
        gp[here, ff:] = (back_hidden * activated).astype(jnp.bfloat16)
        grads = dot(gp[here, :], win_t[...], ((1,), (0,))).astype(jnp.bfloat16)
        for n, (q, r) in enumerate(blocks):
            piece = grads[n * count_rows : (n + 1) * count_rows]
            if u is None:
                if r == 0:
                    igb[k, q, c] = piece
                else:
                    igs[k, q] = piece
                    send_ig(q, k).start()
            else:
                at = pl.ds(u * few, few)
                if r == 0:
                    igb[k, q, c, at] = piece
                else:
                    igs[k, q, at] = piece
                    send_last_ig(q, u).start()
        for n, (q, r) in enumerate(blocks):
            s, chosen = picks[n]
            line = jnp.sum(chosen * scores[n * count_rows : (n + 1) * count_rows], axis=0, keepdims=True)
            if u is not None:
                ahead = (HALVES - 1) * half + u * part
                parts = [jnp.zeros((1, ahead), jnp.float32), line]
                if u < SPLIT - 1:
                    parts.append(jnp.zeros((1, local - ahead - part), jnp.float32))
                scs[s] = scs[s] + jnp.broadcast_to(jnp.concatenate(parts, axis=1), scs.shape[1:])
                if u == SPLIT - 1:
                    if q == 0 and r == 0:
                        scr[me] = scs[me]
                    else:
                        send_score(s).start()
                continue
            rest = jnp.zeros_like(line)
            first = jnp.concatenate([line, rest], axis=1)
            second = jnp.concatenate([rest, line], axis=1)

            @pl.when(h == 0)
            def _():
                scs[s] = jnp.broadcast_to(first, scs.shape[1:])

            @pl.when(h == 1)
            def _():
                scs[s] = scs[s] + jnp.broadcast_to(second, scs.shape[1:])
                send_score(s).start()

    def send_sum(zz, h, q, u, side, to_z):
        place = jnp.where((zz == to_z) & (side == 1), depth, zz)
        at = pl.ds(u * part, part) if q else pl.ds(0, half)
        landed = cr_sem.at[place, h, q + u]
        return send(cs.at[zz, h, q, at], cr.at[place, h, q, at], sent_sem.at[6], landed, x, to_z, c)

    def send_across(h, u=None):
        at = pl.ds(0, half) if u is None else pl.ds(u * part, part)
        landed = rx_sem.at[0 if u is None else 1 + u]
        return send(cs.at[z, h, 1, at], rx.at[h, at], sent_sem.at[6], landed, 1 - x, z, c)

    def gather(zz, h, q, u, total):
        at = pl.ds(u * part, part) if q else pl.ds(0, half)
        to = pl.ds(0, part if q else half)
        acc[to, :] = total
        for side, ok in ((0, (zz <= z) & (z < depth - 1)), (1, (zz >= z) & (z > 0))):

            @pl.when(ok)
            def _():
                send_sum(zz, h, q, u, side, z).wait_recv()
                place = jnp.where((zz == z) & (side == 1), depth, zz)
                acc[to, :] += cr[place, h, q, at].astype(jnp.float32)

        return at, to

    def hot_of(s, h):
        return [pick(s, slot(x, z, m), h)[0] for m in range(CORES)]

    def pass_on(k, q):
        zz, h = step_of(k)
        hot = jnp.concatenate(hot_of(slot((x + q) % cols, zz, c), h), axis=0).astype(jnp.bfloat16)
        if q == 1:
            settle(igs.at[0], igr_sem.at[k])
        pair = igb[k, q].reshape(CORES * rows, features)
        for u in range(SPLIT if q else 1):
            mine = hot[:, u * part : (u + 1) * part] if q else hot
            at, to = gather(zz, h, q, u, dot(mine, pair, ((0,), (0,))))
            cs[zz, h, q, at] = acc[to, :].astype(jnp.bfloat16)

            @pl.when(zz < z)
            def _():
                send_sum(zz, h, q, u, 0, z - 1).start()

            @pl.when(zz > z)
            def _():
                send_sum(zz, h, q, u, 1, z + 1).start()

    def home_sum(k, h, q):
        hot = jnp.concatenate(hot_of(slot((x + q) % cols, z, c), h), axis=0).astype(jnp.bfloat16)
        pair = igb[k, q].reshape(CORES * rows, features)
        return hot, pair

    def home_first():
        settle(igs.at[0], igr_sem.at[0])
        hot, pair = home_sum(0, 0, 1)
        for u in range(SPLIT):
            span = slice(u * part, (u + 1) * part)
            at, to = gather(z, 0, 1, u, dot(hot[:, span], pair, ((0,), (0,))))
            cs[z, 0, 1, at] = acc[to, :].astype(jnp.bfloat16)
        send_across(0).start()

    def home_last(u):
        k = steps - 1
        s = slot(1 - x, z, c)
        here, span = slice(u * few, (u + 1) * few), slice(u * part, (u + 1) * part)
        hot = jnp.concatenate([one[here, span] for one in hot_of(s, HALVES - 1)], axis=0)
        settle(igs.at[0, 0], igr_sem.at[k] if u == 0 else igr_tail_sem.at[0])
        pair = igb[k, 1, :, pl.ds(u * few, few)].reshape(CORES * few, features)
        at, to = gather(z, HALVES - 1, 1, u, dot(hot.astype(jnp.bfloat16), pair, ((0,), (0,))))
        cs[z, HALVES - 1, 1, at] = acc[to, :].astype(jnp.bfloat16)
        send_across(HALVES - 1, u).start()

    def home_own():
        for k, h in ((0, 0), (steps - 1, HALVES - 1)):
            hot, pair = home_sum(k, h, 0)
            gather(z, h, 0, 0, dot(hot, pair, ((0,), (0,))))
            rk[h] = acc[...]

    words = lag_words(depth)
    word = jnp.int32(words[0])
    for k in range(1, depth):
        word = jnp.where(z == k, words[k], word)

    edge = (z == 0) | (z == depth - 1)
    inner = jnp.logical_not(edge)

    def pass_all(i, q):
        def one(j, left):
            k = steps - 1 - j
            due = (k + 2 + left % 8 == i) & (j > 0)

            @pl.when(due)
            def _():
                pass_on(k, q)

            return left // 8

        lax.fori_loop(0, steps - 1, one, word)

    along_z(0, 0)
    across(0, 0)

    def step(i, carry):
        @pl.when(i < steps)
        def _():
            along_z(i, 1)
            across(i, 1)

        @pl.when(i == 0)
        def _():
            loads[4].wait()
            loads[5].wait()
            win_t[...] = win[...].T
            wout_t[...] = wout[...].T

        @pl.when(inner & (i >= 2))
        def _():
            pass_all(i, 1)

        @pl.when(i >= 1)
        def _():
            from_across(i - 1, 1)

        @pl.when(inner & (i >= 2))
        def _():
            pass_all(i, 0)

        @pl.when(i >= 1)
        def _():
            from_partner(i - 1)
            compute(i - 1)

        @pl.when(i + 1 < steps)
        def _():
            along_z(i + 1, 0)
            across(i + 1, 0)

        @pl.when(i < steps - 1)
        def _():
            from_across(i, 0)

        @pl.when(i == steps - 1)
        def _():
            last_from_across(0)

        @pl.when(edge & (i >= 1))
        def _():
            pass_all(i + 1, 1)
            pass_all(i + 1, 0)

        return carry

    lax.fori_loop(0, steps, step, 0)

    @pl.when(inner)
    def _():
        pass_all(steps, 1)

    last_from_partner(0)
    compute(steps - 1, 0)
    last_from_across(1)
    home_first()

    @pl.when(inner)
    def _():
        pass_all(steps, 0)

    last_from_partner(1)
    compute(steps - 1, 1)
    home_last(0)

    wide = min(features, 256)

    def gin(t, carry):
        at = pl.ds(pl.multiple_of(t * wide, wide), wide)
        gin_ref[0, at, :] = dot(xs[:, at], gp[...], ((0,), (0,))).astype(jnp.bfloat16)
        return carry

    early = jnp.where(edge, 2, 1)
    lax.fori_loop(0, early, gin, 0)
    home_last(1)
    lax.fori_loop(early, features // wide, gin, 0)

    thin = 128

    @pl.loop(0, ff // thin)
    def _(t):
        at = pl.ds(pl.multiple_of(t * thin, thin), thin)
        gdown_ref[0, at, :] = dot(hid[:, at], su[...], ((0,), (0,))).astype(jnp.bfloat16)

    home_own()
    settle(scr.at[pl.ds(0, count - 1)], scr_sem.at[0])
    scores = scr[:, 0, :]
    place = lax.broadcasted_iota(jnp.int32, (top, local), 0)
    gate_grads = jnp.zeros((top, local), jnp.float32)
    for k in range(top):
        value = jnp.sum(jnp.where(routes[k : k + 1] == ids, scores, 0.0), axis=0, keepdims=True)
        gate_grads = jnp.where(place == k, value, gate_grads)
    gg_ref[...] = gate_grads.astype(jnp.bfloat16)

    def finish(h):
        for u in (None,) if h == 0 else range(SPLIT):
            send_across(h, u).wait_recv()
        tg_ref[pl.ds(h * half, half), :] = (rk[h] + rx[h].astype(jnp.float32)).astype(jnp.bfloat16)

    for h in range(HALVES - 1):
        finish(h)

    for at in range(depth):
        sent = (depth - at if at > 0 else 0) + (at + 1 if at < depth - 1 else 0)

        @pl.when(z == at)
        def _():
            settle(tok.at[pl.ds(0, 2 * sent)], sent_sem.at[0])
            settle(table.at[pl.ds(0, sent)], sent_sem.at[3])

    settle(tok.at[pl.ds(0, 2 * depth)], sent_sem.at[1])
    settle(tok, sent_sem.at[2])
    settle(table.at[pl.ds(0, 3 * depth)], sent_sem.at[4])
    settle(igs, sent_sem.at[5])
    settle(scs.at[pl.ds(0, count - 1)], sent_sem.at[7])

    finish(HALVES - 1)
    settle(tok.at[pl.ds(0, depth * cols - 1)], sent_sem.at[6])


def store_kernel(*refs):
    count = len(refs) // 2
    sems = refs[-1]
    copies = [
        pltpu.make_async_copy(refs[k], refs[count + k], sems.at[k]) for k in range(count)
    ]
    for one in copies:
        one.start()
    for one in copies:
        one.wait()


def store(*arrays):
    anywhere = pl.BlockSpec(memory_space=pl.ANY)
    return pl.pallas_call(
        store_kernel,
        out_shape=tuple(jax.ShapeDtypeStruct(a.shape, a.dtype) for a in arrays),
        in_specs=[pl.BlockSpec(memory_space=pltpu.VMEM)] * len(arrays),
        out_specs=(pl.BlockSpec(memory_space=pltpu.HBM),) * len(arrays),
        scratch_shapes=[pltpu.SemaphoreType.DMA((len(arrays),))],
        compiler_params=pltpu.CompilerParams(vmem_limit_bytes=8 * 2**20),
    )(*arrays)


def fused(tokens, grad_out, routes, gates, w_gate_up, w_down):
    first_size, depth = lax.axis_size("da"), lax.axis_size("db")
    cols = first_size // CORES
    experts = first_size * depth
    local, features = tokens.shape
    top = routes.shape[1]
    group = experts // top
    ff = w_down.shape[1]
    bf, f32 = jnp.bfloat16, jnp.float32
    half = local // HALVES
    rows = half // group
    steps = HALVES * depth
    total = rows * experts * HALVES
    dma = pltpu.SemaphoreType.DMA
    scratch = [
        pltpu.VMEM((top, local), routes.dtype),
        pltpu.VMEM((top, local), gates.dtype),
        pltpu.VMEM((experts, HALVES, half, features), bf),
        pltpu.VMEM((experts, HALVES, half, features), bf),
        pltpu.VMEM((experts, experts, local), bf),
        pltpu.VMEM((features, 2 * ff), bf),
        pltpu.VMEM((ff, features), bf),
        pltpu.VMEM((2 * ff, features), bf),
        pltpu.VMEM((features, ff), bf),
        pltpu.VMEM((total, features), bf),
        pltpu.VMEM((total, features), bf),
        pltpu.VMEM((total, ff), bf),
        pltpu.VMEM((total, 2 * ff), bf),
        pltpu.VMEM((steps, cols, rows, features), bf),
        pltpu.VMEM((steps, cols, CORES, rows, features), bf),
        pltpu.VMEM((half, features), f32),
        pltpu.VMEM((depth, HALVES, cols, half, features), bf),
        pltpu.VMEM((depth + 1, HALVES, cols, half, features), bf),
        pltpu.VMEM((HALVES, half, features), f32),
        pltpu.VMEM((HALVES, half, features), bf),
        pltpu.VMEM((experts, 8, local), f32),
        pltpu.VMEM((experts, 8, local), f32),
        pltpu.VMEM((2 * cols * half * features // 128 + cols * experts, 128), bf),
        dma((5,)),
        dma((cols, depth, HALVES, 2)),
        dma((steps,)),
        dma((steps,)),
        dma((depth + 1, HALVES, 1 + SPLIT)),
        dma((1 + SPLIT,)),
        dma((1,)),
        dma((8,)),
        dma((2,)),
        dma((1,)),
        dma((1,)),
    ]
    vmem = pl.BlockSpec(memory_space=pltpu.VMEM)
    hbm = pl.BlockSpec(memory_space=pltpu.HBM)
    token_grads, gate_grads, grad_in, grad_down = pl.pallas_call(
        functools.partial(fused_kernel, cols, depth, group),
        out_shape=(
            jax.ShapeDtypeStruct((local, features), bf),
            jax.ShapeDtypeStruct((top, local), bf),
            jax.ShapeDtypeStruct(w_gate_up.shape, bf),
            jax.ShapeDtypeStruct(w_down.shape, bf),
        ),
        in_specs=[hbm] * 6,
        out_specs=(vmem, vmem, vmem, vmem),
        scratch_shapes=scratch,
        compiler_params=pltpu.CompilerParams(
            collective_id=0, has_side_effects=True, vmem_limit_bytes=44 * 2**20
        ),
    )(
        *(
            pltpu.with_memory_space_constraint(a, pltpu.HBM)
            for a in (tokens, grad_out, routes.T, gates.T, w_gate_up, w_down)
        )
    )
    token_grads, gate_grads, grad_in, grad_down = store(token_grads, gate_grads, grad_in, grad_down)
    return token_grads, gate_grads.T, grad_in, grad_down


def fits(tokens, routes, w_down):
    first_size = lax.axis_size("da")
    experts = first_size * lax.axis_size("db")
    local, features = tokens.shape
    group = experts // routes.shape[1]
    held = 2 * experts * local * features * 2
    return (
        lax.axis_size("replica") == 1
        and first_size % CORES == 0
        and first_size == 2 * CORES
        and 2 * 3 * lax.axis_size("db") <= 30
        and held <= 16 * 2**20
        and local == 128
        and experts <= local
        and max(map(max, relay_slots(lax.axis_size("db")))) == HALVES * lax.axis_size("db") + 1
        and (local // (HALVES * SPLIT * group)) % 16 == 0
        and w_down.shape[1] % 128 == 0
    )


def route(*arrays):
    if fits(arrays[0], arrays[2], arrays[5]):
        return fused(*arrays)
    return body(*arrays)


def solution(mesh):
    placed = (
        P(("groups", "replica", "da", "db"), None),
        P(("groups", "replica", "da", "db"), None),
        P(("groups", "replica", "da", "db"), None),
        P(("groups", "replica", "da", "db"), None),
        P(("da", "db"), "replica", None),
        P(("da", "db"), "replica", None),
    )
    return jax.shard_map(
        route,
        mesh=mesh,
        in_specs=placed,
        out_specs=(
            P(("groups", "replica", "da", "db"), None),
            P(("groups", "replica", "da", "db"), None),
            P(("groups", "da", "db"), "replica", None),
            P(("groups", "da", "db"), "replica", None),
        ),
        check_vma=False,
    )
```
